32 devices in a mesh: wide: 8 (over y, x, core), narrow: 4 (over z).
Axes of the slice: x: 2, y: 2, z: 4, core: 2. Of those that a mesh axis runs over, the one named last changes fastest.
Arguments:
- tokens: bfloat16 [256, 128, 768], P(('wide', 'narrow')), may hold values from -6 to 6
- segments: int32 [256, 128], P(('wide', 'narrow')), may hold values from 0 to 7, never falling along the last dimension, each value on 1 to 32 neighbouring positions
- destination: int32 [256], P(('wide', 'narrow')), may hold values from -1 to 7, as said below
- pair_index: int32 [1024, 2], P(('wide', 'narrow')), may hold values from 0 to 63, as said below
- targets: float32 [1024], P(('wide', 'narrow')), may hold values from -0.5 to 1
- w_qkv: bfloat16 [768, 2304], replicated, may hold values from -0.21875 to 0.21875
- b_qv: float32 [1536], replicated, may hold values from -3 to 3
- w_o: bfloat16 [768, 768], replicated, may hold values from -0.4375 to 0.4375
- b_o: float32 [768], replicated, may hold values from -3 to 3
- gain_one: float32 [768], replicated, may hold values from 0.1 to 1.9
- shift_one: float32 [768], replicated, may hold values from -2 to 2
- w_in: bfloat16 [768, 3072], replicated, may hold values from -0.21875 to 0.21875
- b_in: float32 [3072], replicated, may hold values from -3 to 3
- w_out: bfloat16 [3072, 768], replicated, may hold values from -0.109375 to 0.109375
- b_out: float32 [768], replicated, may hold values from -3 to 3
- gain_two: float32 [768], replicated, may hold values from 0.1 to 1.9
- shift_two: float32 [768], replicated, may hold values from -2 to 2
Outputs:
- encoded: bfloat16 [128, 128, 768], P(('wide', 'narrow'))
- similarity: float32 [1024], P(('wide', 'narrow'))
- grad_tokens: bfloat16 [256, 128, 768], P(('wide', 'narrow'))
- grad_w_qkv: float32 [768, 2304], P('narrow', 'wide')
- grad_b_qv: float32 [1536], replicated
- grad_w_o: float32 [768, 768], P('narrow', 'wide')
- grad_b_o: float32 [768], replicated
- grad_gain_one: float32 [768], replicated
- grad_shift_one: float32 [768], replicated
- grad_w_in: float32 [768, 3072], P('narrow', 'wide')
- grad_b_in: float32 [3072], replicated
- grad_w_out: float32 [3072, 768], P('narrow', 'wide')
- grad_b_out: float32 [768], replicated
- grad_gain_two: float32 [768], replicated
- grad_shift_two: float32 [768], replicated
The draws below stay inside these ranges and needn't reach their ends.
Inputs may be any that keep to these rules, and one draw needn't show every extreme that they name: `destination`: -1 marks an empty row slot. Among the slots held by the devices of one narrow index, every wide index owns exactly 4 live slots; one device sends at most 1 slot to one owner, holds 0 to 8 live slots, and in every such group some device holds 8. `pair_index`: every sentence slot of a device is in exactly one pair; a pair joins two slots of live rows or two slots of empty rows. `segments`: within a row the numbers never fall and each of 0 to 7 covers 1 to 32 tokens.
All inputs are finite; a program needn't handle non-finite values.
Results may differ from the reference program's by a relative error of at most 0.017.
Values may be sent and summed in bfloat16 or wider, within the bound.
No kernel may reach another device: no remote copies, remote signals or barrier semaphores. Data moves between devices by JAX's collectives and lax.ppermute only.
A program may use at most 192 MiB of HBM per device.

```python
import math
import jax
import jax.numpy as jnp
import numpy as np
from jax import lax

D = 768
HEADS = 12
HEAD_DIM = 64
FF = 3072
ROW_LEN = 128
SEG_ROW = 8
R_DEV = 4
SEG_MOST = 32
ROWS = 128
SLOTS = 256
PAIR_DEV = 32
PAIRS = 1024
N_WIDE = 8
N_NARROW = 4
DEVICES = 32


def routing_plan(key):
    base_key = jax.random.fold_in(key, 7)
    key_delta, key_order, key_place, key_label = jax.random.split(base_key, 4)
    slot_dev = 2 * R_DEV
    delta = jax.random.randint(key_delta, (N_NARROW, N_WIDE // 2), 0, R_DEV + 1)
    delta = delta.at[:, 0].set(R_DEV)
    live_counts = jnp.concatenate([R_DEV + delta, R_DEV - delta], axis=1).astype(jnp.int32)
    order_keys = jax.random.split(key_order, N_NARROW)
    shuffle = jax.vmap(lambda subkey: jax.random.permutation(subkey, N_WIDE))(order_keys).astype(jnp.int32)
    live_counts = jnp.take_along_axis(live_counts, shuffle, axis=1)
    place_keys = jax.random.split(key_place, N_NARROW * N_WIDE)
    places = jax.vmap(lambda subkey: jax.random.permutation(subkey, slot_dev))(place_keys)
    places = places.astype(jnp.int32).reshape(N_NARROW, N_WIDE, slot_dev)
    live = places < live_counts[:, :, None]
    within = jnp.cumsum(live.astype(jnp.int32), axis=2) - 1
    offsets = jnp.cumsum(live_counts, axis=1) - live_counts
    global_rank = offsets[:, :, None] + within
    label_keys = jax.random.split(key_label, N_NARROW)
    labels = jax.vmap(lambda subkey: jax.random.permutation(subkey, N_WIDE))(label_keys).astype(jnp.int32)
    residue = (global_rank % N_WIDE).reshape(N_NARROW, N_WIDE * slot_dev)
    owners = jnp.take_along_axis(labels, residue, axis=1).reshape(N_NARROW, N_WIDE, slot_dev)
    owners = jnp.where(live, owners, -1)
    return (owners, live)


def draw_destination(key, part):
    owners, live = routing_plan(key)
    return jnp.transpose(owners, (1, 0, 2)).reshape(-1).astype(jnp.int32)


def draw_pair_index(key, part):
    owners, live = routing_plan(key)
    seg_slots = 2 * R_DEV * SEG_ROW
    live_seg = jnp.repeat(live, SEG_ROW, axis=2).astype(jnp.int32)
    base_key = jax.random.fold_in(key, 13)
    pair_keys = jax.random.split(base_key, N_NARROW * N_WIDE)
    shuffled = jax.vmap(lambda subkey: jax.random.permutation(subkey, seg_slots))(pair_keys)
    shuffled = shuffled.astype(jnp.int32).reshape(N_NARROW, N_WIDE, seg_slots)
    ranked = live_seg * seg_slots + shuffled
    picked = jnp.argsort(-ranked, axis=2).astype(jnp.int32)
    return jnp.transpose(picked, (1, 0, 2)).reshape(N_WIDE * N_NARROW * seg_slots // 2, 2)


def block_scale(own_key, extent, cuts, smallest, top_value):
    level = 1.0
    for position, shards_of in cuts:
        heights = jax.random.uniform(jax.random.fold_in(jax.random.fold_in(own_key, 6), position), (shards_of,), jnp.float32, smallest / len(cuts), top_value / len(cuts))
        level = level * jnp.repeat(jnp.exp(heights), extent[position] // shards_of).reshape((-1,) + (1,) * (len(extent) - 1 - position))
    return level


def profile(count, total, limit, skew):
    portions = [(1 << 20) // math.isqrt(rank ** skew) + 1 for rank in range(2, count + 1)]
    surplus, counts = total - limit - (count - 1), [1] * (count - 1)
    while surplus > 0:
        candidates = [i for i in range(count - 1) if counts[i] < limit]
        pool, budget = sum([portions[i] for i in candidates]), surplus
        for i in candidates:
            extra = min(limit - counts[i], max(1, budget * portions[i] // pool), surplus)
            counts[i] = counts[i] + extra
            surplus = surplus - extra
    return np.array([limit] + counts)


def uneven_parts(key, amount, total, limit, lean):
    if amount == 2:
        one = jax.random.randint(key, (), max(1, total - limit), min(limit, total - 1) + 1)
        return jnp.stack([one, total - one])
    lengths = jnp.asarray(profile(amount, total, limit, lean), jnp.int32)
    pairs = (amount - 1) // 2
    donor, sink = lengths[1:1 + 2 * pairs:2], lengths[2:2 + 2 * pairs:2]
    slack = jnp.minimum(donor - 1, limit - sink)
    moved = jax.random.randint(jax.random.fold_in(key, 1), (pairs,), 0, 1 << 20) % (slack + 1)
    lengths = lengths.at[1:1 + 2 * pairs:2].set(donor - moved).at[2:2 + 2 * pairs:2].set(sink + moved)
    return lengths[jax.random.permutation(jax.random.fold_in(key, 2), amount)]


def noise(key, dims, width, reach, cuts=(), kind=jnp.bfloat16):
    loudness = block_scale(key, dims, cuts, -0.22, 0.18) if cuts else 1.0
    drawn = jax.random.normal(key, dims, jnp.float32) * width * loudness
    return jnp.minimum(jnp.maximum(drawn, -reach), reach).astype(kind)


def setup_inputs(seed: int = 0) -> dict:
    key_of = jax.random.split(jax.random.key(seed), 18)
    return {
        "tokens": noise(key_of[0], (SLOTS, ROW_LEN, D), 1.0, 6.0, ((0, 32),)),
        "segments": jax.vmap(lambda own: jnp.searchsorted(jnp.cumsum(uneven_parts(own, SEG_ROW, ROW_LEN, SEG_MOST, 1)), jnp.arange(ROW_LEN), side="right"))(jax.random.split(key_of[1], SLOTS)).reshape((SLOTS, ROW_LEN)).astype(jnp.int32),
        "destination": draw_destination(jax.random.fold_in(key_of[17], 71), 0),
        "pair_index": draw_pair_index(jax.random.fold_in(key_of[17], 71), 0),
        "targets": jnp.clip(-0.5 + 1.5 * jax.random.uniform(key_of[4], (PAIRS,), jnp.float32) ** block_scale(key_of[4], (PAIRS,), ((0, 32),), -0.2, 0.2), -0.5, 1.0),
        "w_qkv": noise(key_of[5], (D, 3 * D), D ** -0.5, 0.21875),
        "b_qv": noise(key_of[6], (2 * D,), 0.5, 3.0, (), jnp.float32),
        "w_o": noise(key_of[7], (D, D), (D // 4) ** -0.5, 0.4375),
        "b_o": noise(key_of[8], (D,), 0.5, 3.0, (), jnp.float32),
        "gain_one": jnp.clip(1.0 + 0.18 * jax.random.normal(key_of[9], (D,), jnp.float32), 0.1, 1.9),
        "shift_one": noise(key_of[10], (D,), 0.3, 2.0, (), jnp.float32),
        "w_in": noise(key_of[11], (D, FF), D ** -0.5, 0.21875),
        "b_in": noise(key_of[12], (FF,), 0.5, 3.0, (), jnp.float32),
        "w_out": noise(key_of[13], (FF, D), FF ** -0.5, 0.109375),
        "b_out": noise(key_of[14], (D,), 0.5, 3.0, (), jnp.float32),
        "gain_two": jnp.clip(1.0 + 0.18 * jax.random.normal(key_of[15], (D,), jnp.float32), 0.1, 1.9),
        "shift_two": noise(key_of[16], (D,), 0.3, 2.0, (), jnp.float32),
    }


HIGH_PRECISION = lax.Precision.HIGHEST
NEG_FILL = -1e+30

@jax.custom_vjp
def low(v):
    return lax.optimization_barrier(v.astype(jnp.bfloat16)).astype(jnp.float32)

@jax.custom_vjp
def low_back(v):
    return v

def low_keep(v):
    return (low(v), None)

def low_pass(kept, grad):
    return (grad,)

def back_keep(v):
    return (v, None)

def back_low(kept, grad):
    return (low(grad),)
low.defvjp(low_keep, low_pass)
low_back.defvjp(back_keep, back_low)

def layer_norm(values, gain, shift):
    middle = lax.optimization_barrier(jnp.mean(values, axis=-1, keepdims=True))
    centered = values - middle
    spread = lax.optimization_barrier(jnp.mean(centered * centered, axis=-1, keepdims=True))
    return centered * lax.rsqrt(spread + 1e-12) * gain + shift

def cosine_of(left_vec, right_vec):
    inner = lax.optimization_barrier(jnp.mean(left_vec * right_vec, axis=-1))
    left_sq = lax.optimization_barrier(jnp.mean(left_vec * left_vec, axis=-1))
    right_sq = lax.optimization_barrier(jnp.mean(right_vec * right_vec, axis=-1))
    return inner * lax.rsqrt(left_sq + 1e-06) * lax.rsqrt(right_sq + 1e-06)

def block_forward(params, row_data, labels):
    w_qkv, b_qv, w_o, b_o, gain_one, shift_one, w_in, b_in, w_out, b_out, gain_two, shift_two = params
    row_count = row_data.shape[0]
    model_width = row_data.shape[2]
    score_scale = 1.0 / math.sqrt(HEAD_DIM)
    flat_in = low_back(row_data.reshape(row_count * ROW_LEN, model_width))
    full_bias = jnp.concatenate([b_qv[:model_width], jnp.zeros((model_width,), jnp.float32), b_qv[model_width:]])
    mixed_proj = jnp.dot(flat_in, w_qkv, precision=HIGH_PRECISION) + full_bias

    def heads_of(member):
        return low(low_back(member)).reshape(row_count, ROW_LEN, HEADS, HEAD_DIM)
    queries = heads_of(mixed_proj[:, :model_width])
    key_rows = heads_of(mixed_proj[:, model_width:2 * model_width])
    values = heads_of(mixed_proj[:, 2 * model_width:])
    raw_scores = jnp.einsum('rqhd,rkhd->rhqk', queries, key_rows, precision=HIGH_PRECISION) * score_scale
    same_segment = labels[:, :, None] == labels[:, None, :]
    scores = low_back(jnp.where(same_segment[:, None, :, :], raw_scores, NEG_FILL))
    row_top = lax.optimization_barrier(jnp.max(scores, axis=-1, keepdims=True))
    expo = jnp.exp(scores - row_top)
    probability = expo / lax.optimization_barrier(jnp.sum(expo, axis=-1, keepdims=True))
    context = jnp.einsum('rhqk,rkhd->rqhd', low(probability), values, precision=HIGH_PRECISION)
    context = low(low_back(context.reshape(row_count * ROW_LEN, model_width)))
    attn_out = low_back(jnp.dot(context, w_o, precision=HIGH_PRECISION) + b_o)
    hidden = layer_norm(flat_in + attn_out, gain_one, shift_one)
    up_proj = low_back(jnp.dot(low(hidden), w_in, precision=HIGH_PRECISION) + b_in)
    activated = jax.nn.gelu(up_proj, approximate=False)
    ffn_out = low_back(jnp.dot(low(activated), w_out, precision=HIGH_PRECISION) + b_out)
    normed_out = layer_norm(hidden + ffn_out, gain_two, shift_two).reshape(row_count, ROW_LEN, model_width)
    onehot = (labels[:, :, None] == jnp.arange(SEG_ROW, dtype=jnp.int32)[None, None, :]).astype(jnp.float32)
    seg_count = lax.optimization_barrier(jnp.sum(onehot, axis=1))
    pooled = jnp.einsum('rtd,rts->rsd', normed_out, onehot, precision=HIGH_PRECISION) / seg_count[:, :, None]
    return (normed_out, low(low_back(pooled)))

def reference(tokens, segments, destination, pair_index, targets, w_qkv, b_qv, w_o, b_o, gain_one, shift_one, w_in, b_in, w_out, b_out, gain_two, shift_two):
    slot_total = destination.shape[0]
    model_width = tokens.shape[2]
    slot_ids = jnp.arange(slot_total, dtype=jnp.int32)
    narrow_of = slot_ids // (2 * R_DEV) % N_NARROW
    owner_block = jnp.where(destination >= 0, destination * N_NARROW + narrow_of, DEVICES)
    owner_order = jnp.argsort(owner_block * slot_total + slot_ids)[:ROWS].astype(jnp.int32)
    row_data = tokens[owner_order].astype(jnp.float32).reshape(DEVICES, R_DEV, ROW_LEN, model_width)
    row_labels = segments[owner_order].reshape(DEVICES, R_DEV, ROW_LEN)
    params = (w_qkv.astype(jnp.float32), b_qv, w_o.astype(jnp.float32), b_o, gain_one, shift_one, w_in.astype(jnp.float32), b_in, w_out.astype(jnp.float32), b_out, gain_two, shift_two)
    live_slot = destination >= 0
    seg_per_dev = 2 * R_DEV * SEG_ROW
    pair_block = jnp.arange(pair_index.shape[0], dtype=jnp.int32) // PAIR_DEV
    first = pair_index[:, 0] + pair_block * seg_per_dev
    second = pair_index[:, 1] + pair_block * seg_per_dev
    live_pair = live_slot[first // SEG_ROW]
    place_at = (owner_order[:, None] * SEG_ROW + jnp.arange(SEG_ROW, dtype=jnp.int32)[None, :]).reshape(-1)

    def forward(param_set, rows_in):
        run_block = jax.checkpoint(lambda member: block_forward(param_set, member[0], member[1]))
        normed_out, pooled = lax.map(run_block, (rows_in, row_labels))
        home_slots = jnp.zeros((slot_total * SEG_ROW, model_width), jnp.float32)
        home_slots = home_slots.at[place_at].set(pooled.reshape(-1, model_width))
        cosine = jnp.where(live_pair, cosine_of(home_slots[first], home_slots[second]), 0.0)
        loss_value = jnp.sum(jnp.where(live_pair, (cosine - targets) ** 2, 0.0))
        return (loss_value, (normed_out, cosine))
    loss_value, pull_back, aux_out = jax.vjp(forward, params, row_data, has_aux=True)
    weight_grads, grad_rows = pull_back(jnp.ones((), jnp.float32))
    normed_out, similarity = aux_out
    encoded = normed_out.reshape(ROWS, ROW_LEN, model_width).astype(jnp.bfloat16)
    grad_home = jnp.zeros((slot_total, ROW_LEN, model_width), jnp.float32)
    grad_home = grad_home.at[owner_order].set(grad_rows.reshape(ROWS, ROW_LEN, model_width))
    grad_tokens = grad_home.astype(jnp.bfloat16)
    return (encoded, similarity, grad_tokens, weight_grads[0], weight_grads[1], weight_grads[2], weight_grads[3], weight_grads[4], weight_grads[5], weight_grads[6], weight_grads[7], weight_grads[8], weight_grads[9], weight_grads[10], weight_grads[11])
```

```python
import functools
import math

import jax
import jax.numpy as jnp
from jax import lax
from jax.experimental import pallas as pl
from jax.experimental.pallas import tpu as pltpu
from jax.sharding import PartitionSpec as P

HEAD_DIM = 64
SEG_ROW = 8
LANES = 128
META_ROWS = 16
NEG_FILL = -1e30
NORM_EPS = 1e-12
COS_EPS = 1e-06
F32 = jnp.float32
BF16 = jnp.bfloat16
VMEM_LIMIT = 60 * 1024 * 1024

NT = (((1,), (1,)), ((), ()))
TN = (((0,), (0,)), ((), ()))


def vmem_spec():
    return pl.BlockSpec(memory_space=pltpu.VMEM)


def params(steps=0):
    return pltpu.CompilerParams(
        dimension_semantics=("arbitrary",) * steps if steps else None,
        vmem_limit_bytes=VMEM_LIMIT,
    )


def split_three(values):
    high = values.astype(BF16)
    rest = values - high.astype(F32)
    middle = rest.astype(BF16)
    low = (rest - middle.astype(F32)).astype(BF16)
    return (high, middle, low)


def dot(left, right, dims=None):
    if dims is None:
        return jnp.dot(left, right, preferred_element_type=F32)
    return lax.dot_general(left, right, dims, preferred_element_type=F32)


def column_sum(values):
    return jnp.sum(values, axis=0, keepdims=True)


def row_mean(values):
    return jnp.mean(values, axis=-1, keepdims=True)


def prep_kernel(dest_ref, tok_ref, seg_ref, dest64_ref, pair_ref, targ_ref, out_ref):
    owner = pl.program_id(0)
    slot_dev = dest_ref.shape[0]
    filled = dest_ref[0] == owner
    for slot in range(1, slot_dev):
        filled = filled | (dest_ref[slot] == owner)
    row_len = tok_ref.shape[1]
    out_ref[0, :row_len, :] = tok_ref[0]
    slots = dest64_ref.shape[1]
    lane = lax.broadcasted_iota(jnp.int32, (pair_ref.shape[0], slots), 1)
    first = pair_ref[:, 0:1]
    second = pair_ref[:, 1:2]
    at_first = (lane == first).astype(F32)
    at_second = (lane == second).astype(F32)
    partner = column_sum(at_first * second.astype(F32) + at_second * first.astype(F32))
    target = column_sum((at_first + at_second) * targ_ref[...])
    high, middle, low = split_three(target)
    labels = seg_ref[0].astype(F32)
    labels = jnp.where(filled, labels, -1.0)
    rows = [
        labels,
        jnp.pad(dest64_ref[...].astype(F32), ((0, 0), (0, LANES - slots))),
        jnp.pad(partner, ((0, 0), (0, LANES - slots))),
        jnp.pad(high.astype(F32), ((0, 0), (0, LANES - slots))),
        jnp.pad(middle.astype(F32), ((0, 0), (0, LANES - slots))),
        jnp.pad(low.astype(F32), ((0, 0), (0, LANES - slots))),
    ]
    rows.append(jnp.zeros((META_ROWS - len(rows), LANES), F32))
    out_ref[0, row_len:, :LANES] = jnp.concatenate(rows, axis=0).astype(BF16)
    out_ref[0, row_len:, LANES:] = jnp.zeros((META_ROWS, out_ref.shape[2] - LANES), BF16)


def build_send(tokens, segments, destination, pair_index, targets, wide_count):
    slot_dev, row_len, width = tokens.shape

    def source(owner, dest_ref):
        found = jnp.int32(0)
        for slot in range(slot_dev):
            found = jnp.where(dest_ref[slot] == owner, slot, found)
        return found

    whole = lambda owner, dest_ref: (0, 0)
    slots = slot_dev * SEG_ROW
    pairs = pair_index.shape[0]
    return pl.pallas_call(
        prep_kernel,
        out_shape=jax.ShapeDtypeStruct((wide_count, row_len + META_ROWS, width), BF16),
        grid_spec=pltpu.PrefetchScalarGridSpec(
            num_scalar_prefetch=1,
            grid=(wide_count,),
            in_specs=[
                pl.BlockSpec((1, row_len, width), lambda o, d: (source(o, d), 0, 0)),
                pl.BlockSpec((1, 1, row_len), lambda o, d: (source(o, d), 0, 0)),
                pl.BlockSpec((1, slots), whole),
                pl.BlockSpec((pairs, 2), whole),
                pl.BlockSpec((pairs, 1), whole),
            ],
            out_specs=pl.BlockSpec((1, row_len + META_ROWS, width), lambda o, d: (o, 0, 0)),
        ),
        compiler_params=params(1),
        name="build_send",
    )(
        destination,
        tokens,
        segments.reshape(slot_dev, 1, row_len),
        jnp.repeat(destination, SEG_ROW).reshape(1, slots),
        pair_index,
        targets.reshape(pairs, 1),
    )


def attend_kernel(
    got_ref,
    wqkv_ref,
    bias_ref,
    wo_ref,
    bo_ref,
    gain_ref,
    shift_ref,
    x_ref,
    proj_ref,
    probs_ref,
    ctx_ref,
    hid_ref,
    low_ref,
    norm_ref,
    rstd_ref,
    lab_ref,
    labcol_ref,
):
    wide_count = got_ref.shape[0]
    tok_count, width = x_ref.shape
    row_len = got_ref.shape[1] - META_ROWS
    kept_rows = tok_count // row_len
    seen = jnp.int32(0)
    sources = [jnp.int32(0)] * kept_rows
    for slot in range(wide_count):
        top = jnp.max(got_ref[slot, row_len : row_len + 1, :LANES].astype(F32))
        live = top >= 0.0
        for row in range(kept_rows):
            sources[row] = jnp.where(live & (seen == row), slot, sources[row])
        seen = seen + live.astype(jnp.int32)
    for row in range(kept_rows):
        span = pl.ds(row * row_len, row_len)
        x_ref[span, :] = got_ref[sources[row], :row_len, :]
        tag = got_ref[sources[row], row_len : row_len + 1, :LANES].astype(F32)
        lab_ref[row : row + 1, :] = tag
        labcol_ref[span, :] = jnp.broadcast_to(tag, (LANES, LANES)).T
    total_cols = proj_ref.shape[1]
    tile = 256
    for start in range(0, total_cols, tile):
        cols = slice(start, start + tile)
        proj_ref[:, cols] = (dot(x_ref[...], wqkv_ref[:, cols]) + bias_ref[:, cols]).astype(BF16)

    scale = 1.0 / math.sqrt(HEAD_DIM)
    lane = lax.broadcasted_iota(jnp.int32, (row_len, LANES), 1)
    left = (lane < HEAD_DIM).astype(BF16)
    right = (lane >= HEAD_DIM).astype(BF16)

    def attend_row(row, carry):
        span = pl.ds(pl.multiple_of(row * row_len, row_len), row_len)
        same = labcol_ref[span, :] == lab_ref[pl.ds(row, 1), :]
        same = jnp.concatenate([same, same], axis=0)
        for pair in range(width // LANES):
            col = pair * LANES
            queries = proj_ref[span, col : col + LANES]
            key_rows = proj_ref[span, width + col : width + col + LANES]
            values = proj_ref[span, 2 * width + col : 2 * width + col + LANES]
            both = jnp.concatenate([queries * left, queries * right], axis=0)
            scores = jnp.where(same, dot(both, key_rows, NT) * scale, NEG_FILL)
            top = jnp.max(scores, axis=-1, keepdims=True)
            expo = jnp.exp(scores - top)
            total = jnp.sum(expo, axis=-1, keepdims=True)
            probs = (expo / total).astype(BF16)
            probs_ref[row, pair] = probs
            wide_probs = jnp.concatenate([probs[:row_len], probs[row_len:]], axis=1)
            split_values = jnp.concatenate([values * left, values * right], axis=0)
            ctx_ref[span, col : col + LANES] = dot(wide_probs, split_values).astype(BF16)
        return carry

    lax.fori_loop(0, kept_rows, attend_row, 0)
    for row in range(kept_rows):
        span = pl.ds(row * row_len, row_len)
        total = x_ref[span, :].astype(F32) + dot(ctx_ref[span, :], wo_ref[...]) + bo_ref[...]
        centered = total - row_mean(total)
        rstd = lax.rsqrt(row_mean(centered * centered) + NORM_EPS)
        normed = centered * rstd
        hidden = normed * gain_ref[...] + shift_ref[...]
        norm_ref[span, :] = normed
        rstd_ref[span, :] = rstd
        hid_ref[span, :] = hidden
        low_ref[span, :] = hidden.astype(BF16)


def attend_forward(got, w_qkv, bias, w_o, b_o, gain, shift, kept_rows):
    wide_count, slot_len, width = got.shape
    row_len = slot_len - META_ROWS
    tok_count = kept_rows * row_len
    shapes = (
        ((tok_count, width), BF16),
        ((tok_count, 3 * width), BF16),
        ((kept_rows, width // LANES, 2 * row_len, row_len), BF16),
        ((tok_count, width), BF16),
        ((tok_count, width), F32),
        ((tok_count, width), BF16),
        ((tok_count, width), F32),
        ((tok_count, 1), F32),
        ((8, LANES), F32),
        ((tok_count, LANES), F32),
    )
    return pl.pallas_call(
        attend_kernel,
        out_shape=[jax.ShapeDtypeStruct(*item) for item in shapes],
        in_specs=[vmem_spec()] * 7,
        out_specs=[vmem_spec()] * len(shapes),
        compiler_params=params(),
        name="attend_forward",
    )(got, w_qkv, bias, w_o, b_o, gain, shift)


def feed_kernel(
    low_ref,
    hid_ref,
    win_ref,
    bin_ref,
    wout_ref,
    bout_ref,
    gain_ref,
    shift_ref,
    lab_ref,
    act_ref,
    slope_ref,
    enc_ref,
    norm_ref,
    rstd_ref,
    pooled_ref,
    total_ref,
):
    step = pl.program_id(0)
    up = dot(low_ref[...], win_ref[...]) + bin_ref[...]
    phi = 0.5 * (1.0 + lax.erf(up * (1.0 / math.sqrt(2.0))))
    density = jnp.exp(-0.5 * up * up) * (1.0 / math.sqrt(2.0 * math.pi))
    act = (up * phi).astype(BF16)
    act_ref[...] = act
    slope_ref[...] = (phi + up * density).astype(BF16)
    part = dot(act, wout_ref[...])

    @pl.when(step == 0)
    def _():
        total_ref[...] = part + (hid_ref[...] + bout_ref[...])

    @pl.when(step > 0)
    def _():
        total_ref[...] += part

    @pl.when(step == pl.num_programs(0) - 1)
    def _():
        tok_count, width = total_ref.shape
        kept_rows = tok_count // LANES
        for row in range(kept_rows):
            span = slice(row * LANES, (row + 1) * LANES)
            total = total_ref[span, :]
            centered = total - row_mean(total)
            rstd = lax.rsqrt(row_mean(centered * centered) + NORM_EPS)
            normed = centered * rstd
            out = normed * gain_ref[...] + shift_ref[...]
            norm_ref[span, :] = normed
            rstd_ref[span, :] = rstd
            enc_ref[span, :] = out.astype(BF16)
            segment = lax.broadcasted_iota(jnp.int32, (SEG_ROW, LANES), 0).astype(F32)
            onehot = (lab_ref[row : row + 1, :] == segment).astype(F32)
            count = jnp.sum(onehot, axis=1, keepdims=True)
            high, middle, low = split_three(out)
            mask = onehot.astype(BF16)
            summed = dot(mask, high) + dot(mask, middle) + dot(mask, low)
            pooled_ref[row * SEG_ROW : (row + 1) * SEG_ROW, :] = (summed / count).astype(BF16)


def feed_forward(low, hidden, w_in, b_in, w_out, b_out, gain, shift, labels):
    tok_count, width = low.shape
    units = w_in.shape[1]
    tile = 512
    kept_rows = tok_count // LANES
    whole = lambda step: (0, 0)
    shapes = (
        ((tok_count, units), BF16),
        ((tok_count, units), BF16),
        ((tok_count, width), BF16),
        ((tok_count, width), F32),
        ((tok_count, 1), F32),
        ((kept_rows * SEG_ROW, width), BF16),
    )
    return pl.pallas_call(
        feed_kernel,
        out_shape=[jax.ShapeDtypeStruct(*item) for item in shapes],
        grid_spec=pltpu.PrefetchScalarGridSpec(
            num_scalar_prefetch=0,
            grid=(units // tile,),
            in_specs=[
                pl.BlockSpec((tok_count, width), whole),
                pl.BlockSpec((tok_count, width), whole),
                pl.BlockSpec((width, tile), lambda step: (0, step)),
                pl.BlockSpec((1, tile), lambda step: (0, step)),
                pl.BlockSpec((tile, width), lambda step: (step, 0)),
                pl.BlockSpec((1, width), whole),
                pl.BlockSpec((1, width), whole),
                pl.BlockSpec((1, width), whole),
                pl.BlockSpec((8, LANES), whole),
            ],
            out_specs=[
                pl.BlockSpec((tok_count, tile), lambda step: (0, step)),
                pl.BlockSpec((tok_count, tile), lambda step: (0, step)),
                pl.BlockSpec((tok_count, width), whole),
                pl.BlockSpec((tok_count, width), whole),
                pl.BlockSpec((tok_count, 1), whole),
                pl.BlockSpec((kept_rows * SEG_ROW, width), whole),
            ],
            scratch_shapes=[pltpu.VMEM((tok_count, width), F32)],
        ),
        compiler_params=params(1),
        name="feed_forward",
    )(low, hidden, w_in, b_in, w_out, b_out, gain, shift, labels)


def route_kernel(me_ref, meta_ref, pair_ref, place_ref, targ_ref, first_ref, second_ref, back_ref):
    wide_count = meta_ref.shape[0]
    me = me_ref[0]
    kept_rows = place_ref.shape[0] // SEG_ROW
    me_f = me.astype(F32)

    def table(row):
        return jnp.concatenate(
            [meta_ref[j, row : row + 1, :LANES].astype(F32) for j in range(wide_count)], axis=0
        )

    labels = table(0)
    dest = table(1)
    lane = lax.broadcasted_iota(jnp.int32, (wide_count, LANES), 1)
    slots = SEG_ROW * 2 * kept_rows
    dest = jnp.where(lane < slots, dest, -1.0)
    partner = table(2)
    target = table(3) + table(4) + table(5)
    sends = jnp.zeros((wide_count, LANES), F32)
    for owner in range(wide_count):
        to_owner = jnp.max((dest == float(owner)).astype(F32), axis=1, keepdims=True)
        sends = sends + jnp.where(lane == owner, to_owner, 0.0)
    row_id = lax.broadcasted_iota(jnp.int32, (wide_count, wide_count), 0)
    col_id = lax.broadcasted_iota(jnp.int32, (wide_count, wide_count), 1)
    below = (col_id < row_id).astype(BF16)
    earlier = dot(below, sends.astype(BF16))
    rank = jnp.zeros((wide_count, LANES), F32)
    for owner in range(wide_count):
        rank = rank + jnp.where(dest == float(owner), earlier[:, owner : owner + 1], 0.0)
    segment = (lane % SEG_ROW).astype(F32)
    per_owner = float(kept_rows * SEG_ROW)
    place = jnp.where(dest >= 0.0, dest * per_owner + rank * float(SEG_ROW) + segment, -1.0)
    live = (labels[:, 0:1] >= 0.0).astype(F32)
    my_rank = dot(below, jnp.broadcast_to(live, (wide_count, LANES)).astype(BF16))
    back = jnp.clip(my_rank, 0.0, float(kept_rows - 1))
    diagonal = lax.broadcasted_iota(jnp.int32, (wide_count, LANES), 0) == lane
    back_ref[...] = column_sum(jnp.where(diagonal, back, 0.0)).astype(jnp.int32)
    seg_lane = lax.broadcasted_iota(jnp.int32, (SEG_ROW, LANES), 1)
    seg_id = lax.broadcasted_iota(jnp.int32, (SEG_ROW, LANES), 0)
    for row in range(kept_rows):
        chosen = (live > 0.0) & (my_rank[:, 0:1] == float(row))
        pick = lambda values: column_sum(jnp.where(chosen, values, 0.0))
        own = (pick(dest) == me_f) & (seg_lane % SEG_ROW == seg_id)
        gather = lambda mask, values: jnp.sum(jnp.where(mask, values, 0.0), axis=1, keepdims=True)
        other = gather(own, pick(partner))
        at_other = seg_lane.astype(F32) == other
        out = slice(row * SEG_ROW, (row + 1) * SEG_ROW)
        place_ref[out, :] = gather(at_other, pick(place))
        targ_ref[out, :] = gather(own, pick(target))
    mine = lax.broadcasted_iota(jnp.int32, (wide_count, LANES), 0) == me
    my_place = column_sum(jnp.where(mine, place, 0.0))
    pair_lane = lax.broadcasted_iota(jnp.int32, (pair_ref.shape[0], LANES), 1)
    for column, out_ref in ((0, first_ref), (1, second_ref)):
        at_slot = pair_lane == pair_ref[:, column : column + 1]
        out_ref[...] = jnp.sum(jnp.where(at_slot, my_place, 0.0), axis=1, keepdims=True)


def route(me, meta, pair_index, kept_rows):
    wide_count = meta.shape[0]
    own = kept_rows * SEG_ROW
    pairs = pair_index.shape[0]
    shapes = (
        ((own, 1), F32),
        ((own, 1), F32),
        ((pairs, 1), F32),
        ((pairs, 1), F32),
        ((1, LANES), jnp.int32),
    )
    return pl.pallas_call(
        route_kernel,
        out_shape=[jax.ShapeDtypeStruct(*item) for item in shapes],
        in_specs=[pl.BlockSpec(memory_space=pltpu.SMEM), vmem_spec(), vmem_spec()],
        out_specs=[vmem_spec()] * len(shapes),
        compiler_params=params(),
        name="route",
    )(me, meta, pair_index)


def pick_rows(place_ref, all_ref):
    lane = lax.broadcasted_iota(jnp.int32, (place_ref.shape[0], all_ref.shape[0]), 1)
    return dot((lane.astype(F32) == place_ref[...]).astype(BF16), all_ref[...])


def cosine_parts(left, right):
    inner = row_mean(left * right)
    left_inv = lax.rsqrt(row_mean(left * left) + COS_EPS)
    right_inv = lax.rsqrt(row_mean(right * right) + COS_EPS)
    return (inner, left_inv, right_inv)


def cosine_kernel(first_ref, second_ref, all_ref, sim_ref):
    left = pick_rows(first_ref, all_ref)
    right = pick_rows(second_ref, all_ref)
    inner, left_inv, right_inv = cosine_parts(left, right)
    sim = inner * left_inv * right_inv
    sim_ref[...] = jnp.where(first_ref[...] >= 0.0, sim, 0.0)


def cosine_pairs(first, second, pooled_all):
    return pl.pallas_call(
        cosine_kernel,
        out_shape=jax.ShapeDtypeStruct(first.shape, F32),
        in_specs=[vmem_spec()] * 3,
        out_specs=vmem_spec(),
        compiler_params=params(),
        name="cosine_pairs",
    )(first, second, pooled_all)


def norm_back(grad, normed, rstd, gain):
    scaled = grad * gain
    return rstd * (scaled - row_mean(scaled) - normed * row_mean(scaled * normed))


def loss_back_kernel(
    own_ref,
    all_ref,
    place_ref,
    targ_ref,
    lab_ref,
    labcol_ref,
    norm_ref,
    rstd_ref,
    gain_ref,
    dres_ref,
    dffn_ref,
    dffn_t_ref,
    sums_ref,
):
    tok_count, width = norm_ref.shape
    kept_rows = tok_count // LANES
    left = own_ref[...].astype(F32)
    right = pick_rows(place_ref, all_ref)
    inner, left_inv, right_inv = cosine_parts(left, right)
    error = 2.0 * (inner * left_inv * right_inv - targ_ref[...])
    factor = error * left_inv * right_inv * (1.0 / width)
    d_pooled = (factor * (right - left * (inner * left_inv * left_inv))).astype(BF16).astype(F32)
    gain_sum = jnp.zeros((1, width), F32)
    shift_sum = jnp.zeros((1, width), F32)
    bias_sum = jnp.zeros((1, width), F32)
    lane = lax.broadcasted_iota(jnp.int32, (LANES, LANES), 1).astype(F32)
    for row in range(kept_rows):
        span = slice(row * LANES, (row + 1) * LANES)
        segment = lax.broadcasted_iota(jnp.int32, (SEG_ROW, LANES), 0).astype(F32)
        count = jnp.sum(
            (lab_ref[row : row + 1, :] == segment).astype(F32), axis=1, keepdims=True
        )
        per_token = d_pooled[row * SEG_ROW : (row + 1) * SEG_ROW, :] / count
        shift_sum = shift_sum + column_sum(per_token * count)
        padded = jnp.concatenate([per_token, jnp.zeros((LANES - SEG_ROW, width), F32)], axis=0)
        onehot = (labcol_ref[span, :] == lane).astype(BF16)
        high, middle, low = split_three(padded)
        d_out = dot(onehot, high) + dot(onehot, middle) + dot(onehot, low)
        normed = norm_ref[span, :]
        d_res = norm_back(d_out, normed, rstd_ref[span, :], gain_ref[...])
        d_low = d_res.astype(BF16)
        dres_ref[span, :] = d_res
        dffn_ref[span, :] = d_low
        dffn_t_ref[:, span] = d_low.T
        gain_sum = gain_sum + column_sum(d_out * normed)
        bias_sum = bias_sum + column_sum(d_low.astype(F32))
    sums_ref[0:1, :] = gain_sum
    sums_ref[1:2, :] = shift_sum
    sums_ref[2:3, :] = bias_sum
    sums_ref[3:8, :] = jnp.zeros((5, width), F32)


def loss_back(own, pooled_all, place, target, labels, label_cols, normed, rstd, gain):
    tok_count, width = normed.shape
    shapes = (
        ((tok_count, width), F32),
        ((tok_count, width), BF16),
        ((width, tok_count), BF16),
        ((8, width), F32),
    )
    return pl.pallas_call(
        loss_back_kernel,
        out_shape=[jax.ShapeDtypeStruct(*item) for item in shapes],
        in_specs=[vmem_spec()] * 9,
        out_specs=[vmem_spec()] * len(shapes),
        compiler_params=params(),
        name="loss_back",
    )(own, pooled_all, place, target, labels, label_cols, normed, rstd, gain)


def feed_back_kernel(
    dffn_ref,
    dres_ref,
    wout_ref,
    win_ref,
    slope_ref,
    norm_ref,
    rstd_ref,
    gain_ref,
    wo_ref,
    dup_t_ref,
    bsum_ref,
    done_ref,
    dattn_t_ref,
    dctx_ref,
    sums_ref,
    total_ref,
):
    step = pl.program_id(0)
    d_up = (dot(dffn_ref[...], wout_ref[...], NT) * slope_ref[...].astype(F32)).astype(BF16)
    dup_t_ref[...] = d_up.T
    bsum_ref[...] = column_sum(d_up.astype(F32))
    part = dot(d_up, win_ref[...], NT)

    @pl.when(step == 0)
    def _():
        total_ref[...] = part + dres_ref[...]

    @pl.when(step > 0)
    def _():
        total_ref[...] += part

    @pl.when(step == pl.num_programs(0) - 1)
    def _():
        tok_count, width = total_ref.shape
        kept_rows = tok_count // LANES
        gain_sum = jnp.zeros((1, width), F32)
        shift_sum = jnp.zeros((1, width), F32)
        bias_sum = jnp.zeros((1, width), F32)
        for row in range(kept_rows):
            span = slice(row * LANES, (row + 1) * LANES)
            d_hidden = total_ref[span, :]
            normed = norm_ref[span, :]
            d_res = norm_back(d_hidden, normed, rstd_ref[span, :], gain_ref[...])
            d_low = d_res.astype(BF16)
            done_ref[span, :] = d_res
            dattn_t_ref[:, span] = d_low.T
            dctx_ref[span, :] = dot(d_low, wo_ref[...], NT).astype(BF16)
            gain_sum = gain_sum + column_sum(d_hidden * normed)
            shift_sum = shift_sum + column_sum(d_hidden)
            bias_sum = bias_sum + column_sum(d_low.astype(F32))
        sums_ref[0:1, :] = gain_sum
        sums_ref[1:2, :] = shift_sum
        sums_ref[2:3, :] = bias_sum
        sums_ref[3:8, :] = jnp.zeros((5, width), F32)


def feed_back(d_ffn, d_res, w_out, w_in, slope, normed, rstd, gain, w_o):
    tok_count, width = d_ffn.shape
    units = w_in.shape[1]
    tile = 512
    whole = lambda step: (0, 0)
    shapes = (
        ((units, tok_count), BF16),
        ((1, units), F32),
        ((tok_count, width), F32),
        ((width, tok_count), BF16),
        ((tok_count, width), BF16),
        ((8, width), F32),
    )
    return pl.pallas_call(
        feed_back_kernel,
        out_shape=[jax.ShapeDtypeStruct(*item) for item in shapes],
        grid_spec=pltpu.PrefetchScalarGridSpec(
            num_scalar_prefetch=0,
            grid=(units // tile,),
            in_specs=[
                pl.BlockSpec((tok_count, width), whole),
                pl.BlockSpec((tok_count, width), whole),
                pl.BlockSpec((tile, width), lambda step: (step, 0)),
                pl.BlockSpec((width, tile), lambda step: (0, step)),
                pl.BlockSpec((tok_count, tile), lambda step: (0, step)),
                pl.BlockSpec((tok_count, width), whole),
                pl.BlockSpec((tok_count, 1), whole),
                pl.BlockSpec((1, width), whole),
                pl.BlockSpec((width, width), whole),
            ],
            out_specs=[
                pl.BlockSpec((tile, tok_count), lambda step: (step, 0)),
                pl.BlockSpec((1, tile), lambda step: (0, step)),
                pl.BlockSpec((tok_count, width), whole),
                pl.BlockSpec((width, tok_count), whole),
                pl.BlockSpec((tok_count, width), whole),
                pl.BlockSpec((8, width), whole),
            ],
            scratch_shapes=[pltpu.VMEM((tok_count, width), F32)],
        ),
        compiler_params=params(1),
        name="feed_back",
    )(d_ffn, d_res, w_out, w_in, slope, normed, rstd, gain, w_o)


def attend_back_kernel(
    proj_ref, probs_ref, dctx_ref, done_ref, wqkv_ref, dproj_t_ref, dtok_ref, sums_ref, dproj_ref
):
    row = pl.program_id(0)
    row_len, width = dctx_ref.shape
    scale = 1.0 / math.sqrt(HEAD_DIM)
    lane = lax.broadcasted_iota(jnp.int32, (row_len, LANES), 1)
    left = (lane < HEAD_DIM).astype(BF16)
    right = (lane >= HEAD_DIM).astype(BF16)

    def twice(values):
        return jnp.concatenate([values * left, values * right], axis=0)

    for pair in range(width // LANES):
        col = pair * LANES
        queries = proj_ref[:, col : col + LANES]
        key_rows = proj_ref[:, width + col : width + col + LANES]
        values = proj_ref[:, 2 * width + col : 2 * width + col + LANES]
        probs = probs_ref[0, pair]
        d_ctx = twice(dctx_ref[:, col : col + LANES])
        d_probs = dot(d_ctx, values, NT)
        probs_f = probs.astype(F32)
        inner = jnp.sum(probs_f * d_probs, axis=-1, keepdims=True)
        d_scores = (probs_f * (d_probs - inner)).astype(BF16)
        wide_scores = jnp.concatenate([d_scores[:row_len], d_scores[row_len:]], axis=1)
        d_query = dot(wide_scores, twice(key_rows)) * scale
        d_key = dot(d_scores, twice(queries), TN) * scale
        d_value = dot(probs, d_ctx, TN)
        for part, grad in ((0, d_query), (1, d_key), (2, d_value)):
            low = grad.astype(BF16)
            place = part * width + col
            dproj_ref[:, place : place + LANES] = low
            dproj_t_ref[place : place + LANES, :] = low.T
            summed = column_sum(low.astype(F32))

            @pl.when(row == 0)
            def _():
                sums_ref[:, place : place + LANES] = summed

            @pl.when(row > 0)
            def _():
                sums_ref[:, place : place + LANES] += summed

    grad = done_ref[...] + dot(dproj_ref[...], wqkv_ref[...], NT)
    dtok_ref[...] = grad.astype(BF16)


def attend_back(proj, probs, d_ctx, d_one, w_qkv):
    tok_count, width = d_ctx.shape
    kept_rows = tok_count // LANES
    shapes = (
        ((3 * width, tok_count), BF16),
        ((tok_count, width), BF16),
        ((1, 3 * width), F32),
    )
    return pl.pallas_call(
        attend_back_kernel,
        out_shape=[jax.ShapeDtypeStruct(*item) for item in shapes],
        grid_spec=pltpu.PrefetchScalarGridSpec(
            num_scalar_prefetch=0,
            grid=(kept_rows,),
            in_specs=[
                pl.BlockSpec((LANES, 3 * width), lambda row: (row, 0)),
                pl.BlockSpec((1,) + probs.shape[1:], lambda row: (row, 0, 0, 0)),
                pl.BlockSpec((LANES, width), lambda row: (row, 0)),
                pl.BlockSpec((LANES, width), lambda row: (row, 0)),
                pl.BlockSpec((width, 3 * width), lambda row: (0, 0)),
            ],
            out_specs=[
                pl.BlockSpec((3 * width, LANES), lambda row: (0, row)),
                pl.BlockSpec((LANES, width), lambda row: (row, 0)),
                pl.BlockSpec((1, 3 * width), lambda row: (0, 0)),
            ],
            scratch_shapes=[pltpu.VMEM((LANES, 3 * width), BF16)],
        ),
        compiler_params=params(1),
        name="attend_back",
    )(proj, probs, d_ctx, d_one, w_qkv)


def spread_kernel(index_ref, rows_ref, out_ref):
    out_ref[...] = rows_ref[...]


def spread_rows(index, rows, count):
    block = (1,) + rows.shape[1:]
    return pl.pallas_call(
        spread_kernel,
        out_shape=jax.ShapeDtypeStruct((count,) + rows.shape[1:], rows.dtype),
        grid_spec=pltpu.PrefetchScalarGridSpec(
            num_scalar_prefetch=1,
            grid=(count,),
            in_specs=[pl.BlockSpec(block, lambda slot, idx: (idx[slot], 0, 0))],
            out_specs=pl.BlockSpec(block, lambda slot, idx: (slot, 0, 0)),
        ),
        compiler_params=params(1),
        name="spread_rows",
    )(index, rows)


def home_kernel(dest_ref, rows_ref, out_ref):
    live = dest_ref[pl.program_id(0)] >= 0

    @pl.when(live)
    def _():
        out_ref[...] = rows_ref[...]

    @pl.when(jnp.logical_not(live))
    def _():
        out_ref[...] = jnp.zeros_like(out_ref)


def home_rows(destination, rows):
    block = (1,) + rows.shape[1:]
    count = destination.shape[0]
    return pl.pallas_call(
        home_kernel,
        out_shape=jax.ShapeDtypeStruct((count,) + rows.shape[1:], rows.dtype),
        grid_spec=pltpu.PrefetchScalarGridSpec(
            num_scalar_prefetch=1,
            grid=(count,),
            in_specs=[
                pl.BlockSpec(block, lambda slot, dest: (jnp.maximum(dest[slot], 0), 0, 0))
            ],
            out_specs=pl.BlockSpec(block, lambda slot, dest: (slot, 0, 0)),
        ),
        compiler_params=params(1),
        name="home_rows",
    )(destination, rows)


def swap(values, axis, bit):
    count = lax.axis_size(axis)
    return lax.ppermute(values, axis, [(i, i ^ (1 << bit)) for i in range(count)])


def pick(values, dim, index):
    return lax.dynamic_index_in_dim(values, index, dim, keepdims=False)


def add_low(kept, received):
    return (kept.astype(F32) + received.astype(F32)).astype(BF16)


def half_terms(lefts, rights, side):
    wide_count = lax.axis_size("wide")
    parts = []
    for left, right in zip(lefts, rights):
        rows = left.shape[0] // wide_count
        chosen = pick(left.reshape(wide_count // 2, 2, rows, left.shape[1]), 1, side)
        parts.append(
            jnp.einsum("prt,tk->prk", chosen, right, preferred_element_type=F32)
        )
    return parts[0] if len(parts) == 1 else jnp.concatenate(parts, axis=1)


def reduce_wide(lefts, rights, order):
    place = lax.axis_index("wide")
    wide_count = lax.axis_size("wide")
    bits = wide_count.bit_length() - 1
    mine = place & 1
    sent = half_terms(lefts, rights, 1 - mine).astype(BF16)
    received = swap(sent, "wide", 0)
    held = (half_terms(lefts, rights, mine) + received.astype(F32)).astype(BF16)
    held = held.reshape((2,) * (bits - 1) + held.shape[1:])
    left_bits = list(range(bits - 1, 0, -1))
    for bit in order:
        dim = left_bits.index(bit)
        side = (place >> bit) & 1
        received = swap(pick(held, dim, 1 - side), "wide", bit)
        held = add_low(pick(held, dim, side), received)
        left_bits.remove(bit)
    return held


def sum_pieces(pieces):
    received = lax.all_to_all(pieces, "narrow", split_axis=0, concat_axis=0, tiled=True)
    return jnp.sum(received.astype(F32), axis=0)


def sum_vectors(values):
    for axis in ("wide", "narrow"):
        count = lax.axis_size(axis)
        for bit in range(count.bit_length() - 1):
            values = values + swap(values, axis, bit)
    return values


def on_device(
    tokens,
    segments,
    destination,
    pair_index,
    targets,
    w_qkv,
    b_qv,
    w_o,
    b_o,
    gain_one,
    shift_one,
    w_in,
    b_in,
    w_out,
    b_out,
    gain_two,
    shift_two,
):
    wide_count = lax.axis_size("wide")
    narrow_count = lax.axis_size("narrow")
    slot_dev, row_len, width = tokens.shape
    kept_rows = slot_dev // 2
    units = w_in.shape[1]
    me = lax.axis_index("wide")
    line = lambda vector: vector.reshape(1, -1)

    sent = build_send(tokens, segments, destination, pair_index, targets, wide_count)
    got = lax.all_to_all(sent, "wide", split_axis=0, concat_axis=0, tiled=True)
    full_bias = jnp.concatenate(
        [b_qv[:width], jnp.zeros((width,), F32), b_qv[width:]]
    ).reshape(1, 3 * width)
    x, proj, probs, context, hidden, hidden_low, norm_one, rstd_one, labels, label_cols = (
        attend_forward(
            got, w_qkv, full_bias, w_o, line(b_o), line(gain_one), line(shift_one), kept_rows
        )
    )
    act, slope, encoded, norm_two, rstd_two, pooled = feed_forward(
        hidden_low,
        hidden,
        w_in,
        line(b_in),
        w_out,
        line(b_out),
        line(gain_two),
        line(shift_two),
        labels,
    )
    place, target, first, second, back = route(
        me.astype(jnp.int32).reshape(1), got[:, row_len:, :], pair_index, kept_rows
    )
    pooled_all = lax.all_to_all(
        jnp.broadcast_to(pooled[None], (wide_count,) + pooled.shape),
        "wide",
        split_axis=0,
        concat_axis=0,
        tiled=True,
    ).reshape(wide_count * kept_rows * SEG_ROW, width)
    similarity = cosine_pairs(first, second, pooled_all).reshape(-1)
    d_res_two, d_ffn, d_ffn_t, sums_two = loss_back(
        pooled, pooled_all, place, target, labels, label_cols, norm_two, rstd_two, line(gain_two)
    )

    bits = wide_count.bit_length() - 1
    half = 1 + (bits - 1) // 2
    low_first = list(range(1, bits))
    high_first = list(range(half, bits)) + list(range(1, half))

    sum_out = reduce_wide([d_ffn_t], [act], low_first)
    d_up_t, sum_b_in, d_one, d_attn_t, d_ctx, sums_one = feed_back(
        d_ffn, d_res_two, w_out, w_in, slope, norm_one, rstd_one, line(gain_one), w_o
    )
    sum_in = reduce_wide([d_up_t], [hidden_low], high_first)
    d_proj_t, d_rows, sums_qkv = attend_back(proj, probs, d_ctx, d_one, w_qkv)
    sum_mix = reduce_wide([d_proj_t, d_attn_t], [x, context], low_first)

    home = lax.all_to_all(
        spread_rows(back[0, :wide_count], d_rows.reshape(kept_rows, row_len, width), wide_count),
        "wide",
        split_axis=0,
        concat_axis=0,
        tiled=True,
    )
    grad_tokens = home_rows(destination, home)

    rows_out = sum_out.shape[0]
    cols_out = units // narrow_count
    pieces_out = sum_out.reshape(rows_out, narrow_count, cols_out).transpose(1, 0, 2)
    grad_w_out = sum_pieces(pieces_out).T
    rows_in = width // narrow_count
    grad_w_in = sum_pieces(sum_in.T.reshape(narrow_count, rows_in, sum_in.shape[0]))
    grad_mix = sum_pieces(sum_mix.T.reshape(narrow_count, rows_in, sum_mix.shape[0]))
    cols_qkv = 3 * width // wide_count
    grad_w_qkv = grad_mix[:, :cols_qkv]
    grad_w_o = grad_mix[:, cols_qkv:]

    vectors = jnp.concatenate(
        [
            sums_qkv[0, :width],
            sums_qkv[0, 2 * width :],
            sums_one[2],
            sums_one[0],
            sums_one[1],
            sum_b_in[0],
            sums_two[2],
            sums_two[0],
            sums_two[1],
        ]
    )
    vectors = sum_vectors(vectors.reshape(-1, LANES)).reshape(-1)
    cuts = (2 * width, width, width, width, units, width, width, width)
    outs = []
    start = 0
    for size in cuts:
        outs.append(vectors[start : start + size])
        start += size
    grad_b_qv, grad_b_o, grad_gain_one, grad_shift_one = outs[:4]
    grad_b_in, grad_b_out, grad_gain_two, grad_shift_two = outs[4:]
    return (
        encoded.reshape(kept_rows, row_len, width),
        similarity,
        grad_tokens,
        grad_w_qkv,
        grad_b_qv,
        grad_w_o,
        grad_b_o,
        grad_gain_one,
        grad_shift_one,
        grad_w_in,
        grad_b_in,
        grad_w_out,
        grad_b_out,
        grad_gain_two,
        grad_shift_two,
    )


def solution(mesh):
    rows = ("wide", "narrow")
    in_specs = (P(rows, None, None), P(rows, None), P(rows), P(rows, None), P(rows)) + (P(),) * 12
    matrix = P("narrow", "wide")
    out_specs = (
        P(rows, None, None),
        P(rows),
        P(rows, None, None),
        matrix,
        P(),
        matrix,
        P(),
        P(),
        P(),
        matrix,
        P(),
        matrix,
        P(),
        P(),
        P(),
    )
    return jax.shard_map(
        on_device, mesh=mesh, in_specs=in_specs, out_specs=out_specs, check_vma=False
    )
```

```python
import functools
import math

import jax
import jax.numpy as jnp
from jax import lax
from jax.experimental import pallas as pl
from jax.experimental.pallas import tpu as pltpu
from jax.sharding import PartitionSpec as P

HEAD_DIM = 64
SEG_ROW = 8
LANES = 128
META_ROWS = 16
NEG_FILL = -1e30
NORM_EPS = 1e-12
COS_EPS = 1e-06
F32 = jnp.float32
BF16 = jnp.bfloat16
VMEM_LIMIT = 24 * 1024 * 1024


def cost(micros):
    return pl.CostEstimate(flops=0, bytes_accessed=int(micros * 3.0e6), transcendentals=0)


NT = (((1,), (1,)), ((), ()))
TN = (((0,), (0,)), ((), ()))


def vmem_spec():
    return pl.BlockSpec(memory_space=pltpu.VMEM)


def params(steps=0):
    return pltpu.CompilerParams(
        dimension_semantics=("arbitrary",) * steps if steps else None,
        vmem_limit_bytes=VMEM_LIMIT,
    )


def split_three(values):
    high = values.astype(BF16)
    rest = values - high.astype(F32)
    middle = rest.astype(BF16)
    low = (rest - middle.astype(F32)).astype(BF16)
    return (high, middle, low)


def dot(left, right, dims=None):
    if dims is None:
        return jnp.dot(left, right, preferred_element_type=F32)
    return lax.dot_general(left, right, dims, preferred_element_type=F32)


def column_sum(values):
    return jnp.sum(values, axis=0, keepdims=True)


def row_mean(values):
    return jnp.mean(values, axis=-1, keepdims=True)


def prep_kernel(dest_ref, pair_ref, targ_ref, tok_ref, seg_ref, out_ref, sems):
    slot_dev = dest_ref.shape[0]
    wide_count, _, width = out_ref.shape
    row_len = tok_ref.shape[1]
    sources = []
    lives = []
    copies = []
    for owner in range(wide_count):
        found = jnp.int32(0)
        live = dest_ref[0] == owner
        for slot in range(1, slot_dev):
            match = dest_ref[slot] == owner
            found = jnp.where(match, slot, found)
            live = live | match
        sources.append(found)
        lives.append(live)
        copy = pltpu.make_async_copy(
            tok_ref.at[found], out_ref.at[owner, pl.ds(0, row_len), :], sems.at[owner]
        )
        copy.start()
        copies.append(copy)
    lane = lax.broadcasted_iota(jnp.int32, (1, LANES), 1)
    dest = jnp.full((1, LANES), -1, jnp.int32)
    for slot in range(slot_dev):
        dest = jnp.where(lane // SEG_ROW == slot, dest_ref[slot], dest)
    partner = jnp.zeros((1, LANES), jnp.int32)
    target = jnp.zeros((1, LANES), F32)
    for pair in range(pair_ref.shape[1]):
        first = pair_ref[0, pair]
        second = pair_ref[1, pair]
        at_first = lane == first
        at_second = lane == second
        partner = jnp.where(at_first, second, jnp.where(at_second, first, partner))
        target = jnp.where(at_first | at_second, targ_ref[0, pair], target)
    high, middle, low = split_three(target)
    fixed = [dest.astype(F32), partner.astype(F32)]
    fixed += [high.astype(F32), middle.astype(F32), low.astype(F32)]
    fixed.append(jnp.zeros((META_ROWS - 1 - len(fixed), LANES), F32))
    for owner in range(wide_count):
        labels = seg_ref[pl.ds(sources[owner], 1), :].astype(F32)
        labels = jnp.where(lives[owner], labels, -1.0)
        table = jnp.concatenate([labels] + fixed, axis=0)
        out_ref[owner, row_len:, :LANES] = table.astype(BF16)
        out_ref[owner, row_len:, LANES:] = jnp.zeros((META_ROWS, width - LANES), BF16)
    for copy in copies:
        copy.wait()


def smem_spec():
    return pl.BlockSpec(memory_space=pltpu.SMEM)


def build_send(tokens, segments, destination, pair_index, targets, wide_count):
    slot_dev, row_len, width = tokens.shape
    return pl.pallas_call(
        prep_kernel,
        out_shape=jax.ShapeDtypeStruct((wide_count, row_len + META_ROWS, width), BF16),
        in_specs=[smem_spec()] * 3 + [pl.BlockSpec(memory_space=pl.ANY), vmem_spec()],
        out_specs=vmem_spec(),
        scratch_shapes=[pltpu.SemaphoreType.DMA((wide_count,))],
        cost_estimate=cost(3),
        compiler_params=params(),
        name="build_send",
    )(destination, pair_index.T, targets.reshape(1, -1), tokens, segments)


def attend_kernel(
    got_ref,
    wqkv_ref,
    bias_ref,
    wo_ref,
    bo_ref,
    gain_ref,
    shift_ref,
    stack_ref,
    proj_ref,
    probs_ref,
    hid_ref,
    norm_ref,
    rstd_ref,
    lab_ref,
    labcol_ref,
    meta_ref,
    source_ref,
):
    x_ref, ctx_ref, low_ref = stack_ref.at[0], stack_ref.at[1], stack_ref.at[2]
    wide_count = got_ref.shape[0]
    tok_count, width = hid_ref.shape
    row_len = got_ref.shape[1] - META_ROWS
    kept_rows = tok_count // row_len
    seen = jnp.int32(0)
    sources = [jnp.int32(0)] * kept_rows
    for slot in range(wide_count):
        top = jnp.max(got_ref[slot, row_len : row_len + 1, :LANES].astype(F32))
        live = top >= 0.0
        for row in range(kept_rows):
            sources[row] = jnp.where(live & (seen == row), slot, sources[row])
        seen = seen + live.astype(jnp.int32)
    meta_ref[...] = got_ref[:, row_len:, :LANES]
    for row in range(kept_rows):
        source_ref[row] = sources[row]
        span = pl.ds(row * row_len, row_len)
        x_ref[span, :] = got_ref[sources[row], :row_len, :]
        tag = got_ref[sources[row], row_len : row_len + 1, :LANES].astype(F32)
        lab_ref[row : row + 1, :] = tag
        labcol_ref[span, :] = jnp.broadcast_to(tag, (LANES, LANES)).T
    total_cols = proj_ref.shape[1]
    tile = 256
    for start in range(0, total_cols, tile):
        cols = slice(start, start + tile)
        proj_ref[:, cols] = (dot(x_ref[...], wqkv_ref[:, cols]) + bias_ref[:, cols]).astype(BF16)

    scale = 1.0 / math.sqrt(HEAD_DIM)
    lane = lax.broadcasted_iota(jnp.int32, (row_len, LANES), 1)
    left = (lane < HEAD_DIM).astype(BF16)
    right = (lane >= HEAD_DIM).astype(BF16)

    def attend_row(row, carry):
        span = pl.ds(pl.multiple_of(row * row_len, row_len), row_len)
        same = labcol_ref[span, :] == lab_ref[pl.ds(row, 1), :]
        same = jnp.concatenate([same, same], axis=0)
        for pair in range(width // LANES):
            col = pair * LANES
            queries = proj_ref[span, col : col + LANES]
            key_rows = proj_ref[span, width + col : width + col + LANES]
            values = proj_ref[span, 2 * width + col : 2 * width + col + LANES]
            both = jnp.concatenate([queries * left, queries * right], axis=0)
            scores = jnp.where(same, dot(both, key_rows, NT) * scale, NEG_FILL)
            top = jnp.max(scores, axis=-1, keepdims=True)
            expo = jnp.exp(scores - top)
            total = jnp.sum(expo, axis=-1, keepdims=True)
            probs = (expo / total).astype(BF16)
            probs_ref[row, pair] = probs
            wide_probs = jnp.concatenate([probs[:row_len], probs[row_len:]], axis=1)
            split_values = jnp.concatenate([values * left, values * right], axis=0)
            ctx_ref[span, col : col + LANES] = dot(wide_probs, split_values).astype(BF16)
        return carry

    lax.fori_loop(0, kept_rows, attend_row, 0)
    for row in range(kept_rows):
        span = pl.ds(row * row_len, row_len)
        total = x_ref[span, :].astype(F32) + dot(ctx_ref[span, :], wo_ref[...]) + bo_ref[...]
        centered = total - row_mean(total)
        rstd = lax.rsqrt(row_mean(centered * centered) + NORM_EPS)
        normed = centered * rstd
        hidden = normed * gain_ref[...] + shift_ref[...]
        norm_ref[span, :] = normed
        rstd_ref[span, :] = rstd
        hid_ref[span, :] = hidden
        low_ref[span, :] = hidden.astype(BF16)


def attend_forward(got, w_qkv, bias, w_o, b_o, gain, shift, kept_rows):
    wide_count, slot_len, width = got.shape
    row_len = slot_len - META_ROWS
    tok_count = kept_rows * row_len
    shapes = (
        ((3, tok_count, width), BF16),
        ((tok_count, 3 * width), BF16),
        ((kept_rows, width // LANES, 2 * row_len, row_len), BF16),
        ((tok_count, width), F32),
        ((tok_count, width), F32),
        ((tok_count, 1), F32),
        ((8, LANES), F32),
        ((tok_count, LANES), F32),
        ((wide_count, META_ROWS, LANES), BF16),
        ((kept_rows,), jnp.int32),
    )
    return pl.pallas_call(
        attend_kernel,
        out_shape=[jax.ShapeDtypeStruct(*item) for item in shapes],
        in_specs=[vmem_spec()] * 7,
        out_specs=[vmem_spec()] * (len(shapes) - 1) + [smem_spec()],
        cost_estimate=cost(8),
        compiler_params=params(),
        name="attend_forward",
    )(got, w_qkv, bias, w_o, b_o, gain, shift)


def feed_kernel(
    low_ref,
    hid_ref,
    win_ref,
    bin_ref,
    wout_ref,
    bout_ref,
    gain_ref,
    shift_ref,
    lab_ref,
    act_ref,
    slope_ref,
    enc_ref,
    norm_ref,
    rstd_ref,
    pooled_ref,
    copies_ref,
    total_ref,
):
    step = pl.program_id(0)
    up = dot(low_ref[...], win_ref[...]) + bin_ref[...]
    phi = 0.5 * (1.0 + lax.erf(up * (1.0 / math.sqrt(2.0))))
    density = jnp.exp(-0.5 * up * up) * (1.0 / math.sqrt(2.0 * math.pi))
    act = (up * phi).astype(BF16)
    act_ref[...] = act
    slope_ref[...] = (phi + up * density).astype(BF16)
    part = dot(act, wout_ref[...])

    @pl.when(step == 0)
    def _():
        total_ref[...] = part + (hid_ref[...] + bout_ref[...])

    @pl.when(step > 0)
    def _():
        total_ref[...] += part

    @pl.when(step == pl.num_programs(0) - 1)
    def _():
        tok_count, width = total_ref.shape
        kept_rows = tok_count // LANES
        for row in range(kept_rows):
            span = slice(row * LANES, (row + 1) * LANES)
            total = total_ref[span, :]
            centered = total - row_mean(total)
            rstd = lax.rsqrt(row_mean(centered * centered) + NORM_EPS)
            normed = centered * rstd
            out = normed * gain_ref[...] + shift_ref[...]
            norm_ref[span, :] = normed
            rstd_ref[span, :] = rstd
            enc_ref[span, :] = out.astype(BF16)
            segment = lax.broadcasted_iota(jnp.int32, (SEG_ROW, LANES), 0).astype(F32)
            onehot = (lab_ref[row : row + 1, :] == segment).astype(F32)
            count = jnp.sum(onehot, axis=1, keepdims=True)
            high, middle, low = split_three(out)
            mask = onehot.astype(BF16)
            summed = dot(mask, high) + dot(mask, middle) + dot(mask, low)
            pooled_ref[row * SEG_ROW : (row + 1) * SEG_ROW, :] = (summed / count).astype(BF16)
        for owner in range(copies_ref.shape[0]):
            copies_ref[owner] = pooled_ref[...]


def feed_forward(stack, hidden, w_in, b_in, w_out, b_out, gain, shift, labels, wide_count):
    _, tok_count, width = stack.shape
    units = w_in.shape[1]
    tile = 512
    kept_rows = tok_count // LANES
    whole = lambda step: (0, 0)
    shapes = (
        ((tok_count, units), BF16),
        ((tok_count, units), BF16),
        ((tok_count, width), BF16),
        ((tok_count, width), F32),
        ((tok_count, 1), F32),
        ((kept_rows * SEG_ROW, width), BF16),
        ((wide_count, kept_rows * SEG_ROW, width), BF16),
    )
    return pl.pallas_call(
        feed_kernel,
        out_shape=[jax.ShapeDtypeStruct(*item) for item in shapes],
        grid_spec=pltpu.PrefetchScalarGridSpec(
            num_scalar_prefetch=0,
            grid=(units // tile,),
            in_specs=[
                pl.BlockSpec((pl.Squeezed(), tok_count, width), lambda step: (2, 0, 0)),
                pl.BlockSpec((tok_count, width), whole),
                pl.BlockSpec((width, tile), lambda step: (0, step)),
                pl.BlockSpec((1, tile), lambda step: (0, step)),
                pl.BlockSpec((tile, width), lambda step: (step, 0)),
                pl.BlockSpec((1, width), whole),
                pl.BlockSpec((1, width), whole),
                pl.BlockSpec((1, width), whole),
                pl.BlockSpec((8, LANES), whole),
            ],
            out_specs=[
                pl.BlockSpec((tok_count, tile), lambda step: (0, step)),
                pl.BlockSpec((tok_count, tile), lambda step: (0, step)),
                pl.BlockSpec((tok_count, width), whole),
                pl.BlockSpec((tok_count, width), whole),
                pl.BlockSpec((tok_count, 1), whole),
                pl.BlockSpec((kept_rows * SEG_ROW, width), whole),
                pl.BlockSpec((wide_count, kept_rows * SEG_ROW, width), lambda step: (0, 0, 0)),
            ],
            scratch_shapes=[pltpu.VMEM((tok_count, width), F32)],
        ),
        cost_estimate=cost(10),
        compiler_params=params(1),
        name="feed_forward",
    )(stack, hidden, w_in, b_in, w_out, b_out, gain, shift, labels)


def route_kernel(me_ref, meta_ref, pair_ref, place_ref, targ_ref, first_ref, second_ref):
    wide_count = meta_ref.shape[0]
    me = me_ref[0]
    kept_rows = place_ref.shape[0] // SEG_ROW
    me_f = me.astype(F32)

    def table(row):
        return jnp.concatenate(
            [meta_ref[j, row : row + 1, :LANES].astype(F32) for j in range(wide_count)], axis=0
        )

    labels = table(0)
    dest = table(1)
    lane = lax.broadcasted_iota(jnp.int32, (wide_count, LANES), 1)
    slots = SEG_ROW * 2 * kept_rows
    dest = jnp.where(lane < slots, dest, -1.0)
    partner = table(2)
    target = table(3) + table(4) + table(5)
    sends = jnp.zeros((wide_count, LANES), F32)
    for owner in range(wide_count):
        to_owner = jnp.max((dest == float(owner)).astype(F32), axis=1, keepdims=True)
        sends = sends + jnp.where(lane == owner, to_owner, 0.0)
    row_id = lax.broadcasted_iota(jnp.int32, (wide_count, wide_count), 0)
    col_id = lax.broadcasted_iota(jnp.int32, (wide_count, wide_count), 1)
    below = (col_id < row_id).astype(BF16)
    earlier = dot(below, sends.astype(BF16))
    rank = jnp.zeros((wide_count, LANES), F32)
    for owner in range(wide_count):
        rank = rank + jnp.where(dest == float(owner), earlier[:, owner : owner + 1], 0.0)
    segment = (lane % SEG_ROW).astype(F32)
    per_owner = float(kept_rows * SEG_ROW)
    place = jnp.where(dest >= 0.0, dest * per_owner + rank * float(SEG_ROW) + segment, -1.0)
    live = (labels[:, 0:1] >= 0.0).astype(F32)
    my_rank = dot(below, jnp.broadcast_to(live, (wide_count, LANES)).astype(BF16))
    seg_lane = lax.broadcasted_iota(jnp.int32, (SEG_ROW, LANES), 1)
    seg_id = lax.broadcasted_iota(jnp.int32, (SEG_ROW, LANES), 0)
    for row in range(kept_rows):
        chosen = (live > 0.0) & (my_rank[:, 0:1] == float(row))
        pick = lambda values: column_sum(jnp.where(chosen, values, 0.0))
        own = (pick(dest) == me_f) & (seg_lane % SEG_ROW == seg_id)
        gather = lambda mask, values: jnp.sum(jnp.where(mask, values, 0.0), axis=1, keepdims=True)
        other = gather(own, pick(partner))
        at_other = seg_lane.astype(F32) == other
        out = slice(row * SEG_ROW, (row + 1) * SEG_ROW)
        place_ref[out, :] = gather(at_other, pick(place))
        targ_ref[out, :] = gather(own, pick(target))
    mine = lax.broadcasted_iota(jnp.int32, (wide_count, LANES), 0) == me
    my_place = column_sum(jnp.where(mine, place, 0.0))
    pair_lane = lax.broadcasted_iota(jnp.int32, (pair_ref.shape[0], LANES), 1)
    for column, out_ref in ((0, first_ref), (1, second_ref)):
        at_slot = pair_lane == pair_ref[:, column : column + 1]
        out_ref[...] = jnp.sum(jnp.where(at_slot, my_place, 0.0), axis=1, keepdims=True)


def route(me, meta, pair_index, kept_rows):
    wide_count = meta.shape[0]
    own = kept_rows * SEG_ROW
    pairs = pair_index.shape[0]
    shapes = (
        ((own, 1), F32),
        ((own, 1), F32),
        ((pairs, 1), F32),
        ((pairs, 1), F32),
    )
    return pl.pallas_call(
        route_kernel,
        out_shape=[jax.ShapeDtypeStruct(*item) for item in shapes],
        in_specs=[smem_spec(), vmem_spec(), vmem_spec()],
        out_specs=[vmem_spec()] * len(shapes),
        cost_estimate=cost(1),
        compiler_params=params(),
        name="route",
    )(me, meta, pair_index)


def pick_rows(place_ref, all_ref):
    lane = lax.broadcasted_iota(jnp.int32, (place_ref.shape[0], all_ref.shape[0]), 1)
    return dot((lane.astype(F32) == place_ref[...]).astype(BF16), all_ref[...])


def cosine_parts(left, right):
    inner = row_mean(left * right)
    left_inv = lax.rsqrt(row_mean(left * left) + COS_EPS)
    right_inv = lax.rsqrt(row_mean(right * right) + COS_EPS)
    return (inner, left_inv, right_inv)


def cosine_kernel(first_ref, second_ref, all_ref, sim_ref):
    left = pick_rows(first_ref, all_ref)
    right = pick_rows(second_ref, all_ref)
    inner, left_inv, right_inv = cosine_parts(left, right)
    sim = inner * left_inv * right_inv
    sim_ref[...] = jnp.where(first_ref[...] >= 0.0, sim, 0.0)


def cosine_pairs(first, second, pooled_all):
    return pl.pallas_call(
        cosine_kernel,
        out_shape=jax.ShapeDtypeStruct(first.shape, F32),
        in_specs=[vmem_spec()] * 3,
        out_specs=vmem_spec(),
        cost_estimate=cost(1),
        compiler_params=params(),
        name="cosine_pairs",
    )(first, second, pooled_all)


def norm_back(grad, normed, rstd, gain):
    scaled = grad * gain
    return rstd * (scaled - row_mean(scaled) - normed * row_mean(scaled * normed))


def loss_back_kernel(
    own_ref,
    all_ref,
    place_ref,
    targ_ref,
    lab_ref,
    labcol_ref,
    norm_ref,
    rstd_ref,
    gain_ref,
    dres_ref,
    dffn_ref,
    dffn_t_ref,
    sums_ref,
):
    tok_count, width = norm_ref.shape
    kept_rows = tok_count // LANES
    left = own_ref[...].astype(F32)
    right = pick_rows(place_ref, all_ref)
    inner, left_inv, right_inv = cosine_parts(left, right)
    error = 2.0 * (inner * left_inv * right_inv - targ_ref[...])
    factor = error * left_inv * right_inv * (1.0 / width)
    d_pooled = (factor * (right - left * (inner * left_inv * left_inv))).astype(BF16).astype(F32)
    gain_sum = jnp.zeros((1, width), F32)
    shift_sum = jnp.zeros((1, width), F32)
    bias_sum = jnp.zeros((1, width), F32)
    lane = lax.broadcasted_iota(jnp.int32, (LANES, LANES), 1).astype(F32)
    for row in range(kept_rows):
        span = slice(row * LANES, (row + 1) * LANES)
        segment = lax.broadcasted_iota(jnp.int32, (SEG_ROW, LANES), 0).astype(F32)
        count = jnp.sum(
            (lab_ref[row : row + 1, :] == segment).astype(F32), axis=1, keepdims=True
        )
        per_token = d_pooled[row * SEG_ROW : (row + 1) * SEG_ROW, :] / count
        shift_sum = shift_sum + column_sum(per_token * count)
        padded = jnp.concatenate([per_token, jnp.zeros((LANES - SEG_ROW, width), F32)], axis=0)
        onehot = (labcol_ref[span, :] == lane).astype(BF16)
        high, middle, low = split_three(padded)
        d_out = dot(onehot, high) + dot(onehot, middle) + dot(onehot, low)
        normed = norm_ref[span, :]
        d_res = norm_back(d_out, normed, rstd_ref[span, :], gain_ref[...])
        d_low = d_res.astype(BF16)
        dres_ref[span, :] = d_res
        dffn_ref[span, :] = d_low
        dffn_t_ref[:, span] = d_low.T
        gain_sum = gain_sum + column_sum(d_out * normed)
        bias_sum = bias_sum + column_sum(d_low.astype(F32))
    sums_ref[0:1, :] = gain_sum
    sums_ref[1:2, :] = shift_sum
    sums_ref[2:3, :] = bias_sum
    sums_ref[3:8, :] = jnp.zeros((5, width), F32)


def loss_back(own, pooled_all, place, target, labels, label_cols, normed, rstd, gain):
    tok_count, width = normed.shape
    shapes = (
        ((tok_count, width), F32),
        ((tok_count, width), BF16),
        ((width, tok_count), BF16),
        ((8, width), F32),
    )
    return pl.pallas_call(
        loss_back_kernel,
        out_shape=[jax.ShapeDtypeStruct(*item) for item in shapes],
        in_specs=[vmem_spec()] * 9,
        out_specs=[vmem_spec()] * len(shapes),
        cost_estimate=cost(3),
        compiler_params=params(),
        name="loss_back",
    )(own, pooled_all, place, target, labels, label_cols, normed, rstd, gain)


def feed_back_kernel(
    dffn_ref,
    dres_ref,
    wout_ref,
    win_ref,
    slope_ref,
    norm_ref,
    rstd_ref,
    gain_ref,
    wo_ref,
    dup_t_ref,
    bsum_ref,
    done_ref,
    dattn_t_ref,
    dctx_ref,
    sums_ref,
    total_ref,
):
    step = pl.program_id(0)
    d_up = (dot(dffn_ref[...], wout_ref[...], NT) * slope_ref[...].astype(F32)).astype(BF16)
    dup_t_ref[...] = d_up.T
    bsum_ref[...] = column_sum(d_up.astype(F32))
    part = dot(d_up, win_ref[...], NT)

    @pl.when(step == 0)
    def _():
        total_ref[...] = part + dres_ref[...]

    @pl.when(step > 0)
    def _():
        total_ref[...] += part

    @pl.when(step == pl.num_programs(0) - 1)
    def _():
        tok_count, width = total_ref.shape
        kept_rows = tok_count // LANES
        gain_sum = jnp.zeros((1, width), F32)
        shift_sum = jnp.zeros((1, width), F32)
        bias_sum = jnp.zeros((1, width), F32)
        for row in range(kept_rows):
            span = slice(row * LANES, (row + 1) * LANES)
            d_hidden = total_ref[span, :]
            normed = norm_ref[span, :]
            d_res = norm_back(d_hidden, normed, rstd_ref[span, :], gain_ref[...])
            d_low = d_res.astype(BF16)
            done_ref[span, :] = d_res
            dattn_t_ref[:, span] = d_low.T
            dctx_ref[span, :] = dot(d_low, wo_ref[...], NT).astype(BF16)
            gain_sum = gain_sum + column_sum(d_hidden * normed)
            shift_sum = shift_sum + column_sum(d_hidden)
            bias_sum = bias_sum + column_sum(d_low.astype(F32))
        sums_ref[0:1, :] = gain_sum
        sums_ref[1:2, :] = shift_sum
        sums_ref[2:3, :] = bias_sum
        sums_ref[3:8, :] = jnp.zeros((5, width), F32)


def feed_back(d_ffn, d_res, w_out, w_in, slope, normed, rstd, gain, w_o):
    tok_count, width = d_ffn.shape
    units = w_in.shape[1]
    tile = 512
    whole = lambda step: (0, 0)
    shapes = (
        ((units, tok_count), BF16),
        ((1, units), F32),
        ((tok_count, width), F32),
        ((width, tok_count), BF16),
        ((tok_count, width), BF16),
        ((8, width), F32),
    )
    return pl.pallas_call(
        feed_back_kernel,
        out_shape=[jax.ShapeDtypeStruct(*item) for item in shapes],
        grid_spec=pltpu.PrefetchScalarGridSpec(
            num_scalar_prefetch=0,
            grid=(units // tile,),
            in_specs=[
                pl.BlockSpec((tok_count, width), whole),
                pl.BlockSpec((tok_count, width), whole),
                pl.BlockSpec((tile, width), lambda step: (step, 0)),
                pl.BlockSpec((width, tile), lambda step: (0, step)),
                pl.BlockSpec((tok_count, tile), lambda step: (0, step)),
                pl.BlockSpec((tok_count, width), whole),
                pl.BlockSpec((tok_count, 1), whole),
                pl.BlockSpec((1, width), whole),
                pl.BlockSpec((width, width), whole),
            ],
            out_specs=[
                pl.BlockSpec((tile, tok_count), lambda step: (step, 0)),
                pl.BlockSpec((1, tile), lambda step: (0, step)),
                pl.BlockSpec((tok_count, width), whole),
                pl.BlockSpec((width, tok_count), whole),
                pl.BlockSpec((tok_count, width), whole),
                pl.BlockSpec((8, width), whole),
            ],
            scratch_shapes=[pltpu.VMEM((tok_count, width), F32)],
        ),
        cost_estimate=cost(10),
        compiler_params=params(1),
        name="feed_back",
    )(d_ffn, d_res, w_out, w_in, slope, normed, rstd, gain, w_o)


def attend_back_kernel(
    source_ref,
    proj_ref,
    probs_ref,
    dctx_ref,
    done_ref,
    wqkv_ref,
    dattn_t_ref,
    dmix_t_ref,
    dtok_ref,
    sums_ref,
    dproj_ref,
):
    row = pl.program_id(0)
    row_len, width = dctx_ref.shape
    blocks = dmix_t_ref.shape[0]
    main = 3 * width // blocks
    scale = 1.0 / math.sqrt(HEAD_DIM)
    lane = lax.broadcasted_iota(jnp.int32, (row_len, LANES), 1)
    left = (lane < HEAD_DIM).astype(BF16)
    right = (lane >= HEAD_DIM).astype(BF16)

    def twice(values):
        return jnp.concatenate([values * left, values * right], axis=0)

    for pair in range(width // LANES):
        col = pair * LANES
        queries = proj_ref[:, col : col + LANES]
        key_rows = proj_ref[:, width + col : width + col + LANES]
        values = proj_ref[:, 2 * width + col : 2 * width + col + LANES]
        probs = probs_ref[0, pair]
        d_ctx = twice(dctx_ref[:, col : col + LANES])
        d_probs = dot(d_ctx, values, NT)
        probs_f = probs.astype(F32)
        inner = jnp.sum(probs_f * d_probs, axis=-1, keepdims=True)
        d_scores = (probs_f * (d_probs - inner)).astype(BF16)
        wide_scores = jnp.concatenate([d_scores[:row_len], d_scores[row_len:]], axis=1)
        d_query = dot(wide_scores, twice(key_rows)) * scale
        d_key = dot(d_scores, twice(queries), TN) * scale
        d_value = dot(probs, d_ctx, TN)
        for part, grad in ((0, d_query), (1, d_key), (2, d_value)):
            low = grad.astype(BF16)
            place = part * width + col
            dproj_ref[:, place : place + LANES] = low
            turned = low.T
            start = place
            while start < place + LANES:
                block, offset = divmod(start, main)
                stop = min(place + LANES, (block + 1) * main)
                dmix_t_ref[block, offset : offset + stop - start, :] = turned[
                    start - place : stop - place, :
                ]
                start = stop
            summed = column_sum(low.astype(F32))

            @pl.when(row == 0)
            def _():
                sums_ref[:, place : place + LANES] = summed

            @pl.when(row > 0)
            def _():
                sums_ref[:, place : place + LANES] += summed

    rest = width // blocks
    for block in range(blocks):
        dmix_t_ref[block, main:, :] = dattn_t_ref[block * rest : (block + 1) * rest, :]
    grad = done_ref[...] + dot(dproj_ref[...], wqkv_ref[...], NT)
    dtok_ref[0] = grad.astype(BF16)


def attend_back(sources, proj, probs, d_ctx, d_one, w_qkv, d_attn_t, blocks, wide_count):
    tok_count, width = d_ctx.shape
    kept_rows = tok_count // LANES
    shapes = (
        ((blocks, 4 * width // blocks, tok_count), BF16),
        ((wide_count, LANES, width), BF16),
        ((1, 3 * width), F32),
    )
    return pl.pallas_call(
        attend_back_kernel,
        out_shape=[jax.ShapeDtypeStruct(*item) for item in shapes],
        grid_spec=pltpu.PrefetchScalarGridSpec(
            num_scalar_prefetch=1,
            grid=(kept_rows,),
            in_specs=[
                pl.BlockSpec((LANES, 3 * width), lambda row, src: (row, 0)),
                pl.BlockSpec((1,) + probs.shape[1:], lambda row, src: (row, 0, 0, 0)),
                pl.BlockSpec((LANES, width), lambda row, src: (row, 0)),
                pl.BlockSpec((LANES, width), lambda row, src: (row, 0)),
                pl.BlockSpec((width, 3 * width), lambda row, src: (0, 0)),
                pl.BlockSpec((width, LANES), lambda row, src: (0, row)),
            ],
            out_specs=[
                pl.BlockSpec((blocks, 4 * width // blocks, LANES), lambda row, src: (0, 0, row)),
                pl.BlockSpec((1, LANES, width), lambda row, src: (src[row], 0, 0)),
                pl.BlockSpec((1, 3 * width), lambda row, src: (0, 0)),
            ],
            scratch_shapes=[pltpu.VMEM((LANES, 3 * width), BF16)],
        ),
        cost_estimate=cost(20),
        compiler_params=params(1),
        name="attend_back",
    )(sources, proj, probs, d_ctx, d_one, w_qkv, d_attn_t)


def home_kernel(dest_ref, rows_ref, out_ref, sems):
    slot_dev = out_ref.shape[0]

    def copy(slot):
        return pltpu.make_async_copy(
            rows_ref.at[jnp.maximum(dest_ref[slot], 0)], out_ref.at[slot], sems.at[slot]
        )

    for slot in range(slot_dev):
        copy(slot).start()
    for slot in range(slot_dev):
        copy(slot).wait()

        @pl.when(dest_ref[slot] < 0)
        def _():
            out_ref[slot] = jnp.zeros(out_ref.shape[1:], out_ref.dtype)


def home_rows(destination, rows):
    count = destination.shape[0]
    return pl.pallas_call(
        home_kernel,
        out_shape=jax.ShapeDtypeStruct((count,) + rows.shape[1:], rows.dtype),
        in_specs=[smem_spec(), pl.BlockSpec(memory_space=pl.ANY)],
        out_specs=vmem_spec(),
        scratch_shapes=[pltpu.SemaphoreType.DMA((count,))],
        cost_estimate=cost(3),
        compiler_params=params(),
        name="home_rows",
    )(destination, rows)


def block_at(index, bit, value):
    low = index & ((1 << bit) - 1)
    return ((index >> bit) << (bit + 1)) | (value << bit) | low


def grad_kernel(first_bit, second_bit, spans, blocks, me_ref, own_ref, *refs):
    recv_refs, refs = refs[:blocks], refs[blocks:]
    step = pl.program_id(0)
    half_steps = pl.num_programs(0) // 2
    terms = len(spans)
    own_xs, recv_xs = refs[:terms], refs[terms : 2 * terms]
    outs = refs[2 * terms : 2 * terms + 4]
    own_lefts = refs[2 * terms + 4 : 3 * terms + 4]
    recv_lefts = refs[3 * terms + 4 :]
    me = me_ref[0]
    for half, bit in ((0, first_bit), (1, second_bit)):

        @pl.when(step == half * half_steps)
        def _():
            side = (me >> bit) & 1
            for block in range(blocks):
                low = block & ((1 << (bit - 1)) - 1)
                rest = ((block >> bit) << (bit - 1)) | low
                kept = ((block >> (bit - 1)) & 1) == side
                index = jnp.where(kept, rest, rest + blocks // 2)
                for (start, stop), own_left, recv_left in zip(spans, own_lefts, recv_lefts):
                    own_left[index] = own_ref[2 * block + (me & 1), start:stop, :]
                    recv_left[index] = recv_refs[block][start:stop, :]

    for term, (start, stop) in enumerate(spans):
        rows = stop - start
        chunk = blocks if blocks * rows <= 384 else blocks // 2
        for base in range(0, blocks, chunk):
            span = slice(base, base + chunk)
            flat = lambda left: left[span].reshape(chunk * rows, left.shape[2])
            part = dot(flat(own_lefts[term]), own_xs[term][...])
            part = part + dot(flat(recv_lefts[term]), recv_xs[term][...])
            part = part.astype(BF16).reshape(chunk, rows, part.shape[1])
            for index in range(chunk):
                block = base + index
                role, place = divmod(block, blocks // 2)
                for half in range(2):

                    @pl.when((step < half_steps) == (half == 0))
                    def _():
                        outs[2 * half + role][place, start:stop, :] = part[index]


def grad_terms(me, own, received, own_xs, recv_xs, spans, first_bit, second_bit, tile):
    blocks = len(received)
    rows, tok_count = received[0].shape
    columns = own_xs[0][0].shape[-1]
    steps = columns // tile
    half = steps // 2

    def x_spec(item):
        array, lead = item
        if lead is None:
            return pl.BlockSpec((tok_count, tile), lambda step: (0, step))
        return pl.BlockSpec((pl.Squeezed(), tok_count, tile), lambda step: (lead, 0, step))

    out_block = (blocks // 2, rows, tile)
    first_spec = pl.BlockSpec(out_block, lambda step: (0, 0, jnp.minimum(step, half - 1)))
    second_spec = pl.BlockSpec(out_block, lambda step: (0, 0, jnp.maximum(step - half, 0)))
    shape = jax.ShapeDtypeStruct((blocks // 2, rows, columns // 2), BF16)
    whole = lambda step: (0, 0, 0)
    lefts = [pltpu.VMEM((blocks, stop - start, tok_count), BF16) for start, stop in spans]
    return pl.pallas_call(
        functools.partial(grad_kernel, first_bit, second_bit, spans, blocks),
        out_shape=[shape] * 4,
        grid_spec=pltpu.PrefetchScalarGridSpec(
            num_scalar_prefetch=0,
            grid=(steps,),
            in_specs=[
                smem_spec(),
                pl.BlockSpec(own.shape, whole),
            ]
            + [pl.BlockSpec((rows, tok_count), lambda step: (0, 0))] * blocks
            + [x_spec(item) for item in own_xs + recv_xs],
            out_specs=[first_spec, first_spec, second_spec, second_spec],
            scratch_shapes=lefts + lefts,
        ),
        cost_estimate=cost(7),
        compiler_params=params(1),
        name="grad_terms",
    )(me, own, *received, *[item[0] for item in own_xs + recv_xs])


def fold_kernel(bits, places, me_ref, *refs):
    me = me_ref[0]
    for half in range(2):
        kept_ref, recv_ref = refs[2 * half], refs[2 * half + 1]
        keep_out, send_out = refs[4 + 2 * half], refs[5 + 2 * half]
        side = (me >> bits[half]) & 1
        for index in range(keep_out.shape[0]):
            for value, out_ref in ((1 - side, send_out), (side, keep_out)):
                block = block_at(index, places[half], value)
                out_ref[index] = add_low(kept_ref[block], recv_ref[block])


def fold(me, halves, bits, places):
    shapes = []
    for kept, _ in halves:
        shapes += [jax.ShapeDtypeStruct((kept.shape[0] // 2,) + kept.shape[1:], BF16)] * 2
    return pl.pallas_call(
        functools.partial(fold_kernel, bits, places),
        out_shape=shapes,
        in_specs=[smem_spec()] + [vmem_spec()] * 4,
        out_specs=[vmem_spec()] * 4,
        cost_estimate=cost(0.5),
        compiler_params=params(),
        name="fold",
    )(me, *halves[0], *halves[1])


def piece_kernel(turned, *refs):
    out_ref = refs[4]
    count = out_ref.shape[0]
    depth = out_ref.shape[1] if turned else out_ref.shape[2]
    for half in range(2):
        total = add_low(refs[2 * half][0], refs[2 * half + 1][0])
        if turned:
            total = total.T
        for index in range(count // 2):
            span = slice(index * depth, (index + 1) * depth)
            out_ref[half * (count // 2) + index] = total[span, :] if turned else total[:, span]


def narrow_pieces(halves, narrow_count, turned):
    _, rows, columns = halves[0][0].shape
    depth = 2 * columns // narrow_count
    shape = (narrow_count,) + ((depth, rows) if turned else (rows, depth))
    return pl.pallas_call(
        functools.partial(piece_kernel, turned),
        out_shape=jax.ShapeDtypeStruct(shape, BF16),
        in_specs=[vmem_spec()] * 4,
        out_specs=vmem_spec(),
        cost_estimate=cost(1),
        compiler_params=params(),
        name="narrow_pieces",
    )(*halves[0], *halves[1])


def swap(values, axis, bit):
    count = lax.axis_size(axis)
    return lax.ppermute(values, axis, [(i, i ^ (1 << bit)) for i in range(count)])


def pick(values, dim, index):
    return lax.dynamic_index_in_dim(values, index, dim, keepdims=False)


def add_low(kept, received):
    return (kept.astype(F32) + received.astype(F32)).astype(BF16)


def after(value, *others):
    return lax.optimization_barrier((value,) + others)[0]


def partner_half(turned, me):
    blocks, rows, tok_count = turned.shape
    pairs = turned.reshape(blocks // 2, 2, rows, tok_count)
    return [swap(pick(pairs[block], 0, 1 - (me & 1)), "wide", 0) for block in range(blocks // 2)]


class Folding:
    def __init__(self, me, outs, orders):
        self.me = me
        self.orders = orders
        self.left = [sorted(order) for order in orders]
        self.kept = [outs[0], outs[2]]
        self.sent = [outs[1], outs[3]]
        self.level = 0
        self.exchange()

    def exchange(self):
        self.received = [
            swap(self.sent[half], "wide", self.orders[half][self.level]) for half in range(2)
        ]
        for half in range(2):
            self.left[half].remove(self.orders[half][self.level])
        self.level += 1

    def halves(self):
        return [(self.kept[half], self.received[half]) for half in range(2)]

    def step(self):
        bits = [order[self.level] for order in self.orders]
        places = [left.index(bit) for left, bit in zip(self.left, bits)]
        outs = fold(self.me, self.halves(), bits, places)
        self.kept = [outs[0], outs[2]]
        self.sent = [outs[1], outs[3]]
        self.exchange()

    def finish(self, narrow_count, turned):
        while self.level < len(self.orders[0]):
            self.step()
        return narrow_pieces(self.halves(), narrow_count, turned)


def sum_pieces(pieces):
    received = lax.all_to_all(pieces, "narrow", split_axis=0, concat_axis=0, tiled=True)
    return jnp.sum(received.astype(F32), axis=0)


def sum_vectors(values):
    wide_bits = lax.axis_size("wide").bit_length() - 1
    narrow_bits = lax.axis_size("narrow").bit_length() - 1
    steps = [("wide", 0)]
    steps += [("narrow", bit) for bit in range(narrow_bits)]
    steps += [("wide", bit) for bit in range(1, wide_bits)]
    for axis, bit in steps:
        values = values + swap(values, axis, bit)
    return values


def on_device(
    tokens,
    segments,
    destination,
    pair_index,
    targets,
    w_qkv,
    b_qv,
    w_o,
    b_o,
    gain_one,
    shift_one,
    w_in,
    b_in,
    w_out,
    b_out,
    gain_two,
    shift_two,
):
    wide_count = lax.axis_size("wide")
    narrow_count = lax.axis_size("narrow")
    slot_dev, row_len, width = tokens.shape
    kept_rows = slot_dev // 2
    units = w_in.shape[1]
    me = lax.axis_index("wide")
    me_line = me.astype(jnp.int32).reshape(1)
    line = lambda vector: vector.reshape(1, -1)

    sent = build_send(tokens, segments, destination, pair_index, targets, wide_count)
    got = lax.all_to_all(sent, "wide", split_axis=0, concat_axis=0, tiled=True)
    full_bias = jnp.concatenate(
        [b_qv[:width], jnp.zeros((width,), F32), b_qv[width:]]
    ).reshape(1, 3 * width)
    stack, proj, probs, hidden, norm_one, rstd_one, labels, label_cols, meta, sources = (
        attend_forward(
            got, w_qkv, full_bias, w_o, line(b_o), line(gain_one), line(shift_one), kept_rows
        )
    )
    stack_recv = swap(stack, "wide", 0)
    act, slope, encoded, norm_two, rstd_two, pooled, pooled_copies = feed_forward(
        stack,
        hidden,
        w_in,
        line(b_in),
        w_out,
        line(b_out),
        line(gain_two),
        line(shift_two),
        labels,
        wide_count,
    )
    act_recv = swap(act, "wide", 0)
    place, target, first, second = route(me_line, meta, pair_index, kept_rows)
    pooled_all = lax.all_to_all(
        pooled_copies, "wide", split_axis=0, concat_axis=0, tiled=True
    ).reshape(wide_count * kept_rows * SEG_ROW, width)
    similarity = cosine_pairs(first, second, pooled_all).reshape(-1)
    d_res_two, d_ffn, d_ffn_t, sums_two = loss_back(
        pooled, pooled_all, place, target, labels, label_cols, norm_two, rstd_two, line(gain_two)
    )

    bits = wide_count.bit_length() - 1
    middle = 1 + (bits - 1) // 2
    low_first = list(range(1, bits))
    high_first = list(range(middle, bits)) + list(range(1, middle))
    orders = (low_first, high_first)
    first_bits = (low_first[0], high_first[0])
    tok_count = kept_rows * row_len
    blocks = lambda turned: turned.reshape(wide_count, -1, tok_count)

    turned_out = blocks(d_ffn_t)
    rows_out = turned_out.shape[1]
    fold_out = Folding(
        me_line,
        grad_terms(
            me_line,
            turned_out,
            partner_half(turned_out, me),
            [(act, None)],
            [(act_recv, None)],
            ((0, rows_out),),
            *first_bits,
            512,
        ),
        orders,
    )
    d_up_t, sum_b_in, d_one, d_attn_t, d_ctx, sums_one = feed_back(
        after(d_ffn, *fold_out.sent),
        d_res_two,
        w_out,
        w_in,
        slope,
        norm_one,
        rstd_one,
        line(gain_one),
        w_o,
    )
    turned_in = blocks(d_up_t)
    rows_in = turned_in.shape[1]
    recv_in = partner_half(turned_in, me)
    fold_out.step()
    fold_in = Folding(
        me_line,
        grad_terms(
            me_line,
            turned_in,
            after(tuple(recv_in), *fold_out.sent),
            [(stack, 2)],
            [(stack_recv, 2)],
            ((0, rows_in),),
            *first_bits,
            width // 2,
        ),
        orders,
    )
    turned_mix, d_rows, sums_qkv = attend_back(
        sources,
        proj,
        probs,
        after(d_ctx, *fold_in.sent),
        d_one,
        w_qkv,
        d_attn_t,
        wide_count,
        wide_count,
    )
    recv_mix = partner_half(turned_mix, me)
    fold_in.step()
    pieces_out = fold_out.finish(narrow_count, False)
    cols_qkv = 3 * width // wide_count
    rows_mix = turned_mix.shape[1]
    fold_mix = Folding(
        me_line,
        grad_terms(
            me_line,
            turned_mix,
            after(tuple(recv_mix), pieces_out, *fold_in.sent),
            [(stack, 0), (stack, 1)],
            [(stack_recv, 0), (stack_recv, 1)],
            ((0, cols_qkv), (cols_qkv, rows_mix)),
            *first_bits,
            width // 2,
        ),
        orders,
    )
    grad_w_out = sum_pieces(pieces_out).T
    pieces_in = fold_in.finish(narrow_count, True)
    grad_w_in = sum_pieces(after(pieces_in, *fold_mix.sent))
    fold_mix.step()
    home = lax.all_to_all(
        after(d_rows, *fold_mix.sent), "wide", split_axis=0, concat_axis=0, tiled=True
    )
    grad_tokens = home_rows(destination, home)
    grad_mix = sum_pieces(fold_mix.finish(narrow_count, True))
    grad_w_qkv = grad_mix[:, :cols_qkv]
    grad_w_o = grad_mix[:, cols_qkv:]

    vectors = jnp.concatenate(
        [
            sums_qkv[0, :width],
            sums_qkv[0, 2 * width :],
            sums_one[2],
            sums_one[0],
            sums_one[1],
            sum_b_in[0],
            sums_two[2],
            sums_two[0],
            sums_two[1],
        ]
    )
    vectors = sum_vectors(vectors.reshape(-1, LANES)).reshape(-1)
    cuts = (2 * width, width, width, width, units, width, width, width)
    outs = []
    start = 0
    for size in cuts:
        outs.append(vectors[start : start + size])
        start += size
    grad_b_qv, grad_b_o, grad_gain_one, grad_shift_one = outs[:4]
    grad_b_in, grad_b_out, grad_gain_two, grad_shift_two = outs[4:]
    return (
        encoded.reshape(kept_rows, row_len, width),
        similarity,
        grad_tokens,
        grad_w_qkv,
        grad_b_qv,
        grad_w_o,
        grad_b_o,
        grad_gain_one,
        grad_shift_one,
        grad_w_in,
        grad_b_in,
        grad_w_out,
        grad_b_out,
        grad_gain_two,
        grad_shift_two,
    )


def solution(mesh):
    rows = ("wide", "narrow")
    in_specs = (P(rows, None, None), P(rows, None), P(rows), P(rows, None), P(rows)) + (P(),) * 12
    matrix = P("narrow", "wide")
    out_specs = (
        P(rows, None, None),
        P(rows),
        P(rows, None, None),
        matrix,
        P(),
        matrix,
        P(),
        P(),
        P(),
        matrix,
        P(),
        matrix,
        P(),
        P(),
        P(),
    )
    return jax.shard_map(
        on_device, mesh=mesh, in_specs=in_specs, out_specs=out_specs, check_vma=False
    )
```

```python
import functools
import math

import jax
import jax.numpy as jnp
from jax import lax
from jax.experimental import pallas as pl
from jax.experimental.pallas import tpu as pltpu
from jax.sharding import PartitionSpec as P

HEAD_DIM = 64
SEG_ROW = 8
LANES = 128
META_ROWS = 16
NEG_FILL = -1e30
NORM_EPS = 1e-12
COS_EPS = 1e-06
F32 = jnp.float32
BF16 = jnp.bfloat16
VMEM_LIMIT = 67043328


def cost(micros):
    return pl.CostEstimate(flops=0, bytes_accessed=int(micros * 3.0e6), transcendentals=0)


NT = (((1,), (1,)), ((), ()))
TN = (((0,), (0,)), ((), ()))


def vmem_spec():
    return pl.BlockSpec(memory_space=pltpu.VMEM)


def hbm_shape(shape, dtype):
    return pltpu.HBM(shape, dtype)


def make_shape(shape, dtype, make=jax.ShapeDtypeStruct):
    return make(shape, dtype)


def params(steps=0):
    return pltpu.CompilerParams(
        dimension_semantics=("arbitrary",) * steps if steps else None,
        vmem_limit_bytes=VMEM_LIMIT,
    )


def split_three(values):
    high = values.astype(BF16)
    rest = values - high.astype(F32)
    middle = rest.astype(BF16)
    low = (rest - middle.astype(F32)).astype(BF16)
    return (high, middle, low)


def dot(left, right, dims=None):
    if dims is None:
        return jnp.dot(left, right, preferred_element_type=F32)
    return lax.dot_general(left, right, dims, preferred_element_type=F32)


def column_sum(values):
    return jnp.sum(values, axis=0, keepdims=True)


def row_mean(values):
    return jnp.mean(values, axis=-1, keepdims=True)


def prep_kernel(dest_ref, pair_ref, targ_ref, tok_ref, seg_ref, out_ref, sems):
    slot_dev = dest_ref.shape[0]
    wide_count, _, width = out_ref.shape
    row_len = tok_ref.shape[1]
    sources = []
    lives = []
    copies = []
    for owner in range(wide_count):
        found = jnp.int32(0)
        live = dest_ref[0] == owner
        for slot in range(1, slot_dev):
            match = dest_ref[slot] == owner
            found = jnp.where(match, slot, found)
            live = live | match
        sources.append(found)
        lives.append(live)
        copy = pltpu.make_async_copy(
            tok_ref.at[found], out_ref.at[owner, pl.ds(0, row_len), :], sems.at[owner]
        )
        copy.start()
        copies.append(copy)
    lane = lax.broadcasted_iota(jnp.int32, (1, LANES), 1)
    dest = jnp.full((1, LANES), -1, jnp.int32)
    for slot in range(slot_dev):
        dest = jnp.where(lane // SEG_ROW == slot, dest_ref[slot], dest)
    partner = jnp.zeros((1, LANES), jnp.int32)
    target = jnp.zeros((1, LANES), F32)
    for pair in range(pair_ref.shape[1]):
        first = pair_ref[0, pair]
        second = pair_ref[1, pair]
        at_first = lane == first
        at_second = lane == second
        partner = jnp.where(at_first, second, jnp.where(at_second, first, partner))
        target = jnp.where(at_first | at_second, targ_ref[0, pair], target)
    high, middle, low = split_three(target)
    fixed = [dest.astype(F32), partner.astype(F32)]
    fixed += [high.astype(F32), middle.astype(F32), low.astype(F32)]
    fixed.append(jnp.zeros((META_ROWS - 1 - len(fixed), LANES), F32))
    for owner in range(wide_count):
        labels = seg_ref[pl.ds(sources[owner], 1), :].astype(F32)
        labels = jnp.where(lives[owner], labels, -1.0)
        table = jnp.concatenate([labels] + fixed, axis=0)
        out_ref[owner, row_len:, :LANES] = table.astype(BF16)
        out_ref[owner, row_len:, LANES:] = jnp.zeros((META_ROWS, width - LANES), BF16)
    for copy in copies:
        copy.wait()


def smem_spec():
    return pl.BlockSpec(memory_space=pltpu.SMEM)


def build_send(tokens, segments, destination, pair_index, targets, wide_count):
    slot_dev, row_len, width = tokens.shape
    return pl.pallas_call(
        prep_kernel,
        out_shape=jax.ShapeDtypeStruct((wide_count, row_len + META_ROWS, width), BF16),
        in_specs=[smem_spec()] * 3 + [pl.BlockSpec(memory_space=pl.ANY), vmem_spec()],
        out_specs=vmem_spec(),
        scratch_shapes=[pltpu.SemaphoreType.DMA((wide_count,))],
        cost_estimate=cost(3),
        compiler_params=params(),
        name="build_send",
    )(destination, pair_index.T, targets.reshape(1, -1), tokens, segments)


def attend_kernel(
    got_ref,
    wqkv_ref,
    bias_ref,
    wo_ref,
    bo_ref,
    gain_ref,
    shift_ref,
    stack_ref,
    proj_ref,
    probs_ref,
    hid_ref,
    norm_ref,
    rstd_ref,
    lab_ref,
    labcol_ref,
    meta_ref,
    source_ref,
):
    x_ref, ctx_ref, low_ref = stack_ref.at[0], stack_ref.at[1], stack_ref.at[2]
    wide_count = got_ref.shape[0]
    tok_count, width = hid_ref.shape
    row_len = got_ref.shape[1] - META_ROWS
    kept_rows = tok_count // row_len
    seen = jnp.int32(0)
    sources = [jnp.int32(0)] * kept_rows
    for slot in range(wide_count):
        top = jnp.max(got_ref[slot, row_len : row_len + 1, :LANES].astype(F32))
        live = top >= 0.0
        for row in range(kept_rows):
            sources[row] = jnp.where(live & (seen == row), slot, sources[row])
        seen = seen + live.astype(jnp.int32)
    meta_ref[...] = got_ref[:, row_len:, :LANES]
    for row in range(kept_rows):
        source_ref[row] = sources[row]
        span = pl.ds(row * row_len, row_len)
        x_ref[span, :] = got_ref[sources[row], :row_len, :]
        tag = got_ref[sources[row], row_len : row_len + 1, :LANES].astype(F32)
        lab_ref[row : row + 1, :] = tag
        labcol_ref[span, :] = jnp.broadcast_to(tag, (LANES, LANES)).T
    total_cols = proj_ref.shape[1]
    tile = 256
    for start in range(0, total_cols, tile):
        cols = slice(start, start + tile)
        proj_ref[:, cols] = (dot(x_ref[...], wqkv_ref[:, cols]) + bias_ref[:, cols]).astype(BF16)

    scale = 1.0 / math.sqrt(HEAD_DIM)
    lane = lax.broadcasted_iota(jnp.int32, (row_len, LANES), 1)
    left = (lane < HEAD_DIM).astype(BF16)
    right = (lane >= HEAD_DIM).astype(BF16)

    def attend_row(row, carry):
        span = pl.ds(pl.multiple_of(row * row_len, row_len), row_len)
        same = labcol_ref[span, :] == lab_ref[pl.ds(row, 1), :]
        same = jnp.concatenate([same, same], axis=0)
        for pair in range(width // LANES):
            col = pair * LANES
            queries = proj_ref[span, col : col + LANES]
            key_rows = proj_ref[span, width + col : width + col + LANES]
            values = proj_ref[span, 2 * width + col : 2 * width + col + LANES]
            both = jnp.concatenate([queries * left, queries * right], axis=0)
            scores = jnp.where(same, dot(both, key_rows, NT) * scale, NEG_FILL)
            top = jnp.max(scores, axis=-1, keepdims=True)
            expo = jnp.exp(scores - top)
            total = jnp.sum(expo, axis=-1, keepdims=True)
            probs = (expo / total).astype(BF16)
            probs_ref[row, pair] = probs
            wide_probs = jnp.concatenate([probs[:row_len], probs[row_len:]], axis=1)
            split_values = jnp.concatenate([values * left, values * right], axis=0)
            ctx_ref[span, col : col + LANES] = dot(wide_probs, split_values).astype(BF16)
        return carry

    lax.fori_loop(0, kept_rows, attend_row, 0)
    for row in range(kept_rows):
        span = pl.ds(row * row_len, row_len)
        total = x_ref[span, :].astype(F32) + dot(ctx_ref[span, :], wo_ref[...]) + bo_ref[...]
        centered = total - row_mean(total)
        rstd = lax.rsqrt(row_mean(centered * centered) + NORM_EPS)
        normed = centered * rstd
        hidden = normed * gain_ref[...] + shift_ref[...]
        norm_ref[span, :] = normed
        rstd_ref[span, :] = rstd
        hid_ref[span, :] = hidden
        low_ref[span, :] = hidden.astype(BF16)


def attend_forward(got, w_qkv, bias, w_o, b_o, gain, shift, kept_rows):
    wide_count, slot_len, width = got.shape
    row_len = slot_len - META_ROWS
    tok_count = kept_rows * row_len
    shapes = (
        ((3, tok_count, width), BF16),
        ((tok_count, 3 * width), BF16),
        ((kept_rows, width // LANES, 2 * row_len, row_len), BF16),
        ((tok_count, width), F32),
        ((tok_count, width), F32),
        ((tok_count, 1), F32),
        ((8, LANES), F32),
        ((tok_count, LANES), F32),
        ((wide_count, META_ROWS, LANES), BF16),
        ((kept_rows,), jnp.int32),
    )
    return pl.pallas_call(
        attend_kernel,
        out_shape=[make_shape(*item) for item in shapes],
        in_specs=[vmem_spec()] * 7,
        out_specs=[vmem_spec()] * (len(shapes) - 1) + [smem_spec()],
        cost_estimate=cost(8),
        compiler_params=params(),
        name="attend_forward",
    )(got, w_qkv, bias, w_o, b_o, gain, shift)


def feed_kernel(
    low_ref,
    hid_ref,
    win_ref,
    bin_ref,
    wout_ref,
    bout_ref,
    gain_ref,
    shift_ref,
    lab_ref,
    act_ref,
    slope_ref,
    enc_ref,
    norm_ref,
    rstd_ref,
    pooled_ref,
    copies_ref,
    total_ref,
):
    step = pl.program_id(0)
    up = dot(low_ref[...], win_ref[...]) + bin_ref[...]
    phi = 0.5 * (1.0 + lax.erf(up * (1.0 / math.sqrt(2.0))))
    density = jnp.exp(-0.5 * up * up) * (1.0 / math.sqrt(2.0 * math.pi))
    act = (up * phi).astype(BF16)
    act_ref[...] = act
    slope_ref[...] = (phi + up * density).astype(BF16)
    part = dot(act, wout_ref[...])

    @pl.when(step == 0)
    def _():
        total_ref[...] = part + (hid_ref[...] + bout_ref[...])

    @pl.when(step > 0)
    def _():
        total_ref[...] += part

    @pl.when(step == pl.num_programs(0) - 1)
    def _():
        tok_count, width = total_ref.shape
        kept_rows = tok_count // LANES
        for row in range(kept_rows):
            span = slice(row * LANES, (row + 1) * LANES)
            total = total_ref[span, :]
            centered = total - row_mean(total)
            rstd = lax.rsqrt(row_mean(centered * centered) + NORM_EPS)
            normed = centered * rstd
            out = normed * gain_ref[...] + shift_ref[...]
            norm_ref[span, :] = normed
            rstd_ref[span, :] = rstd
            enc_ref[span, :] = out.astype(BF16)
            segment = lax.broadcasted_iota(jnp.int32, (SEG_ROW, LANES), 0).astype(F32)
            onehot = (lab_ref[row : row + 1, :] == segment).astype(F32)
            count = jnp.sum(onehot, axis=1, keepdims=True)
            high, middle, low = split_three(out)
            mask = onehot.astype(BF16)
            summed = dot(mask, high) + dot(mask, middle) + dot(mask, low)
            pooled_ref[row * SEG_ROW : (row + 1) * SEG_ROW, :] = (summed / count).astype(BF16)
        for owner in range(copies_ref.shape[0]):
            copies_ref[owner] = pooled_ref[...]


def feed_forward(stack, hidden, w_in, b_in, w_out, b_out, gain, shift, labels, wide_count):
    _, tok_count, width = stack.shape
    units = w_in.shape[1]
    tile = 512
    kept_rows = tok_count // LANES
    whole = lambda step: (0, 0)
    shapes = (
        ((tok_count, units), BF16),
        ((tok_count, units), BF16),
        ((tok_count, width), BF16),
        ((tok_count, width), F32),
        ((tok_count, 1), F32),
        ((kept_rows * SEG_ROW, width), BF16),
        ((wide_count, kept_rows * SEG_ROW, width), BF16),
    )
    return pl.pallas_call(
        feed_kernel,
        out_shape=[make_shape(*item) for item in shapes],
        grid_spec=pltpu.PrefetchScalarGridSpec(
            num_scalar_prefetch=0,
            grid=(units // tile,),
            in_specs=[
                pl.BlockSpec((pl.Squeezed(), tok_count, width), lambda step: (2, 0, 0)),
                pl.BlockSpec((tok_count, width), whole),
                pl.BlockSpec((width, tile), lambda step: (0, step)),
                pl.BlockSpec((1, tile), lambda step: (0, step)),
                pl.BlockSpec((tile, width), lambda step: (step, 0)),
                pl.BlockSpec((1, width), whole),
                pl.BlockSpec((1, width), whole),
                pl.BlockSpec((1, width), whole),
                pl.BlockSpec((8, LANES), whole),
            ],
            out_specs=[
                pl.BlockSpec((tok_count, tile), lambda step: (0, step)),
                pl.BlockSpec((tok_count, tile), lambda step: (0, step)),
                pl.BlockSpec((tok_count, width), whole),
                pl.BlockSpec((tok_count, width), whole),
                pl.BlockSpec((tok_count, 1), whole),
                pl.BlockSpec((kept_rows * SEG_ROW, width), whole),
                pl.BlockSpec((wide_count, kept_rows * SEG_ROW, width), lambda step: (0, 0, 0)),
            ],
            scratch_shapes=[pltpu.VMEM((tok_count, width), F32)],
        ),
        cost_estimate=cost(10),
        compiler_params=params(1),
        name="feed_forward",
    )(stack, hidden, w_in, b_in, w_out, b_out, gain, shift, labels)


def route_kernel(me_ref, meta_ref, pair_ref, place_ref, targ_ref, first_ref, second_ref):
    wide_count = meta_ref.shape[0]
    me = me_ref[0]
    kept_rows = place_ref.shape[0] // SEG_ROW
    me_f = me.astype(F32)

    def table(row):
        return jnp.concatenate(
            [meta_ref[j, row : row + 1, :LANES].astype(F32) for j in range(wide_count)], axis=0
        )

    labels = table(0)
    dest = table(1)
    lane = lax.broadcasted_iota(jnp.int32, (wide_count, LANES), 1)
    slots = SEG_ROW * 2 * kept_rows
    dest = jnp.where(lane < slots, dest, -1.0)
    partner = table(2)
    target = table(3) + table(4) + table(5)
    sends = jnp.zeros((wide_count, LANES), F32)
    for owner in range(wide_count):
        to_owner = jnp.max((dest == float(owner)).astype(F32), axis=1, keepdims=True)
        sends = sends + jnp.where(lane == owner, to_owner, 0.0)
    row_id = lax.broadcasted_iota(jnp.int32, (wide_count, wide_count), 0)
    col_id = lax.broadcasted_iota(jnp.int32, (wide_count, wide_count), 1)
    below = (col_id < row_id).astype(BF16)
    earlier = dot(below, sends.astype(BF16))
    rank = jnp.zeros((wide_count, LANES), F32)
    for owner in range(wide_count):
        rank = rank + jnp.where(dest == float(owner), earlier[:, owner : owner + 1], 0.0)
    segment = (lane % SEG_ROW).astype(F32)
    per_owner = float(kept_rows * SEG_ROW)
    place = jnp.where(dest >= 0.0, dest * per_owner + rank * float(SEG_ROW) + segment, -1.0)
    live = (labels[:, 0:1] >= 0.0).astype(F32)
    my_rank = dot(below, jnp.broadcast_to(live, (wide_count, LANES)).astype(BF16))
    seg_lane = lax.broadcasted_iota(jnp.int32, (SEG_ROW, LANES), 1)
    seg_id = lax.broadcasted_iota(jnp.int32, (SEG_ROW, LANES), 0)
    for row in range(kept_rows):
        chosen = (live > 0.0) & (my_rank[:, 0:1] == float(row))
        pick = lambda values: column_sum(jnp.where(chosen, values, 0.0))
        own = (pick(dest) == me_f) & (seg_lane % SEG_ROW == seg_id)
        gather = lambda mask, values: jnp.sum(jnp.where(mask, values, 0.0), axis=1, keepdims=True)
        other = gather(own, pick(partner))
        at_other = seg_lane.astype(F32) == other
        out = slice(row * SEG_ROW, (row + 1) * SEG_ROW)
        place_ref[out, :] = gather(at_other, pick(place))
        targ_ref[out, :] = gather(own, pick(target))
    mine = lax.broadcasted_iota(jnp.int32, (wide_count, LANES), 0) == me
    my_place = column_sum(jnp.where(mine, place, 0.0))
    pair_lane = lax.broadcasted_iota(jnp.int32, (pair_ref.shape[0], LANES), 1)
    for column, out_ref in ((0, first_ref), (1, second_ref)):
        at_slot = pair_lane == pair_ref[:, column : column + 1]
        out_ref[...] = jnp.sum(jnp.where(at_slot, my_place, 0.0), axis=1, keepdims=True)


def route(me, meta, pair_index, kept_rows):
    wide_count = meta.shape[0]
    own = kept_rows * SEG_ROW
    pairs = pair_index.shape[0]
    shapes = (
        ((own, 1), F32),
        ((own, 1), F32),
        ((pairs, 1), F32),
        ((pairs, 1), F32),
    )
    return pl.pallas_call(
        route_kernel,
        out_shape=[make_shape(*item) for item in shapes],
        in_specs=[smem_spec(), vmem_spec(), vmem_spec()],
        out_specs=[vmem_spec()] * len(shapes),
        cost_estimate=cost(1),
        compiler_params=params(),
        name="route",
    )(me, meta, pair_index)


def pick_rows(place_ref, all_ref):
    lane = lax.broadcasted_iota(jnp.int32, (place_ref.shape[0], all_ref.shape[0]), 1)
    return dot((lane.astype(F32) == place_ref[...]).astype(BF16), all_ref[...])


def cosine_parts(left, right):
    inner = row_mean(left * right)
    left_inv = lax.rsqrt(row_mean(left * left) + COS_EPS)
    right_inv = lax.rsqrt(row_mean(right * right) + COS_EPS)
    return (inner, left_inv, right_inv)


def cosine_kernel(first_ref, second_ref, all_ref, sim_ref):
    left = pick_rows(first_ref, all_ref)
    right = pick_rows(second_ref, all_ref)
    inner, left_inv, right_inv = cosine_parts(left, right)
    sim = inner * left_inv * right_inv
    sim_ref[...] = jnp.where(first_ref[...] >= 0.0, sim, 0.0)


def cosine_pairs(first, second, pooled_all):
    return pl.pallas_call(
        cosine_kernel,
        out_shape=jax.ShapeDtypeStruct(first.shape, F32),
        in_specs=[vmem_spec()] * 3,
        out_specs=vmem_spec(),
        cost_estimate=cost(1),
        compiler_params=params(),
        name="cosine_pairs",
    )(first, second, pooled_all)


def part_blocks(parity, held, own_ref, send_refs, first=0):
    for index in range(held.shape[0] // 2):
        own_ref[index] = held[2 * index + parity]
        send_refs[first + index][...] = held[2 * index + 1 - parity]


def norm_back(grad, normed, rstd, gain):
    scaled = grad * gain
    return rstd * (scaled - row_mean(scaled) - normed * row_mean(scaled * normed))


def loss_back_kernel(
    me_ref,
    own_ref,
    all_ref,
    place_ref,
    targ_ref,
    lab_ref,
    labcol_ref,
    norm_ref,
    rstd_ref,
    gain_ref,
    dres_ref,
    dffn_ref,
    sums_ref,
    kept_ref,
    *refs,
):
    send_refs, held = refs[:-1], refs[-1]
    depth = held.shape[1]
    tok_count, width = norm_ref.shape
    kept_rows = tok_count // LANES
    left = own_ref[...].astype(F32)
    right = pick_rows(place_ref, all_ref)
    inner, left_inv, right_inv = cosine_parts(left, right)
    error = 2.0 * (inner * left_inv * right_inv - targ_ref[...])
    factor = error * left_inv * right_inv * (1.0 / width)
    d_pooled = (factor * (right - left * (inner * left_inv * left_inv))).astype(BF16).astype(F32)
    gain_sum = jnp.zeros((1, width), F32)
    shift_sum = jnp.zeros((1, width), F32)
    bias_sum = jnp.zeros((1, width), F32)
    lane = lax.broadcasted_iota(jnp.int32, (LANES, LANES), 1).astype(F32)
    for row in range(kept_rows):
        span = slice(row * LANES, (row + 1) * LANES)
        segment = lax.broadcasted_iota(jnp.int32, (SEG_ROW, LANES), 0).astype(F32)
        count = jnp.sum(
            (lab_ref[row : row + 1, :] == segment).astype(F32), axis=1, keepdims=True
        )
        per_token = d_pooled[row * SEG_ROW : (row + 1) * SEG_ROW, :] / count
        shift_sum = shift_sum + column_sum(per_token * count)
        padded = jnp.concatenate([per_token, jnp.zeros((LANES - SEG_ROW, width), F32)], axis=0)
        onehot = (labcol_ref[span, :] == lane).astype(BF16)
        high, middle, low = split_three(padded)
        d_out = dot(onehot, high) + dot(onehot, middle) + dot(onehot, low)
        normed = norm_ref[span, :]
        d_res = norm_back(d_out, normed, rstd_ref[span, :], gain_ref[...])
        d_low = d_res.astype(BF16)
        dres_ref[span, :] = d_res
        dffn_ref[span, :] = d_low
        turned = d_low.T
        for block in range(held.shape[0]):
            held[block, :, span] = turned[block * depth : (block + 1) * depth, :]
        gain_sum = gain_sum + column_sum(d_out * normed)
        bias_sum = bias_sum + column_sum(d_low.astype(F32))
    sums_ref[0:1, :] = gain_sum
    sums_ref[1:2, :] = shift_sum
    sums_ref[2:3, :] = bias_sum
    sums_ref[3:8, :] = jnp.zeros((5, width), F32)
    part_blocks(me_ref[0] & 1, held, kept_ref, send_refs)


def loss_back(
    me, own, pooled_all, place, target, labels, label_cols, normed, rstd, gain, wide_count
):
    tok_count, width = normed.shape
    half = wide_count // 2
    depth = width // wide_count
    shapes = (
        ((tok_count, width), F32),
        ((tok_count, width), BF16),
        ((8, width), F32),
        ((half, depth, tok_count), BF16),
    ) + (((depth, tok_count), BF16, hbm_shape),) * half
    return pl.pallas_call(
        loss_back_kernel,
        out_shape=[make_shape(*item) for item in shapes],
        in_specs=[smem_spec()] + [vmem_spec()] * 9,
        out_specs=[vmem_spec()] * len(shapes),
        scratch_shapes=[pltpu.VMEM((wide_count, depth, tok_count), BF16)],
        cost_estimate=cost(3),
        compiler_params=params(),
        name="loss_back",
    )(me, own, pooled_all, place, target, labels, label_cols, normed, rstd, gain)


def feed_back_kernel(
    me_ref,
    dffn_ref,
    dres_ref,
    wout_ref,
    win_ref,
    slope_ref,
    norm_ref,
    rstd_ref,
    gain_ref,
    wo_ref,
    bsum_ref,
    done_ref,
    dattn_t_ref,
    dctx_ref,
    sums_ref,
    kept_ref,
    *refs,
):
    send_refs, held, total_ref = refs[:-2], refs[-2], refs[-1]
    count, depth, _ = held.shape
    step = pl.program_id(0)
    d_up = (dot(dffn_ref[...], wout_ref[...], NT) * slope_ref[...].astype(F32)).astype(BF16)
    turned = d_up.T
    for block in range(count):
        held[block] = turned[block * depth : (block + 1) * depth, :]
    for at in range(len(send_refs) // (count // 2)):

        @pl.when(step == at)
        def _():
            part_blocks(me_ref[0] & 1, held, kept_ref, send_refs, at * (count // 2))

    bsum_ref[...] = column_sum(d_up.astype(F32))
    part = dot(d_up, win_ref[...], NT)

    @pl.when(step == 0)
    def _():
        total_ref[...] = part + dres_ref[...]

    @pl.when(step > 0)
    def _():
        total_ref[...] += part

    @pl.when(step == pl.num_programs(0) - 1)
    def _():
        tok_count, width = total_ref.shape
        kept_rows = tok_count // LANES
        gain_sum = jnp.zeros((1, width), F32)
        shift_sum = jnp.zeros((1, width), F32)
        bias_sum = jnp.zeros((1, width), F32)
        for row in range(kept_rows):
            span = slice(row * LANES, (row + 1) * LANES)
            d_hidden = total_ref[span, :]
            normed = norm_ref[span, :]
            d_res = norm_back(d_hidden, normed, rstd_ref[span, :], gain_ref[...])
            d_low = d_res.astype(BF16)
            done_ref[span, :] = d_res
            dattn_t_ref[:, span] = d_low.T
            dctx_ref[span, :] = dot(d_low, wo_ref[...], NT).astype(BF16)
            gain_sum = gain_sum + column_sum(d_hidden * normed)
            shift_sum = shift_sum + column_sum(d_hidden)
            bias_sum = bias_sum + column_sum(d_low.astype(F32))
        sums_ref[0:1, :] = gain_sum
        sums_ref[1:2, :] = shift_sum
        sums_ref[2:3, :] = bias_sum
        sums_ref[3:8, :] = jnp.zeros((5, width), F32)


def feed_back(me, d_ffn, d_res, w_out, w_in, slope, normed, rstd, gain, w_o, wide_count):
    tok_count, width = d_ffn.shape
    units = w_in.shape[1]
    tile = 768
    depth = units // wide_count
    half = wide_count // 2
    count = tile // depth
    whole = lambda step: (0, 0)
    shapes = (
        ((1, units), F32),
        ((tok_count, width), F32),
        ((width, tok_count), BF16),
        ((tok_count, width), BF16),
        ((8, width), F32),
        ((half, depth, tok_count), BF16),
    ) + (((depth, tok_count), BF16, hbm_shape),) * half
    return pl.pallas_call(
        feed_back_kernel,
        out_shape=[make_shape(*item) for item in shapes],
        grid_spec=pltpu.PrefetchScalarGridSpec(
            num_scalar_prefetch=0,
            grid=(units // tile,),
            in_specs=[
                smem_spec(),
                pl.BlockSpec((tok_count, width), whole),
                pl.BlockSpec((tok_count, width), whole),
                pl.BlockSpec((tile, width), lambda step: (step, 0)),
                pl.BlockSpec((width, tile), lambda step: (0, step)),
                pl.BlockSpec((tok_count, tile), lambda step: (0, step)),
                pl.BlockSpec((tok_count, width), whole),
                pl.BlockSpec((tok_count, 1), whole),
                pl.BlockSpec((1, width), whole),
                pl.BlockSpec((width, width), whole),
            ],
            out_specs=[
                pl.BlockSpec((1, tile), lambda step: (0, step)),
                pl.BlockSpec((tok_count, width), whole),
                pl.BlockSpec((width, tok_count), whole),
                pl.BlockSpec((tok_count, width), whole),
                pl.BlockSpec((8, width), whole),
                pl.BlockSpec((count // 2, depth, tok_count), lambda step: (step, 0, 0)),
            ]
            + [pl.BlockSpec((depth, tok_count), whole)] * half,
            scratch_shapes=[
                pltpu.VMEM((count, depth, tok_count), BF16),
                pltpu.VMEM((tok_count, width), F32),
            ],
        ),
        cost_estimate=cost(10),
        compiler_params=params(1),
        name="feed_back",
    )(me, d_ffn, d_res, w_out, w_in, slope, normed, rstd, gain, w_o)


def attend_back_kernel(
    source_ref,
    me_ref,
    proj_ref,
    probs_ref,
    dctx_ref,
    done_ref,
    wqkv_ref,
    dattn_t_ref,
    dtok_ref,
    sums_ref,
    kept_ref,
    *refs,
):
    send_refs, held, dproj_ref = refs[:-2], refs[-2], refs[-1]
    row = pl.program_id(0)
    row_len, width = dctx_ref.shape
    blocks = held.shape[0]
    main = 3 * width // blocks
    scale = 1.0 / math.sqrt(HEAD_DIM)
    lane = lax.broadcasted_iota(jnp.int32, (row_len, LANES), 1)
    left = (lane < HEAD_DIM).astype(BF16)
    right = (lane >= HEAD_DIM).astype(BF16)

    def twice(values):
        return jnp.concatenate([values * left, values * right], axis=0)

    for pair in range(width // LANES):
        col = pair * LANES
        queries = proj_ref[:, col : col + LANES]
        key_rows = proj_ref[:, width + col : width + col + LANES]
        values = proj_ref[:, 2 * width + col : 2 * width + col + LANES]
        probs = probs_ref[0, pair]
        d_ctx = twice(dctx_ref[:, col : col + LANES])
        d_probs = dot(d_ctx, values, NT)
        probs_f = probs.astype(F32)
        inner = jnp.sum(probs_f * d_probs, axis=-1, keepdims=True)
        d_scores = (probs_f * (d_probs - inner)).astype(BF16)
        wide_scores = jnp.concatenate([d_scores[:row_len], d_scores[row_len:]], axis=1)
        d_query = dot(wide_scores, twice(key_rows)) * scale
        d_key = dot(d_scores, twice(queries), TN) * scale
        d_value = dot(probs, d_ctx, TN)
        for part, grad in ((0, d_query), (1, d_key), (2, d_value)):
            low = grad.astype(BF16)
            place = part * width + col
            dproj_ref[:, place : place + LANES] = low
            turned = low.T
            start = place
            while start < place + LANES:
                block, offset = divmod(start, main)
                stop = min(place + LANES, (block + 1) * main)
                held[block, offset : offset + stop - start, :] = turned[
                    start - place : stop - place, :
                ]
                start = stop
            before = jnp.where(row == 0, 0.0, sums_ref[:, place : place + LANES])
            sums_ref[:, place : place + LANES] = before + column_sum(low.astype(F32))

    rest = width // blocks
    for block in range(blocks):
        held[block, main:, :] = dattn_t_ref[block * rest : (block + 1) * rest, :]
    part_blocks(me_ref[0] & 1, held, kept_ref, send_refs)
    grad = done_ref[...] + dot(dproj_ref[...], wqkv_ref[...], NT)
    dtok_ref[0] = grad.astype(BF16)


def attend_back(sources, me, proj, probs, d_ctx, d_one, w_qkv, d_attn_t, wide_count):
    tok_count, width = d_ctx.shape
    kept_rows = tok_count // LANES
    half = wide_count // 2
    depth = 4 * width // wide_count
    shapes = (
        ((wide_count, LANES, width), BF16),
        ((1, 3 * width), F32),
        ((half, depth, tok_count), BF16),
    ) + (((depth, tok_count), BF16, hbm_shape),) * half
    return pl.pallas_call(
        attend_back_kernel,
        out_shape=[make_shape(*item) for item in shapes],
        grid_spec=pltpu.PrefetchScalarGridSpec(
            num_scalar_prefetch=2,
            grid=(kept_rows,),
            in_specs=[
                pl.BlockSpec((LANES, 3 * width), lambda row, src, me: (row, 0)),
                pl.BlockSpec((1,) + probs.shape[1:], lambda row, src, me: (row, 0, 0, 0)),
                pl.BlockSpec((LANES, width), lambda row, src, me: (row, 0)),
                pl.BlockSpec((LANES, width), lambda row, src, me: (row, 0)),
                pl.BlockSpec((width, 3 * width), lambda row, src, me: (0, 0)),
                pl.BlockSpec((width, LANES), lambda row, src, me: (0, row)),
            ],
            out_specs=[
                pl.BlockSpec((1, LANES, width), lambda row, src, me: (src[row], 0, 0)),
                pl.BlockSpec((1, 3 * width), lambda row, src, me: (0, 0)),
                pl.BlockSpec((half, depth, LANES), lambda row, src, me: (0, 0, row)),
            ]
            + [pl.BlockSpec((depth, LANES), lambda row, src, me: (0, row))] * half,
            scratch_shapes=[
                pltpu.VMEM((wide_count, depth, LANES), BF16),
                pltpu.VMEM((LANES, 3 * width), BF16),
            ],
        ),
        cost_estimate=cost(20),
        compiler_params=params(1),
        name="attend_back",
    )(sources, me, proj, probs, d_ctx, d_one, w_qkv, d_attn_t)


def home_kernel(dest_ref, rows_ref, out_ref, sems):
    slot_dev = out_ref.shape[0]

    def copy(slot):
        return pltpu.make_async_copy(
            rows_ref.at[jnp.maximum(dest_ref[slot], 0)], out_ref.at[slot], sems.at[slot]
        )

    for slot in range(slot_dev):
        copy(slot).start()
    for slot in range(slot_dev):
        copy(slot).wait()

        @pl.when(dest_ref[slot] < 0)
        def _():
            out_ref[slot] = jnp.zeros(out_ref.shape[1:], out_ref.dtype)


def home_rows(destination, rows):
    count = destination.shape[0]
    return pl.pallas_call(
        home_kernel,
        out_shape=jax.ShapeDtypeStruct((count,) + rows.shape[1:], rows.dtype),
        in_specs=[smem_spec(), pl.BlockSpec(memory_space=pl.ANY)],
        out_specs=vmem_spec(),
        scratch_shapes=[pltpu.SemaphoreType.DMA((count,))],
        cost_estimate=cost(3),
        compiler_params=params(),
        name="home_rows",
    )(destination, rows)


def block_at(index, bit, value):
    low = index & ((1 << bit) - 1)
    return ((index >> bit) << (bit + 1)) | (value << bit) | low


def grad_kernel(first_bit, second_bit, spans, blocks, me_ref, own_ref, *refs):
    recv_refs, refs = refs[:blocks], refs[blocks:]
    step = pl.program_id(0)
    half_steps = pl.num_programs(0) // 2
    terms = len(spans)
    own_xs, recv_xs = refs[:terms], refs[terms : 2 * terms]
    outs = refs[2 * terms : 2 * terms + 4]
    own_lefts = refs[2 * terms + 4 : 3 * terms + 4]
    recv_lefts = refs[3 * terms + 4 :]
    me = me_ref[0]
    for half, bit in ((0, first_bit), (1, second_bit)):

        @pl.when(step == half * half_steps)
        def _():
            side = (me >> bit) & 1
            for block in range(blocks):
                low = block & ((1 << (bit - 1)) - 1)
                rest = ((block >> bit) << (bit - 1)) | low
                kept = ((block >> (bit - 1)) & 1) == side
                index = jnp.where(kept, rest, rest + blocks // 2)
                for (start, stop), own_left, recv_left in zip(spans, own_lefts, recv_lefts):
                    own_left[index] = own_ref[block, start:stop, :]
                    recv_left[index] = recv_refs[block][start:stop, :]

    for term, (start, stop) in enumerate(spans):
        rows = stop - start
        chunk = blocks if blocks * rows <= 384 else blocks // 2
        for base in range(0, blocks, chunk):
            span = slice(base, base + chunk)
            flat = lambda left: left[span].reshape(chunk * rows, left.shape[2])
            part = dot(flat(own_lefts[term]), own_xs[term][...])
            part = part + dot(flat(recv_lefts[term]), recv_xs[term][...])
            part = part.astype(BF16).reshape(chunk, rows, part.shape[1])
            for index in range(chunk):
                block = base + index
                role, place = divmod(block, blocks // 2)
                for half in range(2):

                    @pl.when((step < half_steps) == (half == 0))
                    def _():
                        outs[2 * half + role][place, start:stop, :] = part[index]


def grad_terms(me, own, received, own_xs, recv_xs, spans, first_bit, second_bit, tile):
    blocks = len(received)
    rows, tok_count = received[0].shape
    columns = own_xs[0][0].shape[-1]
    steps = columns // tile
    half = steps // 2

    def x_spec(item):
        array, lead = item
        if lead is None:
            return pl.BlockSpec((tok_count, tile), lambda step: (0, step))
        return pl.BlockSpec((pl.Squeezed(), tok_count, tile), lambda step: (lead, 0, step))

    out_block = (blocks // 2, rows, tile)
    first_spec = pl.BlockSpec(out_block, lambda step: (0, 0, jnp.minimum(step, half - 1)))
    second_spec = pl.BlockSpec(out_block, lambda step: (0, 0, jnp.maximum(step - half, 0)))
    shape = hbm_shape((blocks // 2, rows, columns // 2), BF16)
    whole = lambda step: (0, 0, 0)
    lefts = [pltpu.VMEM((blocks, stop - start, tok_count), BF16) for start, stop in spans]
    return pl.pallas_call(
        functools.partial(grad_kernel, first_bit, second_bit, spans, blocks),
        out_shape=[shape] * 4,
        grid_spec=pltpu.PrefetchScalarGridSpec(
            num_scalar_prefetch=0,
            grid=(steps,),
            in_specs=[
                smem_spec(),
                pl.BlockSpec(own.shape, whole),
            ]
            + [pl.BlockSpec((rows, tok_count), lambda step: (0, 0))] * blocks
            + [x_spec(item) for item in own_xs + recv_xs],
            out_specs=[first_spec, first_spec, second_spec, second_spec],
            scratch_shapes=lefts + lefts,
        ),
        cost_estimate=cost(7),
        compiler_params=params(1),
        name="grad_terms",
    )(me, own, *received, *[item[0] for item in own_xs + recv_xs])


def fold_kernel(bits, places, me_ref, *refs):
    me = me_ref[0]
    for half in range(2):
        kept_ref, recv_ref = refs[2 * half], refs[2 * half + 1]
        keep_out, send_out = refs[4 + 2 * half], refs[5 + 2 * half]
        side = (me >> bits[half]) & 1
        for index in range(keep_out.shape[0]):
            for value, out_ref in ((1 - side, send_out), (side, keep_out)):
                block = block_at(index, places[half], value)
                out_ref[index] = add_low(kept_ref[block], recv_ref[block])


def fold(me, halves, bits, places):
    shapes = []
    for kept, _ in halves:
        shapes += [hbm_shape((kept.shape[0] // 2,) + kept.shape[1:], BF16)] * 2
    return pl.pallas_call(
        functools.partial(fold_kernel, bits, places),
        out_shape=shapes,
        in_specs=[smem_spec()] + [vmem_spec()] * 4,
        out_specs=[vmem_spec()] * 4,
        cost_estimate=cost(0.5),
        compiler_params=params(),
        name="fold",
    )(me, *halves[0], *halves[1])


def piece_kernel(turned, me_ref, *refs):
    outs, held = refs[4:-1], refs[-1]
    count = len(outs)
    depth = held.shape[1] if turned else held.shape[2]
    for half in range(2):
        total = add_low(refs[2 * half][0], refs[2 * half + 1][0])
        if turned:
            total = total.T
        for index in range(count // 2):
            span = slice(index * depth, (index + 1) * depth)
            held[half * (count // 2) + index] = total[span, :] if turned else total[:, span]
    for step in range(count):
        outs[step][...] = held[me_ref[0] ^ step]


def narrow_pieces(me, halves, narrow_count, turned):
    _, rows, columns = halves[0][0].shape
    depth = 2 * columns // narrow_count
    shape = (depth, rows) if turned else (rows, depth)
    return pl.pallas_call(
        functools.partial(piece_kernel, turned),
        out_shape=[hbm_shape(shape, BF16)] * narrow_count,
        in_specs=[smem_spec()] + [vmem_spec()] * 4,
        out_specs=[vmem_spec()] * narrow_count,
        scratch_shapes=[pltpu.VMEM((narrow_count,) + shape, BF16)],
        cost_estimate=cost(1),
        compiler_params=params(),
        name="narrow_pieces",
    )(me, *halves[0], *halves[1])


def sum_kernel(count, *refs):
    total = refs[0][...].astype(F32)
    for ref in refs[1:count]:
        total = total + ref[...].astype(F32)
    start = 0
    for out_ref in refs[count:]:
        out_ref[...] = total[:, start : start + out_ref.shape[1]]
        start += out_ref.shape[1]


def sum_pieces(pieces, cuts=None):
    shape = pieces[0].shape
    outs = [jax.ShapeDtypeStruct((shape[0], cut), F32) for cut in cuts or (shape[1],)]
    return pl.pallas_call(
        functools.partial(sum_kernel, len(pieces)),
        out_shape=outs,
        in_specs=[vmem_spec()] * len(pieces),
        out_specs=[vmem_spec()] * len(outs),
        cost_estimate=cost(1),
        compiler_params=params(),
        name="sum_pieces",
    )(*pieces)


def pack_kernel(cuts, *refs):
    out_ref = refs[-1]
    place = 0
    for index, row, start, stop in cuts:
        for at in range(start, stop, LANES):
            out_ref[place : place + 1, :] = refs[index][row : row + 1, at : at + LANES]
            place += 1


def pack_vectors(arrays, cuts):
    lines = sum(stop - start for _, _, start, stop in cuts) // LANES
    return pl.pallas_call(
        functools.partial(pack_kernel, cuts),
        out_shape=jax.ShapeDtypeStruct((lines, LANES), F32),
        in_specs=[vmem_spec()] * len(arrays),
        out_specs=vmem_spec(),
        cost_estimate=cost(0.5),
        compiler_params=params(),
        name="pack_vectors",
    )(*arrays)


def swap(values, axis, bit):
    count = lax.axis_size(axis)
    return lax.ppermute(values, axis, [(i, i ^ (1 << bit)) for i in range(count)])


def trade(pieces):
    count = len(pieces)
    got = [pieces[0]]
    for step in range(1, count):
        got.append(lax.ppermute(pieces[step], "narrow", [(i, i ^ step) for i in range(count)]))
    return got


def pick(values, dim, index):
    return lax.dynamic_index_in_dim(values, index, dim, keepdims=False)


def add_low(kept, received):
    return (kept.astype(F32) + received.astype(F32)).astype(BF16)


def after(value, *others):
    return lax.optimization_barrier((value,) + others)[0]


def to_partner(blocks):
    return [swap(block, "wide", 0) for block in blocks]


class Folding:
    def __init__(self, me, outs, orders, *gates):
        self.me = me
        self.orders = orders
        self.left = [sorted(order) for order in orders]
        self.kept = [outs[0], outs[2]]
        self.sent = [outs[1], outs[3]]
        self.level = 0
        self.exchange(*gates)

    def exchange(self, *gates):
        self.received = [
            swap(after(self.sent[half], *gates), "wide", self.orders[half][self.level])
            for half in range(2)
        ]
        for half in range(2):
            self.left[half].remove(self.orders[half][self.level])
        self.level += 1

    def halves(self):
        return [(self.kept[half], self.received[half]) for half in range(2)]

    def step(self, *gates):
        bits = [order[self.level] for order in self.orders]
        places = [left.index(bit) for left, bit in zip(self.left, bits)]
        outs = fold(self.me, self.halves(), bits, places)
        self.kept = [outs[0], outs[2]]
        self.sent = [outs[1], outs[3]]
        self.exchange(*gates)

    def gate(self, *others):
        self.kept[0] = after(self.kept[0], *others)

    def finish(self, me_narrow, narrow_count, turned):
        while self.level < len(self.orders[0]):
            self.step()
        return narrow_pieces(me_narrow, self.halves(), narrow_count, turned)


def hop(values, axis, bit):
    return values + swap(values, axis, bit)


def on_device(
    tokens,
    segments,
    destination,
    pair_index,
    targets,
    w_qkv,
    b_qv,
    w_o,
    b_o,
    gain_one,
    shift_one,
    w_in,
    b_in,
    w_out,
    b_out,
    gain_two,
    shift_two,
):
    wide_count = lax.axis_size("wide")
    narrow_count = lax.axis_size("narrow")
    slot_dev, row_len, width = tokens.shape
    kept_rows = slot_dev // 2
    units = w_in.shape[1]
    me = lax.axis_index("wide")
    me_line = me.astype(jnp.int32).reshape(1)
    me_narrow = lax.axis_index("narrow").astype(jnp.int32).reshape(1)
    line = lambda vector: vector.reshape(1, -1)

    sent = build_send(tokens, segments, destination, pair_index, targets, wide_count)
    got = lax.all_to_all(sent, "wide", split_axis=0, concat_axis=0, tiled=True)
    full_bias = jnp.concatenate(
        [b_qv[:width], jnp.zeros((width,), F32), b_qv[width:]]
    ).reshape(1, 3 * width)
    stack, proj, probs, hidden, norm_one, rstd_one, labels, label_cols, meta, sources = (
        attend_forward(
            got, w_qkv, full_bias, w_o, line(b_o), line(gain_one), line(shift_one), kept_rows
        )
    )
    stack_recv = swap(stack, "wide", 0)
    act, slope, encoded, norm_two, rstd_two, pooled, pooled_copies = feed_forward(
        stack,
        hidden,
        w_in,
        line(b_in),
        w_out,
        line(b_out),
        line(gain_two),
        line(shift_two),
        labels,
        wide_count,
    )
    act_recv = swap(act, "wide", 0)
    place, target, first, second = route(me_line, meta, pair_index, kept_rows)
    pooled_all = lax.all_to_all(
        pooled_copies, "wide", split_axis=0, concat_axis=0, tiled=True
    ).reshape(wide_count * kept_rows * SEG_ROW, width)
    similarity = cosine_pairs(first, second, pooled_all).reshape(-1)
    d_res_two, d_ffn, sums_two, own_out, *send_out = loss_back(
        me_line,
        pooled,
        pooled_all,
        place,
        target,
        labels,
        label_cols,
        norm_two,
        rstd_two,
        line(gain_two),
        wide_count,
    )

    bits = wide_count.bit_length() - 1
    middle = 1 + (bits - 1) // 2
    low_first = list(range(1, bits))
    high_first = list(range(middle, bits)) + list(range(1, middle))
    orders = (low_first, high_first)
    first_bits = (low_first[0], high_first[0])
    rows_out = own_out.shape[1]
    fold_out = Folding(
        me_line,
        grad_terms(
            me_line,
            own_out,
            to_partner(send_out),
            [(act, None)],
            [(act_recv, None)],
            ((0, rows_out),),
            *first_bits,
            512,
        ),
        orders,
    )
    sum_b_in, d_one, d_attn_t, d_ctx, sums_one, own_in, *send_in = feed_back(
        me_line,
        after(d_ffn, *fold_out.sent),
        d_res_two,
        w_out,
        w_in,
        slope,
        norm_one,
        rstd_one,
        line(gain_one),
        w_o,
        wide_count,
    )
    rows_in = own_in.shape[1]
    recv_in = to_partner(send_in)
    fold_out.step()
    pieces_out = fold_out.finish(me_narrow, narrow_count, False)
    fold_in = Folding(
        me_line,
        grad_terms(
            me_line,
            own_in,
            after(tuple(recv_in), *fold_out.sent),
            [(stack, 2)],
            [(stack_recv, 2)],
            ((0, rows_in),),
            *first_bits,
            width // 2,
        ),
        orders,
        tuple(pieces_out),
    )
    traded_out = trade(pieces_out)
    d_rows, sums_qkv, own_mix, *send_mix = attend_back(
        sources,
        me_line,
        proj,
        probs,
        after(d_ctx, tuple(pieces_out), *fold_in.sent),
        d_one,
        w_qkv,
        d_attn_t,
        wide_count,
    )
    recv_mix = to_partner(after(tuple(send_mix), tuple(traded_out)))
    vectors = pack_vectors(
        (sums_qkv, sums_one, sum_b_in, sums_two),
        (
            (0, 0, 0, width),
            (0, 0, 2 * width, 3 * width),
            (1, 2, 0, width),
            (1, 0, 0, width),
            (1, 1, 0, width),
            (2, 0, 0, units),
            (3, 2, 0, width),
            (3, 0, 0, width),
            (3, 1, 0, width),
        ),
    )
    fold_in.gate(d_rows, tuple(traded_out))
    fold_in.step()
    home = lax.all_to_all(
        after(d_rows, *fold_in.sent), "wide", split_axis=0, concat_axis=0, tiled=True
    )
    cols_qkv = 3 * width // wide_count
    rows_mix = own_mix.shape[1]
    (grad_w_out,) = sum_pieces(traded_out)
    grad_w_out = grad_w_out.T
    outs_mix = grad_terms(
        me_line,
        own_mix,
        after(tuple(recv_mix), *fold_in.sent),
        [(stack, 0), (stack, 1)],
        [(stack_recv, 0), (stack_recv, 1)],
        ((0, cols_qkv), (cols_qkv, rows_mix)),
        *first_bits,
        width // 2,
    )
    vectors = hop(after(vectors, *outs_mix), "wide", 0)
    vectors = hop(vectors, "narrow", 0)
    fold_mix = Folding(
        me_line,
        outs_mix,
        orders,
        vectors,
        grad_w_out,
        similarity,
        *fold_in.received,
    )
    grad_tokens = home_rows(destination, home)
    pieces_in = fold_in.finish(me_narrow, narrow_count, True)
    traded_in = trade(pieces_in)
    fold_mix.gate(grad_tokens, tuple(traded_in))
    fold_mix.step()
    for bit in range(1, narrow_count.bit_length() - 1):
        vectors = hop(vectors, "narrow", bit)
    (grad_w_in,) = sum_pieces(traded_in)
    fold_mix.gate(vectors)
    pieces_mix = fold_mix.finish(me_narrow, narrow_count, True)
    for bit in range(1, bits):
        vectors = hop(vectors if bit > 1 else after(vectors, tuple(pieces_mix)), "wide", bit)
    grad_w_qkv, grad_w_o = sum_pieces(
        after(tuple(trade(pieces_mix)), vectors), (cols_qkv, rows_mix - cols_qkv)
    )
    vectors = vectors.reshape(-1)
    cuts = (2 * width, width, width, width, units, width, width, width)
    outs = []
    start = 0
    for size in cuts:
        outs.append(vectors[start : start + size])
        start += size
    grad_b_qv, grad_b_o, grad_gain_one, grad_shift_one = outs[:4]
    grad_b_in, grad_b_out, grad_gain_two, grad_shift_two = outs[4:]
    return (
        encoded.reshape(kept_rows, row_len, width),
        similarity,
        grad_tokens,
        grad_w_qkv,
        grad_b_qv,
        grad_w_o,
        grad_b_o,
        grad_gain_one,
        grad_shift_one,
        grad_w_in,
        grad_b_in,
        grad_w_out,
        grad_b_out,
        grad_gain_two,
        grad_shift_two,
    )


def solution(mesh):
    rows = ("wide", "narrow")
    in_specs = (P(rows, None, None), P(rows, None), P(rows), P(rows, None), P(rows)) + (P(),) * 12
    matrix = P("narrow", "wide")
    out_specs = (
        P(rows, None, None),
        P(rows),
        P(rows, None, None),
        matrix,
        P(),
        matrix,
        P(),
        P(),
        P(),
        matrix,
        P(),
        matrix,
        P(),
        P(),
        P(),
    )
    return jax.shard_map(
        on_device, mesh=mesh, in_specs=in_specs, out_specs=out_specs, check_vma=False
    )
```

```python
import functools
import math

import jax
import jax.numpy as jnp
from jax import lax
from jax.experimental import pallas as pl
from jax.experimental.pallas import tpu as pltpu
from jax.sharding import PartitionSpec as P

HEAD_DIM = 64
SEG_ROW = 8
LANES = 128
META_ROWS = 16
NEG_FILL = -1e30
NORM_EPS = 1e-12
COS_EPS = 1e-06
F32 = jnp.float32
BF16 = jnp.bfloat16
VMEM_LIMIT = 67043328


def cost(micros):
    return pl.CostEstimate(flops=0, bytes_accessed=int(micros * 3.0e6), transcendentals=0)


NT = (((1,), (1,)), ((), ()))
TN = (((0,), (0,)), ((), ()))


def vmem_spec():
    return pl.BlockSpec(memory_space=pltpu.VMEM)


def hbm_shape(shape, dtype):
    return pltpu.HBM(shape, dtype)


def make_shape(shape, dtype, make=jax.ShapeDtypeStruct):
    return make(shape, dtype)


def params(steps=0):
    return pltpu.CompilerParams(
        dimension_semantics=("arbitrary",) * steps if steps else None,
        vmem_limit_bytes=VMEM_LIMIT,
    )


def split_three(values):
    high = values.astype(BF16)
    rest = values - high.astype(F32)
    middle = rest.astype(BF16)
    low = (rest - middle.astype(F32)).astype(BF16)
    return (high, middle, low)


def dot(left, right, dims=None):
    if dims is None:
        return jnp.dot(left, right, preferred_element_type=F32)
    return lax.dot_general(left, right, dims, preferred_element_type=F32)


def column_sum(values):
    return jnp.sum(values, axis=0, keepdims=True)


def row_mean(values):
    return jnp.mean(values, axis=-1, keepdims=True)


def prep_kernel(dest_ref, pair_ref, targ_ref, tok_ref, seg_ref, out_ref, sems):
    slot_dev = dest_ref.shape[0]
    wide_count, _, width = out_ref.shape
    row_len = tok_ref.shape[1]
    sources = []
    lives = []
    copies = []
    for owner in range(wide_count):
        found = jnp.int32(0)
        live = dest_ref[0] == owner
        for slot in range(1, slot_dev):
            match = dest_ref[slot] == owner
            found = jnp.where(match, slot, found)
            live = live | match
        sources.append(found)
        lives.append(live)
        copy = pltpu.make_async_copy(
            tok_ref.at[found], out_ref.at[owner, pl.ds(0, row_len), :], sems.at[owner]
        )
        copy.start()
        copies.append(copy)
    lane = lax.broadcasted_iota(jnp.int32, (1, LANES), 1)
    dest = jnp.full((1, LANES), -1, jnp.int32)
    for slot in range(slot_dev):
        dest = jnp.where(lane // SEG_ROW == slot, dest_ref[slot], dest)
    partner = jnp.zeros((1, LANES), jnp.int32)
    target = jnp.zeros((1, LANES), F32)
    for pair in range(pair_ref.shape[1]):
        first = pair_ref[0, pair]
        second = pair_ref[1, pair]
        at_first = lane == first
        at_second = lane == second
        partner = jnp.where(at_first, second, jnp.where(at_second, first, partner))
        target = jnp.where(at_first | at_second, targ_ref[0, pair], target)
    high, middle, low = split_three(target)
    fixed = [dest.astype(F32), partner.astype(F32)]
    fixed += [high.astype(F32), middle.astype(F32), low.astype(F32)]
    fixed.append(jnp.zeros((META_ROWS - 1 - len(fixed), LANES), F32))
    for owner in range(wide_count):
        labels = seg_ref[pl.ds(sources[owner], 1), :].astype(F32)
        labels = jnp.where(lives[owner], labels, -1.0)
        table = jnp.concatenate([labels] + fixed, axis=0)
        out_ref[owner, row_len:, :LANES] = table.astype(BF16)
        out_ref[owner, row_len:, LANES:] = jnp.zeros((META_ROWS, width - LANES), BF16)
    for copy in copies:
        copy.wait()


def smem_spec():
    return pl.BlockSpec(memory_space=pltpu.SMEM)


def build_send(tokens, segments, destination, pair_index, targets, wide_count):
    slot_dev, row_len, width = tokens.shape
    return pl.pallas_call(
        prep_kernel,
        out_shape=jax.ShapeDtypeStruct((wide_count, row_len + META_ROWS, width), BF16),
        in_specs=[smem_spec()] * 3 + [pl.BlockSpec(memory_space=pl.ANY), vmem_spec()],
        out_specs=vmem_spec(),
        scratch_shapes=[pltpu.SemaphoreType.DMA((wide_count,))],
        cost_estimate=cost(3),
        compiler_params=params(),
        name="build_send",
    )(destination, pair_index.T, targets.reshape(1, -1), tokens, segments)


def attend_kernel(
    got_ref,
    wqkv_ref,
    bias_ref,
    wo_ref,
    bo_ref,
    gain_ref,
    shift_ref,
    stack_ref,
    proj_ref,
    probs_ref,
    hid_ref,
    norm_ref,
    rstd_ref,
    lab_ref,
    labcol_ref,
    meta_ref,
    source_ref,
):
    x_ref, ctx_ref, low_ref = stack_ref.at[0], stack_ref.at[1], stack_ref.at[2]
    wide_count = got_ref.shape[0]
    tok_count, width = hid_ref.shape
    row_len = got_ref.shape[1] - META_ROWS
    kept_rows = tok_count // row_len
    seen = jnp.int32(0)
    sources = [jnp.int32(0)] * kept_rows
    for slot in range(wide_count):
        top = jnp.max(got_ref[slot, row_len : row_len + 1, :LANES].astype(F32))
        live = top >= 0.0
        for row in range(kept_rows):
            sources[row] = jnp.where(live & (seen == row), slot, sources[row])
        seen = seen + live.astype(jnp.int32)
    meta_ref[...] = got_ref[:, row_len:, :LANES]
    for row in range(kept_rows):
        source_ref[row] = sources[row]
        span = pl.ds(row * row_len, row_len)
        x_ref[span, :] = got_ref[sources[row], :row_len, :]
        tag = got_ref[sources[row], row_len : row_len + 1, :LANES].astype(F32)
        lab_ref[row : row + 1, :] = tag
        labcol_ref[span, :] = jnp.broadcast_to(tag, (LANES, LANES)).T
    total_cols = proj_ref.shape[1]
    tile = 256
    for start in range(0, total_cols, tile):
        cols = slice(start, start + tile)
        proj_ref[:, cols] = (dot(x_ref[...], wqkv_ref[:, cols]) + bias_ref[:, cols]).astype(BF16)

    scale = 1.0 / math.sqrt(HEAD_DIM)
    lane = lax.broadcasted_iota(jnp.int32, (row_len, LANES), 1)
    left = (lane < HEAD_DIM).astype(BF16)
    right = (lane >= HEAD_DIM).astype(BF16)

    def attend_row(row, carry):
        span = pl.ds(pl.multiple_of(row * row_len, row_len), row_len)
        same = labcol_ref[span, :] == lab_ref[pl.ds(row, 1), :]
        same = jnp.concatenate([same, same], axis=0)
        for pair in range(width // LANES):
            col = pair * LANES
            queries = proj_ref[span, col : col + LANES]
            key_rows = proj_ref[span, width + col : width + col + LANES]
            values = proj_ref[span, 2 * width + col : 2 * width + col + LANES]
            both = jnp.concatenate([queries * left, queries * right], axis=0)
            scores = jnp.where(same, dot(both, key_rows, NT) * scale, NEG_FILL)
            top = jnp.max(scores, axis=-1, keepdims=True)
            expo = jnp.exp(scores - top)
            total = jnp.sum(expo, axis=-1, keepdims=True)
            probs = (expo / total).astype(BF16)
            probs_ref[row, pair] = probs
            wide_probs = jnp.concatenate([probs[:row_len], probs[row_len:]], axis=1)
            split_values = jnp.concatenate([values * left, values * right], axis=0)
            ctx_ref[span, col : col + LANES] = dot(wide_probs, split_values).astype(BF16)
        return carry

    lax.fori_loop(0, kept_rows, attend_row, 0)
    for row in range(kept_rows):
        span = pl.ds(row * row_len, row_len)
        total = x_ref[span, :].astype(F32) + dot(ctx_ref[span, :], wo_ref[...]) + bo_ref[...]
        centered = total - row_mean(total)
        rstd = lax.rsqrt(row_mean(centered * centered) + NORM_EPS)
        normed = centered * rstd
        hidden = normed * gain_ref[...] + shift_ref[...]
        norm_ref[span, :] = normed
        rstd_ref[span, :] = rstd
        hid_ref[span, :] = hidden
        low_ref[span, :] = hidden.astype(BF16)


def attend_forward(got, w_qkv, bias, w_o, b_o, gain, shift, kept_rows):
    wide_count, slot_len, width = got.shape
    row_len = slot_len - META_ROWS
    tok_count = kept_rows * row_len
    shapes = (
        ((3, tok_count, width), BF16),
        ((tok_count, 3 * width), BF16),
        ((kept_rows, width // LANES, 2 * row_len, row_len), BF16),
        ((tok_count, width), F32),
        ((tok_count, width), F32),
        ((tok_count, 1), F32),
        ((8, LANES), F32),
        ((tok_count, LANES), F32),
        ((wide_count, META_ROWS, LANES), BF16),
        ((kept_rows,), jnp.int32),
    )
    return pl.pallas_call(
        attend_kernel,
        out_shape=[make_shape(*item) for item in shapes],
        in_specs=[vmem_spec()] * 7,
        out_specs=[vmem_spec()] * (len(shapes) - 1) + [smem_spec()],
        cost_estimate=cost(8),
        compiler_params=params(),
        name="attend_forward",
    )(got, w_qkv, bias, w_o, b_o, gain, shift)


def feed_kernel(
    low_ref,
    hid_ref,
    win_ref,
    bin_ref,
    wout_ref,
    bout_ref,
    gain_ref,
    shift_ref,
    lab_ref,
    act_ref,
    slope_ref,
    enc_ref,
    norm_ref,
    rstd_ref,
    pooled_ref,
    copies_ref,
    total_ref,
):
    step = pl.program_id(0)
    up = dot(low_ref[...], win_ref[...]) + bin_ref[...]
    phi = 0.5 * (1.0 + lax.erf(up * (1.0 / math.sqrt(2.0))))
    density = jnp.exp(-0.5 * up * up) * (1.0 / math.sqrt(2.0 * math.pi))
    act = (up * phi).astype(BF16)
    act_ref[...] = act
    slope_ref[...] = (phi + up * density).astype(BF16)
    part = dot(act, wout_ref[...])

    @pl.when(step == 0)
    def _():
        total_ref[...] = part + (hid_ref[...] + bout_ref[...])

    @pl.when(step > 0)
    def _():
        total_ref[...] += part

    @pl.when(step == pl.num_programs(0) - 1)
    def _():
        tok_count, width = total_ref.shape
        kept_rows = tok_count // LANES
        for row in range(kept_rows):
            span = slice(row * LANES, (row + 1) * LANES)
            total = total_ref[span, :]
            centered = total - row_mean(total)
            rstd = lax.rsqrt(row_mean(centered * centered) + NORM_EPS)
            normed = centered * rstd
            out = normed * gain_ref[...] + shift_ref[...]
            norm_ref[span, :] = normed
            rstd_ref[span, :] = rstd
            enc_ref[span, :] = out.astype(BF16)
            segment = lax.broadcasted_iota(jnp.int32, (SEG_ROW, LANES), 0).astype(F32)
            onehot = (lab_ref[row : row + 1, :] == segment).astype(F32)
            count = jnp.sum(onehot, axis=1, keepdims=True)
            high, middle, low = split_three(out)
            mask = onehot.astype(BF16)
            summed = dot(mask, high) + dot(mask, middle) + dot(mask, low)
            pooled_ref[row * SEG_ROW : (row + 1) * SEG_ROW, :] = (summed / count).astype(BF16)
        for owner in range(copies_ref.shape[0]):
            copies_ref[owner] = pooled_ref[...]


def feed_forward(stack, hidden, w_in, b_in, w_out, b_out, gain, shift, labels, wide_count):
    _, tok_count, width = stack.shape
    units = w_in.shape[1]
    tile = 512
    kept_rows = tok_count // LANES
    whole = lambda step: (0, 0)
    shapes = (
        ((tok_count, units), BF16),
        ((tok_count, units), BF16),
        ((tok_count, width), BF16),
        ((tok_count, width), F32),
        ((tok_count, 1), F32),
        ((kept_rows * SEG_ROW, width), BF16),
        ((wide_count, kept_rows * SEG_ROW, width), BF16),
    )
    return pl.pallas_call(
        feed_kernel,
        out_shape=[make_shape(*item) for item in shapes],
        grid_spec=pltpu.PrefetchScalarGridSpec(
            num_scalar_prefetch=0,
            grid=(units // tile,),
            in_specs=[
                pl.BlockSpec((pl.Squeezed(), tok_count, width), lambda step: (2, 0, 0)),
                pl.BlockSpec((tok_count, width), whole),
                pl.BlockSpec((width, tile), lambda step: (0, step)),
                pl.BlockSpec((1, tile), lambda step: (0, step)),
                pl.BlockSpec((tile, width), lambda step: (step, 0)),
                pl.BlockSpec((1, width), whole),
                pl.BlockSpec((1, width), whole),
                pl.BlockSpec((1, width), whole),
                pl.BlockSpec((8, LANES), whole),
            ],
            out_specs=[
                pl.BlockSpec((tok_count, tile), lambda step: (0, step)),
                pl.BlockSpec((tok_count, tile), lambda step: (0, step)),
                pl.BlockSpec((tok_count, width), whole),
                pl.BlockSpec((tok_count, width), whole),
                pl.BlockSpec((tok_count, 1), whole),
                pl.BlockSpec((kept_rows * SEG_ROW, width), whole),
                pl.BlockSpec((wide_count, kept_rows * SEG_ROW, width), lambda step: (0, 0, 0)),
            ],
            scratch_shapes=[pltpu.VMEM((tok_count, width), F32)],
        ),
        cost_estimate=cost(10),
        compiler_params=params(1),
        name="feed_forward",
    )(stack, hidden, w_in, b_in, w_out, b_out, gain, shift, labels)


def route_kernel(me_ref, meta_ref, pair_ref, place_ref, targ_ref, first_ref, second_ref):
    wide_count = meta_ref.shape[0]
    me = me_ref[0]
    kept_rows = place_ref.shape[0] // SEG_ROW
    me_f = me.astype(F32)

    def table(row):
        return jnp.concatenate(
            [meta_ref[j, row : row + 1, :LANES].astype(F32) for j in range(wide_count)], axis=0
        )

    labels = table(0)
    dest = table(1)
    lane = lax.broadcasted_iota(jnp.int32, (wide_count, LANES), 1)
    slots = SEG_ROW * 2 * kept_rows
    dest = jnp.where(lane < slots, dest, -1.0)
    partner = table(2)
    target = table(3) + table(4) + table(5)
    sends = jnp.zeros((wide_count, LANES), F32)
    for owner in range(wide_count):
        to_owner = jnp.max((dest == float(owner)).astype(F32), axis=1, keepdims=True)
        sends = sends + jnp.where(lane == owner, to_owner, 0.0)
    row_id = lax.broadcasted_iota(jnp.int32, (wide_count, wide_count), 0)
    col_id = lax.broadcasted_iota(jnp.int32, (wide_count, wide_count), 1)
    below = (col_id < row_id).astype(BF16)
    earlier = dot(below, sends.astype(BF16))
    rank = jnp.zeros((wide_count, LANES), F32)
    for owner in range(wide_count):
        rank = rank + jnp.where(dest == float(owner), earlier[:, owner : owner + 1], 0.0)
    segment = (lane % SEG_ROW).astype(F32)
    per_owner = float(kept_rows * SEG_ROW)
    place = jnp.where(dest >= 0.0, dest * per_owner + rank * float(SEG_ROW) + segment, -1.0)
    live = (labels[:, 0:1] >= 0.0).astype(F32)
    my_rank = dot(below, jnp.broadcast_to(live, (wide_count, LANES)).astype(BF16))
    seg_lane = lax.broadcasted_iota(jnp.int32, (SEG_ROW, LANES), 1)
    seg_id = lax.broadcasted_iota(jnp.int32, (SEG_ROW, LANES), 0)
    for row in range(kept_rows):
        chosen = (live > 0.0) & (my_rank[:, 0:1] == float(row))
        pick = lambda values: column_sum(jnp.where(chosen, values, 0.0))
        own = (pick(dest) == me_f) & (seg_lane % SEG_ROW == seg_id)
        gather = lambda mask, values: jnp.sum(jnp.where(mask, values, 0.0), axis=1, keepdims=True)
        other = gather(own, pick(partner))
        at_other = seg_lane.astype(F32) == other
        out = slice(row * SEG_ROW, (row + 1) * SEG_ROW)
        place_ref[out, :] = gather(at_other, pick(place))
        targ_ref[out, :] = gather(own, pick(target))
    mine = lax.broadcasted_iota(jnp.int32, (wide_count, LANES), 0) == me
    my_place = column_sum(jnp.where(mine, place, 0.0))
    pair_lane = lax.broadcasted_iota(jnp.int32, (pair_ref.shape[0], LANES), 1)
    for column, out_ref in ((0, first_ref), (1, second_ref)):
        at_slot = pair_lane == pair_ref[:, column : column + 1]
        out_ref[...] = jnp.sum(jnp.where(at_slot, my_place, 0.0), axis=1, keepdims=True)


def route(me, meta, pair_index, kept_rows):
    wide_count = meta.shape[0]
    own = kept_rows * SEG_ROW
    pairs = pair_index.shape[0]
    shapes = (
        ((own, 1), F32),
        ((own, 1), F32),
        ((pairs, 1), F32),
        ((pairs, 1), F32),
    )
    return pl.pallas_call(
        route_kernel,
        out_shape=[make_shape(*item) for item in shapes],
        in_specs=[smem_spec(), vmem_spec(), vmem_spec()],
        out_specs=[vmem_spec()] * len(shapes),
        cost_estimate=cost(1),
        compiler_params=params(),
        name="route",
    )(me, meta, pair_index)


def pick_rows(place_ref, all_ref):
    lane = lax.broadcasted_iota(jnp.int32, (place_ref.shape[0], all_ref.shape[0]), 1)
    return dot((lane.astype(F32) == place_ref[...]).astype(BF16), all_ref[...])


def cosine_parts(left, right):
    inner = row_mean(left * right)
    left_inv = lax.rsqrt(row_mean(left * left) + COS_EPS)
    right_inv = lax.rsqrt(row_mean(right * right) + COS_EPS)
    return (inner, left_inv, right_inv)


def cosine_kernel(first_ref, second_ref, all_ref, sim_ref):
    left = pick_rows(first_ref, all_ref)
    right = pick_rows(second_ref, all_ref)
    inner, left_inv, right_inv = cosine_parts(left, right)
    sim = inner * left_inv * right_inv
    sim_ref[...] = jnp.where(first_ref[...] >= 0.0, sim, 0.0)


def cosine_pairs(first, second, pooled_all):
    return pl.pallas_call(
        cosine_kernel,
        out_shape=jax.ShapeDtypeStruct(first.shape, F32),
        in_specs=[vmem_spec()] * 3,
        out_specs=vmem_spec(),
        cost_estimate=cost(1),
        compiler_params=params(),
        name="cosine_pairs",
    )(first, second, pooled_all)


def part_blocks(parity, held, own_ref, send_refs, first=0):
    for index in range(held.shape[0] // 2):
        own_ref[index] = held[2 * index + parity]
        send_refs[first + index][...] = held[2 * index + 1 - parity]


def norm_back(grad, normed, rstd, gain):
    scaled = grad * gain
    return rstd * (scaled - row_mean(scaled) - normed * row_mean(scaled * normed))


def loss_back_body(
    me_ref,
    own_ref,
    all_ref,
    place_ref,
    targ_ref,
    lab_ref,
    labcol_ref,
    norm_ref,
    rstd_ref,
    gain_ref,
    dres_ref,
    dffn_ref,
    sums_ref,
    kept_ref,
    send_refs,
    held,
):
    depth = held.shape[1]
    tok_count, width = norm_ref.shape
    kept_rows = tok_count // LANES
    left = own_ref[...].astype(F32)
    right = pick_rows(place_ref, all_ref)
    inner, left_inv, right_inv = cosine_parts(left, right)
    error = 2.0 * (inner * left_inv * right_inv - targ_ref[...])
    factor = error * left_inv * right_inv * (1.0 / width)
    d_pooled = (factor * (right - left * (inner * left_inv * left_inv))).astype(BF16).astype(F32)
    gain_sum = jnp.zeros((1, width), F32)
    shift_sum = jnp.zeros((1, width), F32)
    bias_sum = jnp.zeros((1, width), F32)
    lane = lax.broadcasted_iota(jnp.int32, (LANES, LANES), 1).astype(F32)
    for row in range(kept_rows):
        span = slice(row * LANES, (row + 1) * LANES)
        segment = lax.broadcasted_iota(jnp.int32, (SEG_ROW, LANES), 0).astype(F32)
        count = jnp.sum(
            (lab_ref[row : row + 1, :] == segment).astype(F32), axis=1, keepdims=True
        )
        per_token = d_pooled[row * SEG_ROW : (row + 1) * SEG_ROW, :] / count
        shift_sum = shift_sum + column_sum(per_token * count)
        padded = jnp.concatenate([per_token, jnp.zeros((LANES - SEG_ROW, width), F32)], axis=0)
        onehot = (labcol_ref[span, :] == lane).astype(BF16)
        high, middle, low = split_three(padded)
        d_out = dot(onehot, high) + dot(onehot, middle) + dot(onehot, low)
        normed = norm_ref[span, :]
        d_res = norm_back(d_out, normed, rstd_ref[span, :], gain_ref[...])
        d_low = d_res.astype(BF16)
        dres_ref[span, :] = d_res
        dffn_ref[span, :] = d_low
        turned = d_low.T
        for block in range(held.shape[0]):
            held[block, :, span] = turned[block * depth : (block + 1) * depth, :]
        gain_sum = gain_sum + column_sum(d_out * normed)
        bias_sum = bias_sum + column_sum(d_low.astype(F32))
    sums_ref[0:1, :] = gain_sum
    sums_ref[1:2, :] = shift_sum
    sums_ref[2:3, :] = bias_sum
    sums_ref[3:8, :] = jnp.zeros((5, width), F32)
    part_blocks(me_ref[0] & 1, held, kept_ref, send_refs)


def feed_back_kernel(
    half,
    me_ref,
    own_ref,
    all_ref,
    place_ref,
    targ_ref,
    lab_ref,
    labcol_ref,
    norm_two_ref,
    rstd_two_ref,
    gain_two_ref,
    wout_ref,
    win_ref,
    slope_ref,
    norm_src,
    rstd_ref,
    gain_ref,
    wo_src,
    bsum_ref,
    done_ref,
    dattn_t_ref,
    dctx_ref,
    sums_ref,
    sums_two_ref,
    kept_out_ref,
    kept_ref,
    *refs,
):
    send_out, send_refs, refs = refs[:half], refs[half : 2 * half], refs[2 * half :]
    held_out, held, dffn_ref, total_ref, norm_ref, wo_ref, sems = refs
    count, depth, _ = held.shape
    step = pl.program_id(0)
    copies = [
        pltpu.make_async_copy(norm_src, norm_ref, sems.at[0]),
        pltpu.make_async_copy(wo_src, wo_ref, sems.at[1]),
    ]

    @pl.when(step == 0)
    def _():
        for copy in copies:
            copy.start()
        loss_back_body(
            me_ref,
            own_ref,
            all_ref,
            place_ref,
            targ_ref,
            lab_ref,
            labcol_ref,
            norm_two_ref,
            rstd_two_ref,
            gain_two_ref,
            total_ref,
            dffn_ref,
            sums_two_ref,
            kept_out_ref,
            send_out,
            held_out,
        )

    d_up = (dot(dffn_ref[...], wout_ref[...], NT) * slope_ref[...].astype(F32)).astype(BF16)
    turned = d_up.T
    for block in range(count):
        held[block] = turned[block * depth : (block + 1) * depth, :]
    for at in range(half // (count // 2)):

        @pl.when(step == at)
        def _():
            part_blocks(me_ref[0] & 1, held, kept_ref, send_refs, at * (count // 2))

    bsum_ref[...] = column_sum(d_up.astype(F32))
    total_ref[...] += dot(d_up, win_ref[...], NT)

    @pl.when(step == pl.num_programs(0) - 1)
    def _():
        for copy in copies:
            copy.wait()
        tok_count, width = total_ref.shape
        kept_rows = tok_count // LANES
        gain_sum = jnp.zeros((1, width), F32)
        shift_sum = jnp.zeros((1, width), F32)
        bias_sum = jnp.zeros((1, width), F32)
        for row in range(kept_rows):
            span = slice(row * LANES, (row + 1) * LANES)
            d_hidden = total_ref[span, :]
            normed = norm_ref[span, :]
            d_res = norm_back(d_hidden, normed, rstd_ref[span, :], gain_ref[...])
            d_low = d_res.astype(BF16)
            done_ref[span, :] = d_res
            dattn_t_ref[:, span] = d_low.T
            dctx_ref[span, :] = dot(d_low, wo_ref[...], NT).astype(BF16)
            gain_sum = gain_sum + column_sum(d_hidden * normed)
            shift_sum = shift_sum + column_sum(d_hidden)
            bias_sum = bias_sum + column_sum(d_low.astype(F32))
        sums_ref[0:1, :] = gain_sum
        sums_ref[1:2, :] = shift_sum
        sums_ref[2:3, :] = bias_sum
        sums_ref[3:8, :] = jnp.zeros((5, width), F32)


def feed_back(
    me,
    own,
    pooled_all,
    place,
    target,
    labels,
    label_cols,
    normed_two,
    rstd_two,
    gain_two,
    w_out,
    w_in,
    slope,
    normed,
    rstd,
    gain,
    w_o,
    wide_count,
):
    tok_count, width = normed.shape
    units = w_in.shape[1]
    tile = 768
    depth = units // wide_count
    depth_out = width // wide_count
    half = wide_count // 2
    count = tile // depth
    whole = lambda step: (0, 0)
    fixed = lambda array: pl.BlockSpec(array.shape, whole)
    hbm = pl.BlockSpec(memory_space=pl.ANY)
    shapes = (
        (
            ((1, units), F32),
            ((tok_count, width), F32),
            ((width, tok_count), BF16),
            ((tok_count, width), BF16),
            ((8, width), F32),
            ((8, width), F32),
            ((half, depth_out, tok_count), BF16),
            ((half, depth, tok_count), BF16),
        )
        + (((depth_out, tok_count), BF16, hbm_shape),) * half
        + (((depth, tok_count), BF16, hbm_shape),) * half
    )
    return pl.pallas_call(
        functools.partial(feed_back_kernel, half),
        out_shape=[make_shape(*item) for item in shapes],
        grid_spec=pltpu.PrefetchScalarGridSpec(
            num_scalar_prefetch=0,
            grid=(units // tile,),
            in_specs=[
                smem_spec(),
                fixed(own),
                fixed(pooled_all),
                fixed(place),
                fixed(target),
                fixed(labels),
                fixed(label_cols),
                fixed(normed_two),
                fixed(rstd_two),
                fixed(gain_two),
                pl.BlockSpec((tile, width), lambda step: (step, 0)),
                pl.BlockSpec((width, tile), lambda step: (0, step)),
                pl.BlockSpec((tok_count, tile), lambda step: (0, step)),
                hbm,
                fixed(rstd),
                fixed(gain),
                hbm,
            ],
            out_specs=[
                pl.BlockSpec((1, tile), lambda step: (0, step)),
                pl.BlockSpec((tok_count, width), whole),
                pl.BlockSpec((width, tok_count), whole),
                pl.BlockSpec((tok_count, width), whole),
                pl.BlockSpec((8, width), whole),
                pl.BlockSpec((8, width), whole),
                pl.BlockSpec((half, depth_out, tok_count), lambda step: (0, 0, 0)),
                pl.BlockSpec((count // 2, depth, tok_count), lambda step: (step, 0, 0)),
            ]
            + [pl.BlockSpec((depth_out, tok_count), whole)] * half
            + [pl.BlockSpec((depth, tok_count), whole)] * half,
            scratch_shapes=[
                pltpu.VMEM((wide_count, depth_out, tok_count), BF16),
                pltpu.VMEM((count, depth, tok_count), BF16),
                pltpu.VMEM((tok_count, width), BF16),
                pltpu.VMEM((tok_count, width), F32),
                pltpu.VMEM((tok_count, width), F32),
                pltpu.VMEM(w_o.shape, BF16),
                pltpu.SemaphoreType.DMA((2,)),
            ],
        ),
        cost_estimate=cost(14),
        compiler_params=params(1),
        name="feed_back",
    )(
        me,
        own,
        pooled_all,
        place,
        target,
        labels,
        label_cols,
        normed_two,
        rstd_two,
        gain_two,
        w_out,
        w_in,
        slope,
        normed,
        rstd,
        gain,
        w_o,
    )


def attend_back_kernel(
    source_ref,
    me_ref,
    proj_ref,
    probs_ref,
    dctx_ref,
    done_ref,
    wqkv_ref,
    dattn_t_ref,
    dtok_ref,
    sums_ref,
    kept_ref,
    *refs,
):
    send_refs, held, dproj_ref = refs[:-2], refs[-2], refs[-1]
    row = pl.program_id(0)
    row_len, width = dctx_ref.shape
    blocks = held.shape[0]
    main = 3 * width // blocks
    scale = 1.0 / math.sqrt(HEAD_DIM)
    lane = lax.broadcasted_iota(jnp.int32, (row_len, LANES), 1)
    left = (lane < HEAD_DIM).astype(BF16)
    right = (lane >= HEAD_DIM).astype(BF16)

    def twice(values):
        return jnp.concatenate([values * left, values * right], axis=0)

    for pair in range(width // LANES):
        col = pair * LANES
        queries = proj_ref[:, col : col + LANES]
        key_rows = proj_ref[:, width + col : width + col + LANES]
        values = proj_ref[:, 2 * width + col : 2 * width + col + LANES]
        probs = probs_ref[0, pair]
        d_ctx = twice(dctx_ref[:, col : col + LANES])
        d_probs = dot(d_ctx, values, NT)
        probs_f = probs.astype(F32)
        inner = jnp.sum(probs_f * d_probs, axis=-1, keepdims=True)
        d_scores = (probs_f * (d_probs - inner)).astype(BF16)
        wide_scores = jnp.concatenate([d_scores[:row_len], d_scores[row_len:]], axis=1)
        d_query = dot(wide_scores, twice(key_rows)) * scale
        d_key = dot(d_scores, twice(queries), TN) * scale
        d_value = dot(probs, d_ctx, TN)
        for part, grad in ((0, d_query), (1, d_key), (2, d_value)):
            low = grad.astype(BF16)
            place = part * width + col
            dproj_ref[:, place : place + LANES] = low
            turned = low.T
            start = place
            while start < place + LANES:
                block, offset = divmod(start, main)
                stop = min(place + LANES, (block + 1) * main)
                held[block, offset : offset + stop - start, :] = turned[
                    start - place : stop - place, :
                ]
                start = stop
            before = jnp.where(row == 0, 0.0, sums_ref[:, place : place + LANES])
            sums_ref[:, place : place + LANES] = before + column_sum(low.astype(F32))

    rest = width // blocks
    for block in range(blocks):
        held[block, main:, :] = dattn_t_ref[block * rest : (block + 1) * rest, :]
    part_blocks(me_ref[0] & 1, held, kept_ref, send_refs)
    grad = done_ref[...] + dot(dproj_ref[...], wqkv_ref[...], NT)
    dtok_ref[0] = grad.astype(BF16)


def attend_back(sources, me, proj, probs, d_ctx, d_one, w_qkv, d_attn_t, wide_count):
    tok_count, width = d_ctx.shape
    kept_rows = tok_count // LANES
    half = wide_count // 2
    depth = 4 * width // wide_count
    shapes = (
        ((wide_count, LANES, width), BF16),
        ((1, 3 * width), F32),
        ((half, depth, tok_count), BF16),
    ) + (((depth, tok_count), BF16, hbm_shape),) * half
    return pl.pallas_call(
        attend_back_kernel,
        out_shape=[make_shape(*item) for item in shapes],
        grid_spec=pltpu.PrefetchScalarGridSpec(
            num_scalar_prefetch=2,
            grid=(kept_rows,),
            in_specs=[
                pl.BlockSpec((LANES, 3 * width), lambda row, src, me: (row, 0)),
                pl.BlockSpec((1,) + probs.shape[1:], lambda row, src, me: (row, 0, 0, 0)),
                pl.BlockSpec((LANES, width), lambda row, src, me: (row, 0)),
                pl.BlockSpec((LANES, width), lambda row, src, me: (row, 0)),
                pl.BlockSpec((width, 3 * width), lambda row, src, me: (0, 0)),
                pl.BlockSpec((width, LANES), lambda row, src, me: (0, row)),
            ],
            out_specs=[
                pl.BlockSpec((1, LANES, width), lambda row, src, me: (src[row], 0, 0)),
                pl.BlockSpec((1, 3 * width), lambda row, src, me: (0, 0)),
                pl.BlockSpec((half, depth, LANES), lambda row, src, me: (0, 0, row)),
            ]
            + [pl.BlockSpec((depth, LANES), lambda row, src, me: (0, row))] * half,
            scratch_shapes=[
                pltpu.VMEM((wide_count, depth, LANES), BF16),
                pltpu.VMEM((LANES, 3 * width), BF16),
            ],
        ),
        cost_estimate=cost(20),
        compiler_params=params(1),
        name="attend_back",
    )(sources, me, proj, probs, d_ctx, d_one, w_qkv, d_attn_t)


def home_kernel(dest_ref, rows_ref, out_ref, sems):
    slot_dev = out_ref.shape[0]

    def copy(slot):
        return pltpu.make_async_copy(
            rows_ref.at[jnp.maximum(dest_ref[slot], 0)], out_ref.at[slot], sems.at[slot]
        )

    for slot in range(slot_dev):
        copy(slot).start()
    for slot in range(slot_dev):
        copy(slot).wait()

        @pl.when(dest_ref[slot] < 0)
        def _():
            out_ref[slot] = jnp.zeros(out_ref.shape[1:], out_ref.dtype)


def home_rows(destination, rows):
    count = destination.shape[0]
    return pl.pallas_call(
        home_kernel,
        out_shape=jax.ShapeDtypeStruct((count,) + rows.shape[1:], rows.dtype),
        in_specs=[smem_spec(), pl.BlockSpec(memory_space=pl.ANY)],
        out_specs=vmem_spec(),
        scratch_shapes=[pltpu.SemaphoreType.DMA((count,))],
        cost_estimate=cost(3),
        compiler_params=params(),
        name="home_rows",
    )(destination, rows)


def block_at(index, bit, value):
    low = index & ((1 << bit) - 1)
    return ((index >> bit) << (bit + 1)) | (value << bit) | low


def grad_kernel(first_bit, second_bit, spans, blocks, me_ref, own_ref, *refs):
    recv_refs, refs = refs[:blocks], refs[blocks:]
    step = pl.program_id(0)
    half_steps = pl.num_programs(0) // 2
    terms = len(spans)
    own_xs, recv_xs = refs[:terms], refs[terms : 2 * terms]
    outs = refs[2 * terms : 2 * terms + 4]
    own_lefts = refs[2 * terms + 4 : 3 * terms + 4]
    recv_lefts = refs[3 * terms + 4 :]
    me = me_ref[0]
    for half, bit in ((0, first_bit), (1, second_bit)):

        @pl.when(step == half * half_steps)
        def _():
            side = (me >> bit) & 1
            for block in range(blocks):
                low = block & ((1 << (bit - 1)) - 1)
                rest = ((block >> bit) << (bit - 1)) | low
                kept = ((block >> (bit - 1)) & 1) == side
                index = jnp.where(kept, rest, rest + blocks // 2)
                for (start, stop), own_left, recv_left in zip(spans, own_lefts, recv_lefts):
                    own_left[index] = own_ref[block, start:stop, :]
                    recv_left[index] = recv_refs[block][start:stop, :]

    for term, (start, stop) in enumerate(spans):
        rows = stop - start
        chunk = blocks if blocks * rows <= 384 else blocks // 2
        for base in range(0, blocks, chunk):
            span = slice(base, base + chunk)
            flat = lambda left: left[span].reshape(chunk * rows, left.shape[2])
            part = dot(flat(own_lefts[term]), own_xs[term][...])
            part = part + dot(flat(recv_lefts[term]), recv_xs[term][...])
            part = part.astype(BF16).reshape(chunk, rows, part.shape[1])
            for index in range(chunk):
                block = base + index
                role, place = divmod(block, blocks // 2)
                for half in range(2):

                    @pl.when((step < half_steps) == (half == 0))
                    def _():
                        outs[2 * half + role][place, start:stop, :] = part[index]


def grad_terms(me, own, received, own_xs, recv_xs, spans, first_bit, second_bit, tile):
    blocks = len(received)
    rows, tok_count = received[0].shape
    columns = own_xs[0][0].shape[-1]
    steps = columns // tile
    half = steps // 2

    def x_spec(item):
        array, lead = item
        if lead is None:
            return pl.BlockSpec((tok_count, tile), lambda step: (0, step))
        return pl.BlockSpec((pl.Squeezed(), tok_count, tile), lambda step: (lead, 0, step))

    out_block = (blocks // 2, rows, tile)
    first_spec = pl.BlockSpec(out_block, lambda step: (0, 0, jnp.minimum(step, half - 1)))
    second_spec = pl.BlockSpec(out_block, lambda step: (0, 0, jnp.maximum(step - half, 0)))
    shape = hbm_shape((blocks // 2, rows, columns // 2), BF16)
    whole = lambda step: (0, 0, 0)
    lefts = [pltpu.VMEM((blocks, stop - start, tok_count), BF16) for start, stop in spans]
    return pl.pallas_call(
        functools.partial(grad_kernel, first_bit, second_bit, spans, blocks),
        out_shape=[shape] * 4,
        grid_spec=pltpu.PrefetchScalarGridSpec(
            num_scalar_prefetch=0,
            grid=(steps,),
            in_specs=[
                smem_spec(),
                pl.BlockSpec(own.shape, whole),
            ]
            + [pl.BlockSpec((rows, tok_count), lambda step: (0, 0))] * blocks
            + [x_spec(item) for item in own_xs + recv_xs],
            out_specs=[first_spec, first_spec, second_spec, second_spec],
            scratch_shapes=lefts + lefts,
        ),
        cost_estimate=cost(7),
        compiler_params=params(1),
        name="grad_terms",
    )(me, own, *received, *[item[0] for item in own_xs + recv_xs])


def fold_kernel(bits, places, me_ref, *refs):
    me = me_ref[0]
    for half in range(2):
        kept_ref, recv_ref = refs[2 * half], refs[2 * half + 1]
        keep_out, send_out = refs[4 + 2 * half], refs[5 + 2 * half]
        side = (me >> bits[half]) & 1
        for index in range(keep_out.shape[0]):
            for value, out_ref in ((1 - side, send_out), (side, keep_out)):
                block = block_at(index, places[half], value)
                out_ref[index] = add_low(kept_ref[block], recv_ref[block])


def fold(me, halves, bits, places):
    shapes = []
    for kept, _ in halves:
        shapes += [hbm_shape((kept.shape[0] // 2,) + kept.shape[1:], BF16)] * 2
    return pl.pallas_call(
        functools.partial(fold_kernel, bits, places),
        out_shape=shapes,
        in_specs=[smem_spec()] + [vmem_spec()] * 4,
        out_specs=[vmem_spec()] * 4,
        cost_estimate=cost(0.5),
        compiler_params=params(),
        name="fold",
    )(me, *halves[0], *halves[1])


def piece_kernel(turned, stacked, me_ref, *refs):
    outs, held = (refs[4:], refs[4]) if stacked else (refs[4:-1], refs[-1])
    count = held.shape[0]
    depth = held.shape[1] if turned else held.shape[2]
    for half in range(2):
        total = add_low(refs[2 * half][0], refs[2 * half + 1][0])
        if turned:
            total = total.T
        for index in range(count // 2):
            span = slice(index * depth, (index + 1) * depth)
            held[half * (count // 2) + index] = total[span, :] if turned else total[:, span]
    if not stacked:
        for step in range(count):
            outs[step][...] = held[me_ref[0] ^ step]


def narrow_pieces(me, halves, narrow_count, turned, stacked):
    _, rows, columns = halves[0][0].shape
    depth = 2 * columns // narrow_count
    shape = (depth, rows) if turned else (rows, depth)
    whole = (narrow_count,) + shape
    outs = [hbm_shape(whole, BF16)] if stacked else [hbm_shape(shape, BF16)] * narrow_count
    return pl.pallas_call(
        functools.partial(piece_kernel, turned, stacked),
        out_shape=outs,
        in_specs=[smem_spec()] + [vmem_spec()] * 4,
        out_specs=[vmem_spec()] * len(outs),
        scratch_shapes=[] if stacked else [pltpu.VMEM(whole, BF16)],
        cost_estimate=cost(1),
        compiler_params=params(),
        name="narrow_pieces",
    )(me, *halves[0], *halves[1])


def sum_kernel(count, *refs):
    terms = [ref[...] for ref in refs[:count]]
    if len(terms[0].shape) == 3:
        terms = [terms[0][place] for place in range(terms[0].shape[0])]
    total = terms[0].astype(F32)
    for term in terms[1:]:
        total = total + term.astype(F32)
    start = 0
    for out_ref in refs[count:]:
        out_ref[...] = total[:, start : start + out_ref.shape[1]]
        start += out_ref.shape[1]


def sum_pieces(pieces, cuts=None):
    shape = pieces[0].shape[-2:]
    outs = [jax.ShapeDtypeStruct((shape[0], cut), F32) for cut in cuts or (shape[1],)]
    return pl.pallas_call(
        functools.partial(sum_kernel, len(pieces)),
        out_shape=outs,
        in_specs=[vmem_spec()] * len(pieces),
        out_specs=[vmem_spec()] * len(outs),
        cost_estimate=cost(1),
        compiler_params=params(),
        name="sum_pieces",
    )(*pieces)


def pack_kernel(cuts, *refs):
    out_ref = refs[-1]
    place = 0
    for index, row, start, stop in cuts:
        for at in range(start, stop, LANES):
            out_ref[place : place + 1, :] = refs[index][row : row + 1, at : at + LANES]
            place += 1


def pack_vectors(arrays, cuts):
    lines = sum(stop - start for _, _, start, stop in cuts) // LANES
    return pl.pallas_call(
        functools.partial(pack_kernel, cuts),
        out_shape=jax.ShapeDtypeStruct((lines, LANES), F32),
        in_specs=[vmem_spec()] * len(arrays),
        out_specs=vmem_spec(),
        cost_estimate=cost(0.5),
        compiler_params=params(),
        name="pack_vectors",
    )(*arrays)


def swap(values, axis, bit):
    count = lax.axis_size(axis)
    return lax.ppermute(values, axis, [(i, i ^ (1 << bit)) for i in range(count)])


def trade(pieces):
    count = len(pieces)
    got = [pieces[0]]
    for step in range(1, count):
        got.append(lax.ppermute(pieces[step], "narrow", [(i, i ^ step) for i in range(count)]))
    return got


def pick(values, dim, index):
    return lax.dynamic_index_in_dim(values, index, dim, keepdims=False)


def add_low(kept, received):
    return (kept.astype(F32) + received.astype(F32)).astype(BF16)


def after(value, *others):
    return lax.optimization_barrier((value,) + others)[0]


def to_partner(blocks):
    return [swap(block, "wide", 0) for block in blocks]


class Folding:
    def __init__(self, me, outs, orders, *gates):
        self.me = me
        self.orders = orders
        self.left = [sorted(order) for order in orders]
        self.kept = [outs[0], outs[2]]
        self.sent = [outs[1], outs[3]]
        self.level = 0
        self.exchange(*gates)

    def exchange(self, *gates):
        self.received = [
            swap(after(self.sent[half], *gates), "wide", self.orders[half][self.level])
            for half in range(2)
        ]
        for half in range(2):
            self.left[half].remove(self.orders[half][self.level])
        self.level += 1

    def halves(self):
        return [(self.kept[half], self.received[half]) for half in range(2)]

    def step(self, *gates):
        bits = [order[self.level] for order in self.orders]
        places = [left.index(bit) for left, bit in zip(self.left, bits)]
        outs = fold(self.me, self.halves(), bits, places)
        self.kept = [outs[0], outs[2]]
        self.sent = [outs[1], outs[3]]
        self.exchange(*gates)

    def gate(self, *others):
        self.kept[0] = after(self.kept[0], *others)

    def finish(self, me_narrow, narrow_count, turned, stacked=False):
        while self.level < len(self.orders[0]):
            self.step()
        return narrow_pieces(me_narrow, self.halves(), narrow_count, turned, stacked)


def hop(values, axis, bit):
    return values + swap(values, axis, bit)


def on_device(
    tokens,
    segments,
    destination,
    pair_index,
    targets,
    w_qkv,
    b_qv,
    w_o,
    b_o,
    gain_one,
    shift_one,
    w_in,
    b_in,
    w_out,
    b_out,
    gain_two,
    shift_two,
):
    wide_count = lax.axis_size("wide")
    narrow_count = lax.axis_size("narrow")
    slot_dev, row_len, width = tokens.shape
    kept_rows = slot_dev // 2
    units = w_in.shape[1]
    me = lax.axis_index("wide")
    me_line = me.astype(jnp.int32).reshape(1)
    me_narrow = lax.axis_index("narrow").astype(jnp.int32).reshape(1)
    line = lambda vector: vector.reshape(1, -1)

    sent = build_send(tokens, segments, destination, pair_index, targets, wide_count)
    got = lax.all_to_all(sent, "wide", split_axis=0, concat_axis=0, tiled=True)
    full_bias = jnp.concatenate(
        [b_qv[:width], jnp.zeros((width,), F32), b_qv[width:]]
    ).reshape(1, 3 * width)
    stack, proj, probs, hidden, norm_one, rstd_one, labels, label_cols, meta, sources = (
        attend_forward(
            got, w_qkv, full_bias, w_o, line(b_o), line(gain_one), line(shift_one), kept_rows
        )
    )
    stack_recv = swap(stack, "wide", 0)
    act, slope, encoded, norm_two, rstd_two, pooled, pooled_copies = feed_forward(
        stack,
        hidden,
        w_in,
        line(b_in),
        w_out,
        line(b_out),
        line(gain_two),
        line(shift_two),
        labels,
        wide_count,
    )
    act_recv = swap(act, "wide", 0)
    place, target, first, second = route(me_line, meta, pair_index, kept_rows)
    pooled_all = lax.all_to_all(
        pooled_copies, "wide", split_axis=0, concat_axis=0, tiled=True
    ).reshape(wide_count * kept_rows * SEG_ROW, width)
    similarity = cosine_pairs(first, second, pooled_all).reshape(-1)
    bits = wide_count.bit_length() - 1
    middle = 1 + (bits - 1) // 2
    low_first = list(range(1, bits))
    high_first = list(range(middle, bits)) + list(range(1, middle))
    orders = (low_first, high_first)
    first_bits = (low_first[0], high_first[0])
    half = wide_count // 2
    sum_b_in, d_one, d_attn_t, d_ctx, sums_one, sums_two, own_out, own_in, *sends = feed_back(
        me_line,
        pooled,
        pooled_all,
        place,
        target,
        labels,
        label_cols,
        norm_two,
        rstd_two,
        line(gain_two),
        w_out,
        w_in,
        slope,
        norm_one,
        rstd_one,
        line(gain_one),
        w_o,
        wide_count,
    )
    rows_out = own_out.shape[1]
    rows_in = own_in.shape[1]
    recv_out = to_partner(sends[:half])
    recv_in = to_partner(sends[half:])
    fold_out = Folding(
        me_line,
        grad_terms(
            me_line,
            own_out,
            recv_out,
            [(act, None)],
            [(act_recv, None)],
            ((0, rows_out),),
            *first_bits,
            512,
        ),
        orders,
    )
    outs_in = grad_terms(
        me_line,
        own_in,
        after(tuple(recv_in), *fold_out.sent),
        [(stack, 2)],
        [(stack_recv, 2)],
        ((0, rows_in),),
        *first_bits,
        width // 2,
    )
    fold_out.gate(similarity, *outs_in)
    fold_out.step()
    fold_in = Folding(me_line, outs_in, orders, *fold_out.sent)
    d_rows, sums_qkv, own_mix, *send_mix = attend_back(
        sources,
        me_line,
        proj,
        probs,
        after(d_ctx, *fold_out.sent, *fold_in.sent),
        d_one,
        w_qkv,
        d_attn_t,
        wide_count,
    )
    recv_mix = to_partner(send_mix)
    vectors = pack_vectors(
        (sums_qkv, sums_one, sum_b_in, sums_two),
        (
            (0, 0, 0, width),
            (0, 0, 2 * width, 3 * width),
            (1, 2, 0, width),
            (1, 0, 0, width),
            (1, 1, 0, width),
            (2, 0, 0, units),
            (3, 2, 0, width),
            (3, 0, 0, width),
            (3, 1, 0, width),
        ),
    )
    fold_in.gate(d_rows, *fold_out.received)
    fold_in.step()
    fold_out.gate(d_rows)
    pieces_out = fold_out.finish(me_narrow, narrow_count, False)
    traded_out = trade(pieces_out)
    home = lax.all_to_all(
        after(d_rows, *fold_in.sent), "wide", split_axis=0, concat_axis=0, tiled=True
    )
    cols_qkv = 3 * width // wide_count
    rows_mix = own_mix.shape[1]
    (grad_w_out,) = sum_pieces(traded_out)
    grad_w_out = grad_w_out.T
    outs_mix = grad_terms(
        me_line,
        own_mix,
        after(tuple(recv_mix), tuple(pieces_out), *fold_in.sent),
        [(stack, 0), (stack, 1)],
        [(stack_recv, 0), (stack_recv, 1)],
        ((0, cols_qkv), (cols_qkv, rows_mix)),
        *first_bits,
        width // 2,
    )
    vectors = hop(vectors, "wide", 0)
    vectors = hop(vectors, "narrow", 0)
    fold_mix = Folding(
        me_line,
        outs_mix,
        orders,
        vectors,
        tuple(traded_out),
        *fold_in.received,
    )
    grad_tokens = home_rows(destination, home)
    pieces_in = fold_in.finish(me_narrow, narrow_count, True)
    traded_in = trade(pieces_in)
    fold_mix.gate(grad_tokens, tuple(traded_in))
    fold_mix.step()
    vectors = after(vectors, *fold_mix.sent)
    for bit in range(1, narrow_count.bit_length() - 1):
        vectors = hop(vectors, "narrow", bit)
    (grad_w_in,) = sum_pieces(traded_in)
    fold_mix.gate(vectors)
    (pieces_mix,) = fold_mix.finish(me_narrow, narrow_count, True, True)
    traded_mix = lax.all_to_all(pieces_mix, "narrow", split_axis=0, concat_axis=0, tiled=True)
    vectors = after(vectors, pieces_mix)
    for bit in range(1, bits):
        vectors = hop(vectors, "wide", bit)
    grad_w_qkv, grad_w_o = sum_pieces(
        (after(traded_mix, vectors),), (cols_qkv, rows_mix - cols_qkv)
    )
    vectors = vectors.reshape(-1)
    cuts = (2 * width, width, width, width, units, width, width, width)
    outs = []
    start = 0
    for size in cuts:
        outs.append(vectors[start : start + size])
        start += size
    grad_b_qv, grad_b_o, grad_gain_one, grad_shift_one = outs[:4]
    grad_b_in, grad_b_out, grad_gain_two, grad_shift_two = outs[4:]
    return (
        encoded.reshape(kept_rows, row_len, width),
        similarity,
        grad_tokens,
        grad_w_qkv,
        grad_b_qv,
        grad_w_o,
        grad_b_o,
        grad_gain_one,
        grad_shift_one,
        grad_w_in,
        grad_b_in,
        grad_w_out,
        grad_b_out,
        grad_gain_two,
        grad_shift_two,
    )


def solution(mesh):
    rows = ("wide", "narrow")
    in_specs = (P(rows, None, None), P(rows, None), P(rows), P(rows, None), P(rows)) + (P(),) * 12
    matrix = P("narrow", "wide")
    out_specs = (
        P(rows, None, None),
        P(rows),
        P(rows, None, None),
        matrix,
        P(),
        matrix,
        P(),
        P(),
        P(),
        matrix,
        P(),
        matrix,
        P(),
        P(),
        P(),
    )
    return jax.shard_map(
        on_device, mesh=mesh, in_specs=in_specs, out_specs=out_specs, check_vma=False
    )
```

```python
import functools
import math

import jax
import jax.numpy as jnp
from jax import lax
from jax.experimental import pallas as pl
from jax.experimental.pallas import tpu as pltpu
from jax.sharding import PartitionSpec as P

HEAD_DIM = 64
SEG_ROW = 8
LANES = 128
META_ROWS = 16
NEG_FILL = -1e30
NORM_EPS = 1e-12
COS_EPS = 1e-06
F32 = jnp.float32
BF16 = jnp.bfloat16
VMEM_LIMIT = 67043328


def cost(micros):
    return pl.CostEstimate(flops=0, bytes_accessed=int(micros * 3.0e6), transcendentals=0)


NT = (((1,), (1,)), ((), ()))
TN = (((0,), (0,)), ((), ()))


def vmem_spec():
    return pl.BlockSpec(memory_space=pltpu.VMEM)


def hbm_shape(shape, dtype):
    return pltpu.HBM(shape, dtype)


def make_shape(shape, dtype, make=jax.ShapeDtypeStruct):
    return make(shape, dtype)


def params(steps=0):
    return pltpu.CompilerParams(
        dimension_semantics=("arbitrary",) * steps if steps else None,
        vmem_limit_bytes=VMEM_LIMIT,
    )


def split_three(values):
    high = values.astype(BF16)
    rest = values - high.astype(F32)
    middle = rest.astype(BF16)
    low = (rest - middle.astype(F32)).astype(BF16)
    return (high, middle, low)


def dot(left, right, dims=None):
    if dims is None:
        return jnp.dot(left, right, preferred_element_type=F32)
    return lax.dot_general(left, right, dims, preferred_element_type=F32)


def column_sum(values):
    return jnp.sum(values, axis=0, keepdims=True)


def row_mean(values):
    return jnp.mean(values, axis=-1, keepdims=True)


def prep_kernel(dest_ref, pair_ref, targ_ref, tok_ref, seg_ref, out_ref, sems):
    slot_dev = dest_ref.shape[0]
    wide_count, _, width = out_ref.shape
    row_len = tok_ref.shape[1]
    sources = []
    lives = []
    copies = []
    for owner in range(wide_count):
        found = jnp.int32(0)
        live = dest_ref[0] == owner
        for slot in range(1, slot_dev):
            match = dest_ref[slot] == owner
            found = jnp.where(match, slot, found)
            live = live | match
        sources.append(found)
        lives.append(live)
        copy = pltpu.make_async_copy(
            tok_ref.at[found], out_ref.at[owner, pl.ds(0, row_len), :], sems.at[owner]
        )
        copy.start()
        copies.append(copy)
    lane = lax.broadcasted_iota(jnp.int32, (1, LANES), 1)
    dest = jnp.full((1, LANES), -1, jnp.int32)
    for slot in range(slot_dev):
        dest = jnp.where(lane // SEG_ROW == slot, dest_ref[slot], dest)
    partner = jnp.zeros((1, LANES), jnp.int32)
    target = jnp.zeros((1, LANES), F32)
    for pair in range(pair_ref.shape[1]):
        first = pair_ref[0, pair]
        second = pair_ref[1, pair]
        at_first = lane == first
        at_second = lane == second
        partner = jnp.where(at_first, second, jnp.where(at_second, first, partner))
        target = jnp.where(at_first | at_second, targ_ref[0, pair], target)
    high, middle, low = split_three(target)
    fixed = [dest.astype(F32), partner.astype(F32)]
    fixed += [high.astype(F32), middle.astype(F32), low.astype(F32)]
    fixed.append(jnp.zeros((META_ROWS - 1 - len(fixed), LANES), F32))
    for owner in range(wide_count):
        labels = seg_ref[pl.ds(sources[owner], 1), :].astype(F32)
        labels = jnp.where(lives[owner], labels, -1.0)
        table = jnp.concatenate([labels] + fixed, axis=0)
        out_ref[owner, row_len:, :LANES] = table.astype(BF16)
        out_ref[owner, row_len:, LANES:] = jnp.zeros((META_ROWS, width - LANES), BF16)
    for copy in copies:
        copy.wait()


def smem_spec():
    return pl.BlockSpec(memory_space=pltpu.SMEM)


def build_send(tokens, segments, destination, pair_index, targets, wide_count):
    slot_dev, row_len, width = tokens.shape
    return pl.pallas_call(
        prep_kernel,
        out_shape=jax.ShapeDtypeStruct((wide_count, row_len + META_ROWS, width), BF16),
        in_specs=[smem_spec()] * 3 + [pl.BlockSpec(memory_space=pl.ANY), vmem_spec()],
        out_specs=vmem_spec(),
        scratch_shapes=[pltpu.SemaphoreType.DMA((wide_count,))],
        cost_estimate=cost(3),
        compiler_params=params(),
        name="build_send",
    )(destination, pair_index.T, targets.reshape(1, -1), tokens, segments)


def attend_body(
    got_ref,
    wqkv_src,
    bias_ref,
    wo_src,
    bo_ref,
    gain_ref,
    shift_ref,
    rstd_ref,
    lab_ref,
    labcol_ref,
    meta_ref,
    source_ref,
    stack_ref,
    proj_ref,
    probs_ref,
    norm_ref,
    hid_ref,
    wqkv_ref,
    wo_ref,
    sems,
):
    x_ref, ctx_ref, low_ref = stack_ref.at[0], stack_ref.at[1], stack_ref.at[2]
    wide_count = got_ref.shape[0]
    tok_count, width = hid_ref.shape
    row_len = got_ref.shape[1] - META_ROWS
    kept_rows = tok_count // row_len
    total_cols = proj_ref.shape[1]
    parts = total_cols // width
    get_meta = pltpu.make_async_copy(
        got_ref.at[:, pl.ds(row_len, META_ROWS), pl.ds(0, LANES)], meta_ref, sems.at[0]
    )
    get_meta.start()
    get_weights = []
    for part in range(parts):
        span = pl.ds(part * width, width)
        get_weights.append(
            pltpu.make_async_copy(
                wqkv_src.at[:, span], wqkv_ref.at[:, span], sems.at[1 + part]
            )
        )
    get_wo = pltpu.make_async_copy(wo_src, wo_ref, sems.at[1 + parts])
    get_weights[0].start()
    get_meta.wait()
    seen = jnp.int32(0)
    sources = [jnp.int32(0)] * kept_rows
    for slot in range(wide_count):
        live = jnp.max(meta_ref[slot, 0:1, :].astype(F32)) >= 0.0
        for row in range(kept_rows):
            sources[row] = jnp.where(live & (seen == row), slot, sources[row])
        seen = seen + live.astype(jnp.int32)
    get_rows = []
    for row in range(kept_rows):
        source_ref[row] = sources[row]
        span = pl.ds(row * row_len, row_len)
        get_rows.append(
            pltpu.make_async_copy(
                got_ref.at[sources[row], pl.ds(0, row_len), :],
                x_ref.at[span, :],
                sems.at[2 + parts + row],
            )
        )
        get_rows[row].start()
    for copy in get_weights[1:] + [get_wo]:
        copy.start()
    for row in range(kept_rows):
        span = pl.ds(row * row_len, row_len)
        tag = meta_ref[sources[row], 0:1, :].astype(F32)
        lab_ref[row : row + 1, :] = tag
        labcol_ref[span, :] = jnp.broadcast_to(tag, (LANES, LANES)).T
    for copy in get_rows:
        copy.wait()
    tile = 256
    for start in range(0, total_cols, tile):
        if start % width == 0:
            get_weights[start // width].wait()
        cols = slice(start, start + tile)
        proj_ref[:, cols] = (dot(x_ref[...], wqkv_ref[:, cols]) + bias_ref[:, cols]).astype(BF16)

    scale = 1.0 / math.sqrt(HEAD_DIM)
    lane = lax.broadcasted_iota(jnp.int32, (row_len, LANES), 1)
    left = (lane < HEAD_DIM).astype(BF16)
    right = (lane >= HEAD_DIM).astype(BF16)

    def attend_row(row, carry):
        span = pl.ds(pl.multiple_of(row * row_len, row_len), row_len)
        same = labcol_ref[span, :] == lab_ref[pl.ds(row, 1), :]
        same = jnp.concatenate([same, same], axis=0)
        for pair in range(width // LANES):
            col = pair * LANES
            queries = proj_ref[span, col : col + LANES]
            key_rows = proj_ref[span, width + col : width + col + LANES]
            values = proj_ref[span, 2 * width + col : 2 * width + col + LANES]
            both = jnp.concatenate([queries * left, queries * right], axis=0)
            scores = jnp.where(same, dot(both, key_rows, NT) * scale, NEG_FILL)
            top = jnp.max(scores, axis=-1, keepdims=True)
            expo = jnp.exp(scores - top)
            total = jnp.sum(expo, axis=-1, keepdims=True)
            probs = (expo / total).astype(BF16)
            probs_ref[row, pair] = probs
            wide_probs = jnp.concatenate([probs[:row_len], probs[row_len:]], axis=1)
            split_values = jnp.concatenate([values * left, values * right], axis=0)
            ctx_ref[span, col : col + LANES] = dot(wide_probs, split_values).astype(BF16)
        return carry

    lax.fori_loop(0, kept_rows, attend_row, 0)
    get_wo.wait()
    for row in range(kept_rows):
        span = pl.ds(row * row_len, row_len)
        total = x_ref[span, :].astype(F32) + dot(ctx_ref[span, :], wo_ref[...]) + bo_ref[...]
        centered = total - row_mean(total)
        rstd = lax.rsqrt(row_mean(centered * centered) + NORM_EPS)
        normed = centered * rstd
        hidden = normed * gain_ref[...] + shift_ref[...]
        norm_ref[span, :] = normed
        rstd_ref[span, :] = rstd
        hid_ref[span, :] = hidden
        low_ref[span, :] = hidden.astype(BF16)


def forward_kernel(
    got_ref,
    wqkv_src,
    bias_ref,
    wo_src,
    bo_ref,
    gain_ref,
    shift_ref,
    win_ref,
    bin_ref,
    wout_ref,
    bout_ref,
    gain_two_ref,
    shift_two_ref,
    stack_out,
    proj_out,
    probs_out,
    norm_out,
    rstd_ref,
    lab_ref,
    labcol_ref,
    meta_ref,
    source_ref,
    act_ref,
    slope_ref,
    enc_ref,
    norm_two_ref,
    rstd_two_ref,
    pooled_ref,
    copies_ref,
    stack_ref,
    proj_ref,
    probs_ref,
    norm_ref,
    hid_ref,
    total_ref,
    wqkv_ref,
    wo_ref,
    sems,
    out_sems,
):
    step = pl.program_id(0)
    puts = [
        pltpu.make_async_copy(held, out, out_sems.at[index])
        for index, (held, out) in enumerate(
            (
                (stack_ref, stack_out),
                (proj_ref, proj_out),
                (probs_ref, probs_out),
                (norm_ref, norm_out),
            )
        )
    ]

    @pl.when(step == 0)
    def _():
        attend_body(
            got_ref,
            wqkv_src,
            bias_ref,
            wo_src,
            bo_ref,
            gain_ref,
            shift_ref,
            rstd_ref,
            lab_ref,
            labcol_ref,
            meta_ref,
            source_ref,
            stack_ref,
            proj_ref,
            probs_ref,
            norm_ref,
            hid_ref,
            wqkv_ref,
            wo_ref,
            sems,
        )
        for put in puts:
            put.start()
        total_ref[...] = hid_ref[...] + bout_ref[...]

    up = dot(stack_ref[2], win_ref[...]) + bin_ref[...]
    phi = 0.5 * (1.0 + lax.erf(up * (1.0 / math.sqrt(2.0))))
    density = jnp.exp(-0.5 * up * up) * (1.0 / math.sqrt(2.0 * math.pi))
    act = (up * phi).astype(BF16)
    act_ref[...] = act
    slope_ref[...] = (phi + up * density).astype(BF16)
    total_ref[...] += dot(act, wout_ref[...])

    @pl.when(step == pl.num_programs(0) - 1)
    def _():
        tok_count, width = total_ref.shape
        kept_rows = tok_count // LANES
        for row in range(kept_rows):
            span = slice(row * LANES, (row + 1) * LANES)
            total = total_ref[span, :]
            centered = total - row_mean(total)
            rstd = lax.rsqrt(row_mean(centered * centered) + NORM_EPS)
            normed = centered * rstd
            out = normed * gain_two_ref[...] + shift_two_ref[...]
            norm_two_ref[span, :] = normed
            rstd_two_ref[span, :] = rstd
            enc_ref[span, :] = out.astype(BF16)
            segment = lax.broadcasted_iota(jnp.int32, (SEG_ROW, LANES), 0).astype(F32)
            onehot = (lab_ref[row : row + 1, :] == segment).astype(F32)
            count = jnp.sum(onehot, axis=1, keepdims=True)
            high, middle, low = split_three(out)
            mask = onehot.astype(BF16)
            summed = dot(mask, high) + dot(mask, middle) + dot(mask, low)
            pooled_ref[row * SEG_ROW : (row + 1) * SEG_ROW, :] = (summed / count).astype(BF16)
        for owner in range(copies_ref.shape[0]):
            copies_ref[owner] = pooled_ref[...]
        for put in puts:
            put.wait()


def forward(
    got,
    w_qkv,
    bias,
    w_o,
    b_o,
    gain,
    shift,
    w_in,
    b_in,
    w_out,
    b_out,
    gain_two,
    shift_two,
    kept_rows,
):
    wide_count, slot_len, width = got.shape
    row_len = slot_len - META_ROWS
    tok_count = kept_rows * row_len
    units = w_in.shape[1]
    tile = 768
    whole = lambda step: (0, 0)
    hbm = pl.BlockSpec(memory_space=pl.ANY)
    wide_vector = pl.BlockSpec((1, 3 * width), whole)
    vector = pl.BlockSpec((1, width), whole)
    stack = (3, tok_count, width)
    proj = (tok_count, 3 * width)
    probs = (kept_rows, width // LANES, 2 * row_len, row_len)
    flat = (tok_count, width)
    own = (kept_rows * SEG_ROW, width)
    shapes = (
        (stack, BF16, hbm_shape),
        (proj, BF16, hbm_shape),
        (probs, BF16, hbm_shape),
        (flat, F32, hbm_shape),
        ((tok_count, 1), F32),
        ((8, LANES), F32),
        ((tok_count, LANES), F32),
        ((wide_count, META_ROWS, LANES), BF16),
        ((kept_rows,), jnp.int32),
        ((tok_count, units), BF16),
        ((tok_count, units), BF16),
        (flat, BF16),
        (flat, F32),
        ((tok_count, 1), F32),
        (own, BF16),
        ((wide_count,) + own, BF16),
    )
    return pl.pallas_call(
        forward_kernel,
        out_shape=[make_shape(*item) for item in shapes],
        grid_spec=pltpu.PrefetchScalarGridSpec(
            num_scalar_prefetch=0,
            grid=(units // tile,),
            in_specs=[
                hbm,
                hbm,
                wide_vector,
                hbm,
                vector,
                vector,
                vector,
                pl.BlockSpec((width, tile), lambda step: (0, step)),
                pl.BlockSpec((1, tile), lambda step: (0, step)),
                pl.BlockSpec((tile, width), lambda step: (step, 0)),
                vector,
                vector,
                vector,
            ],
            out_specs=[
                hbm,
                hbm,
                hbm,
                hbm,
                pl.BlockSpec((tok_count, 1), whole),
                pl.BlockSpec((8, LANES), whole),
                pl.BlockSpec((tok_count, LANES), whole),
                pl.BlockSpec((wide_count, META_ROWS, LANES), lambda step: (0, 0, 0)),
                smem_spec(),
                pl.BlockSpec((tok_count, tile), lambda step: (0, step)),
                pl.BlockSpec((tok_count, tile), lambda step: (0, step)),
                pl.BlockSpec(flat, whole),
                pl.BlockSpec(flat, whole),
                pl.BlockSpec((tok_count, 1), whole),
                pl.BlockSpec(own, whole),
                pl.BlockSpec((wide_count,) + own, lambda step: (0, 0, 0)),
            ],
            scratch_shapes=[
                pltpu.VMEM(stack, BF16),
                pltpu.VMEM(proj, BF16),
                pltpu.VMEM(probs, BF16),
                pltpu.VMEM(flat, F32),
                pltpu.VMEM(flat, F32),
                pltpu.VMEM(flat, F32),
                pltpu.VMEM(w_qkv.shape, BF16),
                pltpu.VMEM(w_o.shape, BF16),
                pltpu.SemaphoreType.DMA((5 + kept_rows,)),
                pltpu.SemaphoreType.DMA((4,)),
            ],
        ),
        cost_estimate=cost(20),
        compiler_params=params(1),
        name="forward",
    )(
        got,
        w_qkv,
        bias,
        w_o,
        b_o,
        gain,
        shift,
        w_in,
        b_in,
        w_out,
        b_out,
        gain_two,
        shift_two,
    )


def route_kernel(me_ref, meta_ref, pair_ref, place_ref, targ_ref, first_ref, second_ref):
    wide_count = meta_ref.shape[0]
    me = me_ref[0]
    kept_rows = place_ref.shape[0] // SEG_ROW
    me_f = me.astype(F32)

    def table(row):
        return jnp.concatenate(
            [meta_ref[j, row : row + 1, :LANES].astype(F32) for j in range(wide_count)], axis=0
        )

    labels = table(0)
    dest = table(1)
    lane = lax.broadcasted_iota(jnp.int32, (wide_count, LANES), 1)
    slots = SEG_ROW * 2 * kept_rows
    dest = jnp.where(lane < slots, dest, -1.0)
    partner = table(2)
    target = table(3) + table(4) + table(5)
    sends = jnp.zeros((wide_count, LANES), F32)
    for owner in range(wide_count):
        to_owner = jnp.max((dest == float(owner)).astype(F32), axis=1, keepdims=True)
        sends = sends + jnp.where(lane == owner, to_owner, 0.0)
    row_id = lax.broadcasted_iota(jnp.int32, (wide_count, wide_count), 0)
    col_id = lax.broadcasted_iota(jnp.int32, (wide_count, wide_count), 1)
    below = (col_id < row_id).astype(BF16)
    earlier = dot(below, sends.astype(BF16))
    rank = jnp.zeros((wide_count, LANES), F32)
    for owner in range(wide_count):
        rank = rank + jnp.where(dest == float(owner), earlier[:, owner : owner + 1], 0.0)
    segment = (lane % SEG_ROW).astype(F32)
    per_owner = float(kept_rows * SEG_ROW)
    place = jnp.where(dest >= 0.0, dest * per_owner + rank * float(SEG_ROW) + segment, -1.0)
    live = (labels[:, 0:1] >= 0.0).astype(F32)
    my_rank = dot(below, jnp.broadcast_to(live, (wide_count, LANES)).astype(BF16))
    seg_lane = lax.broadcasted_iota(jnp.int32, (SEG_ROW, LANES), 1)
    seg_id = lax.broadcasted_iota(jnp.int32, (SEG_ROW, LANES), 0)
    for row in range(kept_rows):
        chosen = (live > 0.0) & (my_rank[:, 0:1] == float(row))
        pick = lambda values: column_sum(jnp.where(chosen, values, 0.0))
        own = (pick(dest) == me_f) & (seg_lane % SEG_ROW == seg_id)
        gather = lambda mask, values: jnp.sum(jnp.where(mask, values, 0.0), axis=1, keepdims=True)
        other = gather(own, pick(partner))
        at_other = seg_lane.astype(F32) == other
        out = slice(row * SEG_ROW, (row + 1) * SEG_ROW)
        place_ref[out, :] = gather(at_other, pick(place))
        targ_ref[out, :] = gather(own, pick(target))
    mine = lax.broadcasted_iota(jnp.int32, (wide_count, LANES), 0) == me
    my_place = column_sum(jnp.where(mine, place, 0.0))
    pair_lane = lax.broadcasted_iota(jnp.int32, (pair_ref.shape[0], LANES), 1)
    for column, out_ref in ((0, first_ref), (1, second_ref)):
        at_slot = pair_lane == pair_ref[:, column : column + 1]
        out_ref[...] = jnp.sum(jnp.where(at_slot, my_place, 0.0), axis=1, keepdims=True)


def route(me, meta, pair_index, kept_rows):
    wide_count = meta.shape[0]
    own = kept_rows * SEG_ROW
    pairs = pair_index.shape[0]
    shapes = (
        ((own, 1), F32),
        ((own, 1), F32),
        ((pairs, 1), F32),
        ((pairs, 1), F32),
    )
    return pl.pallas_call(
        route_kernel,
        out_shape=[make_shape(*item) for item in shapes],
        in_specs=[smem_spec(), vmem_spec(), vmem_spec()],
        out_specs=[vmem_spec()] * len(shapes),
        cost_estimate=cost(1),
        compiler_params=params(),
        name="route",
    )(me, meta, pair_index)


def pick_rows(place_ref, all_ref):
    lane = lax.broadcasted_iota(jnp.int32, (place_ref.shape[0], all_ref.shape[0]), 1)
    return dot((lane.astype(F32) == place_ref[...]).astype(BF16), all_ref[...])


def cosine_parts(left, right):
    inner = row_mean(left * right)
    left_inv = lax.rsqrt(row_mean(left * left) + COS_EPS)
    right_inv = lax.rsqrt(row_mean(right * right) + COS_EPS)
    return (inner, left_inv, right_inv)


def cosine_kernel(first_ref, second_ref, all_ref, sim_ref):
    left = pick_rows(first_ref, all_ref)
    right = pick_rows(second_ref, all_ref)
    inner, left_inv, right_inv = cosine_parts(left, right)
    sim = inner * left_inv * right_inv
    sim_ref[...] = jnp.where(first_ref[...] >= 0.0, sim, 0.0)


def cosine_pairs(first, second, pooled_all):
    return pl.pallas_call(
        cosine_kernel,
        out_shape=jax.ShapeDtypeStruct(first.shape, F32),
        in_specs=[vmem_spec()] * 3,
        out_specs=vmem_spec(),
        cost_estimate=cost(1),
        compiler_params=params(),
        name="cosine_pairs",
    )(first, second, pooled_all)


def part_blocks(parity, held, own_ref, send_refs, first=0):
    for index in range(held.shape[0] // 2):
        own_ref[index] = held[2 * index + parity]
        send_refs[first + index][...] = held[2 * index + 1 - parity]


def norm_back(grad, normed, rstd, gain):
    scaled = grad * gain
    return rstd * (scaled - row_mean(scaled) - normed * row_mean(scaled * normed))


def loss_back_body(
    me_ref,
    own_ref,
    all_ref,
    place_ref,
    targ_ref,
    lab_ref,
    labcol_ref,
    norm_ref,
    rstd_ref,
    gain_ref,
    dres_ref,
    dffn_ref,
    sums_ref,
    kept_ref,
    send_refs,
    held,
):
    depth = held.shape[1]
    tok_count, width = norm_ref.shape
    kept_rows = tok_count // LANES
    left = own_ref[...].astype(F32)
    right = pick_rows(place_ref, all_ref)
    inner, left_inv, right_inv = cosine_parts(left, right)
    error = 2.0 * (inner * left_inv * right_inv - targ_ref[...])
    factor = error * left_inv * right_inv * (1.0 / width)
    d_pooled = (factor * (right - left * (inner * left_inv * left_inv))).astype(BF16).astype(F32)
    gain_sum = jnp.zeros((1, width), F32)
    shift_sum = jnp.zeros((1, width), F32)
    bias_sum = jnp.zeros((1, width), F32)
    lane = lax.broadcasted_iota(jnp.int32, (LANES, LANES), 1).astype(F32)
    for row in range(kept_rows):
        span = slice(row * LANES, (row + 1) * LANES)
        segment = lax.broadcasted_iota(jnp.int32, (SEG_ROW, LANES), 0).astype(F32)
        count = jnp.sum(
            (lab_ref[row : row + 1, :] == segment).astype(F32), axis=1, keepdims=True
        )
        per_token = d_pooled[row * SEG_ROW : (row + 1) * SEG_ROW, :] / count
        shift_sum = shift_sum + column_sum(per_token * count)
        padded = jnp.concatenate([per_token, jnp.zeros((LANES - SEG_ROW, width), F32)], axis=0)
        onehot = (labcol_ref[span, :] == lane).astype(BF16)
        high, middle, low = split_three(padded)
        d_out = dot(onehot, high) + dot(onehot, middle) + dot(onehot, low)
        normed = norm_ref[span, :]
        d_res = norm_back(d_out, normed, rstd_ref[span, :], gain_ref[...])
        d_low = d_res.astype(BF16)
        dres_ref[span, :] = d_res
        dffn_ref[span, :] = d_low
        turned = d_low.T
        for block in range(held.shape[0]):
            held[block, :, span] = turned[block * depth : (block + 1) * depth, :]
        gain_sum = gain_sum + column_sum(d_out * normed)
        bias_sum = bias_sum + column_sum(d_low.astype(F32))
    sums_ref[0:1, :] = gain_sum
    sums_ref[1:2, :] = shift_sum
    sums_ref[2:3, :] = bias_sum
    sums_ref[3:8, :] = jnp.zeros((5, width), F32)
    part_blocks(me_ref[0] & 1, held, kept_ref, send_refs)


def feed_back_kernel(
    half,
    me_ref,
    own_ref,
    all_ref,
    place_ref,
    targ_ref,
    lab_ref,
    labcol_ref,
    norm_two_ref,
    rstd_two_ref,
    gain_two_ref,
    wout_ref,
    win_ref,
    slope_ref,
    norm_src,
    rstd_ref,
    gain_ref,
    wo_src,
    bsum_ref,
    done_ref,
    dattn_t_ref,
    dctx_ref,
    sums_ref,
    sums_two_ref,
    kept_out_ref,
    kept_ref,
    *refs,
):
    send_out, send_refs, refs = refs[:half], refs[half : 2 * half], refs[2 * half :]
    held_out, held, dffn_ref, total_ref, norm_ref, wo_ref, sems = refs
    count, depth, _ = held.shape
    step = pl.program_id(0)
    copies = [
        pltpu.make_async_copy(norm_src, norm_ref, sems.at[0]),
        pltpu.make_async_copy(wo_src, wo_ref, sems.at[1]),
    ]

    @pl.when(step == 0)
    def _():
        for copy in copies:
            copy.start()
        loss_back_body(
            me_ref,
            own_ref,
            all_ref,
            place_ref,
            targ_ref,
            lab_ref,
            labcol_ref,
            norm_two_ref,
            rstd_two_ref,
            gain_two_ref,
            total_ref,
            dffn_ref,
            sums_two_ref,
            kept_out_ref,
            send_out,
            held_out,
        )

    d_up = (dot(dffn_ref[...], wout_ref[...], NT) * slope_ref[...].astype(F32)).astype(BF16)
    turned = d_up.T
    for block in range(count):
        held[block] = turned[block * depth : (block + 1) * depth, :]
    for at in range(half // (count // 2)):

        @pl.when(step == at)
        def _():
            part_blocks(me_ref[0] & 1, held, kept_ref, send_refs, at * (count // 2))

    bsum_ref[...] = column_sum(d_up.astype(F32))
    total_ref[...] += dot(d_up, win_ref[...], NT)

    @pl.when(step == pl.num_programs(0) - 1)
    def _():
        for copy in copies:
            copy.wait()
        tok_count, width = total_ref.shape
        kept_rows = tok_count // LANES
        gain_sum = jnp.zeros((1, width), F32)
        shift_sum = jnp.zeros((1, width), F32)
        bias_sum = jnp.zeros((1, width), F32)
        for row in range(kept_rows):
            span = slice(row * LANES, (row + 1) * LANES)
            d_hidden = total_ref[span, :]
            normed = norm_ref[span, :]
            d_res = norm_back(d_hidden, normed, rstd_ref[span, :], gain_ref[...])
            d_low = d_res.astype(BF16)
            done_ref[span, :] = d_res
            dattn_t_ref[:, span] = d_low.T
            dctx_ref[span, :] = dot(d_low, wo_ref[...], NT).astype(BF16)
            gain_sum = gain_sum + column_sum(d_hidden * normed)
            shift_sum = shift_sum + column_sum(d_hidden)
            bias_sum = bias_sum + column_sum(d_low.astype(F32))
        sums_ref[0:1, :] = gain_sum
        sums_ref[1:2, :] = shift_sum
        sums_ref[2:3, :] = bias_sum
        sums_ref[3:8, :] = jnp.zeros((5, width), F32)


def feed_back(
    me,
    own,
    pooled_all,
    place,
    target,
    labels,
    label_cols,
    normed_two,
    rstd_two,
    gain_two,
    w_out,
    w_in,
    slope,
    normed,
    rstd,
    gain,
    w_o,
    wide_count,
):
    tok_count, width = normed.shape
    units = w_in.shape[1]
    tile = 768
    depth = units // wide_count
    depth_out = width // wide_count
    half = wide_count // 2
    count = tile // depth
    whole = lambda step: (0, 0)
    fixed = lambda array: pl.BlockSpec(array.shape, whole)
    hbm = pl.BlockSpec(memory_space=pl.ANY)
    shapes = (
        (
            ((1, units), F32),
            ((tok_count, width), F32),
            ((width, tok_count), BF16),
            ((tok_count, width), BF16),
            ((8, width), F32),
            ((8, width), F32),
            ((half, depth_out, tok_count), BF16),
            ((half, depth, tok_count), BF16),
        )
        + (((depth_out, tok_count), BF16, hbm_shape),) * half
        + (((depth, tok_count), BF16, hbm_shape),) * half
    )
    return pl.pallas_call(
        functools.partial(feed_back_kernel, half),
        out_shape=[make_shape(*item) for item in shapes],
        grid_spec=pltpu.PrefetchScalarGridSpec(
            num_scalar_prefetch=0,
            grid=(units // tile,),
            in_specs=[
                smem_spec(),
                fixed(own),
                fixed(pooled_all),
                fixed(place),
                fixed(target),
                fixed(labels),
                fixed(label_cols),
                fixed(normed_two),
                fixed(rstd_two),
                fixed(gain_two),
                pl.BlockSpec((tile, width), lambda step: (step, 0)),
                pl.BlockSpec((width, tile), lambda step: (0, step)),
                pl.BlockSpec((tok_count, tile), lambda step: (0, step)),
                hbm,
                fixed(rstd),
                fixed(gain),
                hbm,
            ],
            out_specs=[
                pl.BlockSpec((1, tile), lambda step: (0, step)),
                pl.BlockSpec((tok_count, width), whole),
                pl.BlockSpec((width, tok_count), whole),
                pl.BlockSpec((tok_count, width), whole),
                pl.BlockSpec((8, width), whole),
                pl.BlockSpec((8, width), whole),
                pl.BlockSpec((half, depth_out, tok_count), lambda step: (0, 0, 0)),
                pl.BlockSpec((count // 2, depth, tok_count), lambda step: (step, 0, 0)),
            ]
            + [pl.BlockSpec((depth_out, tok_count), whole)] * half
            + [pl.BlockSpec((depth, tok_count), whole)] * half,
            scratch_shapes=[
                pltpu.VMEM((wide_count, depth_out, tok_count), BF16),
                pltpu.VMEM((count, depth, tok_count), BF16),
                pltpu.VMEM((tok_count, width), BF16),
                pltpu.VMEM((tok_count, width), F32),
                pltpu.VMEM((tok_count, width), F32),
                pltpu.VMEM(w_o.shape, BF16),
                pltpu.SemaphoreType.DMA((2,)),
            ],
        ),
        cost_estimate=cost(14),
        compiler_params=params(1),
        name="feed_back",
    )(
        me,
        own,
        pooled_all,
        place,
        target,
        labels,
        label_cols,
        normed_two,
        rstd_two,
        gain_two,
        w_out,
        w_in,
        slope,
        normed,
        rstd,
        gain,
        w_o,
    )


def attend_back_kernel(
    source_ref,
    me_ref,
    proj_ref,
    probs_ref,
    dctx_ref,
    done_ref,
    wqkv_ref,
    dattn_t_ref,
    dtok_ref,
    sums_ref,
    kept_ref,
    *refs,
):
    send_refs, held, dproj_ref = refs[:-2], refs[-2], refs[-1]
    row = pl.program_id(0)
    row_len, width = dctx_ref.shape
    blocks = held.shape[0]
    main = 3 * width // blocks
    scale = 1.0 / math.sqrt(HEAD_DIM)
    lane = lax.broadcasted_iota(jnp.int32, (row_len, LANES), 1)
    left = (lane < HEAD_DIM).astype(BF16)
    right = (lane >= HEAD_DIM).astype(BF16)

    def twice(values):
        return jnp.concatenate([values * left, values * right], axis=0)

    for pair in range(width // LANES):
        col = pair * LANES
        queries = proj_ref[:, col : col + LANES]
        key_rows = proj_ref[:, width + col : width + col + LANES]
        values = proj_ref[:, 2 * width + col : 2 * width + col + LANES]
        probs = probs_ref[0, pair]
        d_ctx = twice(dctx_ref[:, col : col + LANES])
        d_probs = dot(d_ctx, values, NT)
        probs_f = probs.astype(F32)
        inner = jnp.sum(probs_f * d_probs, axis=-1, keepdims=True)
        d_scores = (probs_f * (d_probs - inner)).astype(BF16)
        wide_scores = jnp.concatenate([d_scores[:row_len], d_scores[row_len:]], axis=1)
        d_query = dot(wide_scores, twice(key_rows)) * scale
        d_key = dot(d_scores, twice(queries), TN) * scale
        d_value = dot(probs, d_ctx, TN)
        for part, grad in ((0, d_query), (1, d_key), (2, d_value)):
            low = grad.astype(BF16)
            place = part * width + col
            dproj_ref[:, place : place + LANES] = low
            turned = low.T
            start = place
            while start < place + LANES:
                block, offset = divmod(start, main)
                stop = min(place + LANES, (block + 1) * main)
                held[block, offset : offset + stop - start, :] = turned[
                    start - place : stop - place, :
                ]
                start = stop
            before = jnp.where(row == 0, 0.0, sums_ref[:, place : place + LANES])
            sums_ref[:, place : place + LANES] = before + column_sum(low.astype(F32))

    rest = width // blocks
    for block in range(blocks):
        held[block, main:, :] = dattn_t_ref[block * rest : (block + 1) * rest, :]
    part_blocks(me_ref[0] & 1, held, kept_ref, send_refs)
    grad = done_ref[...] + dot(dproj_ref[...], wqkv_ref[...], NT)
    dtok_ref[0] = grad.astype(BF16)


def attend_back(sources, me, proj, probs, d_ctx, d_one, w_qkv, d_attn_t, wide_count):
    tok_count, width = d_ctx.shape
    kept_rows = tok_count // LANES
    half = wide_count // 2
    depth = 4 * width // wide_count
    shapes = (
        ((wide_count, LANES, width), BF16),
        ((1, 3 * width), F32),
        ((half, depth, tok_count), BF16),
    ) + (((depth, tok_count), BF16, hbm_shape),) * half
    return pl.pallas_call(
        attend_back_kernel,
        out_shape=[make_shape(*item) for item in shapes],
        grid_spec=pltpu.PrefetchScalarGridSpec(
            num_scalar_prefetch=2,
            grid=(kept_rows,),
            in_specs=[
                pl.BlockSpec((LANES, 3 * width), lambda row, src, me: (row, 0)),
                pl.BlockSpec((1,) + probs.shape[1:], lambda row, src, me: (row, 0, 0, 0)),
                pl.BlockSpec((LANES, width), lambda row, src, me: (row, 0)),
                pl.BlockSpec((LANES, width), lambda row, src, me: (row, 0)),
                pl.BlockSpec((width, 3 * width), lambda row, src, me: (0, 0)),
                pl.BlockSpec((width, LANES), lambda row, src, me: (0, row)),
            ],
            out_specs=[
                pl.BlockSpec((1, LANES, width), lambda row, src, me: (src[row], 0, 0)),
                pl.BlockSpec((1, 3 * width), lambda row, src, me: (0, 0)),
                pl.BlockSpec((half, depth, LANES), lambda row, src, me: (0, 0, row)),
            ]
            + [pl.BlockSpec((depth, LANES), lambda row, src, me: (0, row))] * half,
            scratch_shapes=[
                pltpu.VMEM((wide_count, depth, LANES), BF16),
                pltpu.VMEM((LANES, 3 * width), BF16),
            ],
        ),
        cost_estimate=cost(20),
        compiler_params=params(1),
        name="attend_back",
    )(sources, me, proj, probs, d_ctx, d_one, w_qkv, d_attn_t)


def home_kernel(dest_ref, rows_ref, out_ref, sems):
    slot_dev = out_ref.shape[0]

    def copy(slot):
        return pltpu.make_async_copy(
            rows_ref.at[jnp.maximum(dest_ref[slot], 0)], out_ref.at[slot], sems.at[slot]
        )

    for slot in range(slot_dev):
        copy(slot).start()
    for slot in range(slot_dev):
        copy(slot).wait()

        @pl.when(dest_ref[slot] < 0)
        def _():
            out_ref[slot] = jnp.zeros(out_ref.shape[1:], out_ref.dtype)


def home_rows(destination, rows):
    count = destination.shape[0]
    return pl.pallas_call(
        home_kernel,
        out_shape=jax.ShapeDtypeStruct((count,) + rows.shape[1:], rows.dtype),
        in_specs=[smem_spec(), pl.BlockSpec(memory_space=pl.ANY)],
        out_specs=vmem_spec(),
        scratch_shapes=[pltpu.SemaphoreType.DMA((count,))],
        cost_estimate=cost(3),
        compiler_params=params(),
        name="home_rows",
    )(destination, rows)


def block_at(index, bit, value):
    low = index & ((1 << bit) - 1)
    return ((index >> bit) << (bit + 1)) | (value << bit) | low


def grad_kernel(first_bit, second_bit, spans, blocks, me_ref, own_ref, *refs):
    recv_refs, refs = refs[:blocks], refs[blocks:]
    step = pl.program_id(0)
    half_steps = pl.num_programs(0) // 2
    terms = len(spans)
    own_xs, recv_xs = refs[:terms], refs[terms : 2 * terms]
    outs = refs[2 * terms : 2 * terms + 4]
    own_lefts = refs[2 * terms + 4 : 3 * terms + 4]
    recv_lefts = refs[3 * terms + 4 :]
    me = me_ref[0]
    for half, bit in ((0, first_bit), (1, second_bit)):

        @pl.when(step == half * half_steps)
        def _():
            side = (me >> bit) & 1
            for block in range(blocks):
                low = block & ((1 << (bit - 1)) - 1)
                rest = ((block >> bit) << (bit - 1)) | low
                kept = ((block >> (bit - 1)) & 1) == side
                index = jnp.where(kept, rest, rest + blocks // 2)
                for (start, stop), own_left, recv_left in zip(spans, own_lefts, recv_lefts):
                    own_left[index] = own_ref[block, start:stop, :]
                    recv_left[index] = recv_refs[block][start:stop, :]

    for term, (start, stop) in enumerate(spans):
        rows = stop - start
        chunk = blocks if blocks * rows <= 384 else blocks // 2
        for base in range(0, blocks, chunk):
            span = slice(base, base + chunk)
            flat = lambda left: left[span].reshape(chunk * rows, left.shape[2])
            part = dot(flat(own_lefts[term]), own_xs[term][...])
            part = part + dot(flat(recv_lefts[term]), recv_xs[term][...])
            part = part.astype(BF16).reshape(chunk, rows, part.shape[1])
            for index in range(chunk):
                block = base + index
                role, place = divmod(block, blocks // 2)
                for half in range(2):

                    @pl.when((step < half_steps) == (half == 0))
                    def _():
                        outs[2 * half + role][place, start:stop, :] = part[index]


def grad_terms(me, own, received, own_xs, recv_xs, spans, first_bit, second_bit, tile):
    blocks = len(received)
    rows, tok_count = received[0].shape
    columns = own_xs[0][0].shape[-1]
    steps = columns // tile
    half = steps // 2

    def x_spec(item):
        array, lead = item
        if lead is None:
            return pl.BlockSpec((tok_count, tile), lambda step: (0, step))
        return pl.BlockSpec((pl.Squeezed(), tok_count, tile), lambda step: (lead, 0, step))

    out_block = (blocks // 2, rows, tile)
    first_spec = pl.BlockSpec(out_block, lambda step: (0, 0, jnp.minimum(step, half - 1)))
    second_spec = pl.BlockSpec(out_block, lambda step: (0, 0, jnp.maximum(step - half, 0)))
    shape = hbm_shape((blocks // 2, rows, columns // 2), BF16)
    whole = lambda step: (0, 0, 0)
    lefts = [pltpu.VMEM((blocks, stop - start, tok_count), BF16) for start, stop in spans]
    return pl.pallas_call(
        functools.partial(grad_kernel, first_bit, second_bit, spans, blocks),
        out_shape=[shape] * 4,
        grid_spec=pltpu.PrefetchScalarGridSpec(
            num_scalar_prefetch=0,
            grid=(steps,),
            in_specs=[
                smem_spec(),
                pl.BlockSpec(own.shape, whole),
            ]
            + [pl.BlockSpec((rows, tok_count), lambda step: (0, 0))] * blocks
            + [x_spec(item) for item in own_xs + recv_xs],
            out_specs=[first_spec, first_spec, second_spec, second_spec],
            scratch_shapes=lefts + lefts,
        ),
        cost_estimate=cost(7),
        compiler_params=params(1),
        name="grad_terms",
    )(me, own, *received, *[item[0] for item in own_xs + recv_xs])


def fold_kernel(bits, places, me_ref, *refs):
    me = me_ref[0]
    for half in range(2):
        kept_ref, recv_ref = refs[2 * half], refs[2 * half + 1]
        keep_out, send_out = refs[4 + 2 * half], refs[5 + 2 * half]
        side = (me >> bits[half]) & 1
        for index in range(keep_out.shape[0]):
            for value, out_ref in ((1 - side, send_out), (side, keep_out)):
                block = block_at(index, places[half], value)
                out_ref[index] = add_low(kept_ref[block], recv_ref[block])


def fold(me, halves, bits, places):
    shapes = []
    for kept, _ in halves:
        shapes += [hbm_shape((kept.shape[0] // 2,) + kept.shape[1:], BF16)] * 2
    return pl.pallas_call(
        functools.partial(fold_kernel, bits, places),
        out_shape=shapes,
        in_specs=[smem_spec()] + [vmem_spec()] * 4,
        out_specs=[vmem_spec()] * 4,
        cost_estimate=cost(0.5),
        compiler_params=params(),
        name="fold",
    )(me, *halves[0], *halves[1])


def piece_kernel(turned, stacked, me_ref, *refs):
    outs, held = (refs[4:], refs[4]) if stacked else (refs[4:-1], refs[-1])
    count = held.shape[0]
    depth = held.shape[1] if turned else held.shape[2]
    for half in range(2):
        total = add_low(refs[2 * half][0], refs[2 * half + 1][0])
        if turned:
            total = total.T
        for index in range(count // 2):
            span = slice(index * depth, (index + 1) * depth)
            held[half * (count // 2) + index] = total[span, :] if turned else total[:, span]
    if not stacked:
        for step in range(count):
            outs[step][...] = held[me_ref[0] ^ step]


def narrow_pieces(me, halves, narrow_count, turned, stacked):
    _, rows, columns = halves[0][0].shape
    depth = 2 * columns // narrow_count
    shape = (depth, rows) if turned else (rows, depth)
    whole = (narrow_count,) + shape
    outs = [hbm_shape(whole, BF16)] if stacked else [hbm_shape(shape, BF16)] * narrow_count
    return pl.pallas_call(
        functools.partial(piece_kernel, turned, stacked),
        out_shape=outs,
        in_specs=[smem_spec()] + [vmem_spec()] * 4,
        out_specs=[vmem_spec()] * len(outs),
        scratch_shapes=[] if stacked else [pltpu.VMEM(whole, BF16)],
        cost_estimate=cost(1),
        compiler_params=params(),
        name="narrow_pieces",
    )(me, *halves[0], *halves[1])


def sum_kernel(count, *refs):
    terms = [ref[...] for ref in refs[:count]]
    if len(terms[0].shape) == 3:
        terms = [terms[0][place] for place in range(terms[0].shape[0])]
    total = terms[0].astype(F32)
    for term in terms[1:]:
        total = total + term.astype(F32)
    start = 0
    for out_ref in refs[count:]:
        out_ref[...] = total[:, start : start + out_ref.shape[1]]
        start += out_ref.shape[1]


def sum_pieces(pieces, cuts=None):
    shape = pieces[0].shape[-2:]
    outs = [jax.ShapeDtypeStruct((shape[0], cut), F32) for cut in cuts or (shape[1],)]
    return pl.pallas_call(
        functools.partial(sum_kernel, len(pieces)),
        out_shape=outs,
        in_specs=[vmem_spec()] * len(pieces),
        out_specs=[vmem_spec()] * len(outs),
        cost_estimate=cost(1),
        compiler_params=params(),
        name="sum_pieces",
    )(*pieces)


def pack_kernel(cuts, *refs):
    out_ref = refs[-1]
    place = 0
    for index, row, start, stop in cuts:
        for at in range(start, stop, LANES):
            out_ref[place : place + 1, :] = refs[index][row : row + 1, at : at + LANES]
            place += 1


def pack_vectors(arrays, cuts):
    lines = sum(stop - start for _, _, start, stop in cuts) // LANES
    return pl.pallas_call(
        functools.partial(pack_kernel, cuts),
        out_shape=jax.ShapeDtypeStruct((lines, LANES), F32),
        in_specs=[vmem_spec()] * len(arrays),
        out_specs=vmem_spec(),
        cost_estimate=cost(0.5),
        compiler_params=params(),
        name="pack_vectors",
    )(*arrays)


def swap(values, axis, bit):
    count = lax.axis_size(axis)
    return lax.ppermute(values, axis, [(i, i ^ (1 << bit)) for i in range(count)])


def trade(pieces):
    count = len(pieces)
    got = [pieces[0]]
    for step in range(1, count):
        got.append(lax.ppermute(pieces[step], "narrow", [(i, i ^ step) for i in range(count)]))
    return got


def pick(values, dim, index):
    return lax.dynamic_index_in_dim(values, index, dim, keepdims=False)


def add_low(kept, received):
    return (kept.astype(F32) + received.astype(F32)).astype(BF16)


def after(value, *others):
    return lax.optimization_barrier((value,) + others)[0]


def to_partner(blocks):
    return [swap(block, "wide", 0) for block in blocks]


class Folding:
    def __init__(self, me, outs, orders, *gates):
        self.me = me
        self.orders = orders
        self.left = [sorted(order) for order in orders]
        self.kept = [outs[0], outs[2]]
        self.sent = [outs[1], outs[3]]
        self.level = 0
        self.exchange(*gates)

    def exchange(self, *gates):
        self.received = [
            swap(after(self.sent[half], *gates), "wide", self.orders[half][self.level])
            for half in range(2)
        ]
        for half in range(2):
            self.left[half].remove(self.orders[half][self.level])
        self.level += 1

    def halves(self):
        return [(self.kept[half], self.received[half]) for half in range(2)]

    def step(self, *gates):
        bits = [order[self.level] for order in self.orders]
        places = [left.index(bit) for left, bit in zip(self.left, bits)]
        outs = fold(self.me, self.halves(), bits, places)
        self.kept = [outs[0], outs[2]]
        self.sent = [outs[1], outs[3]]
        self.exchange(*gates)

    def gate(self, *others):
        self.kept[0] = after(self.kept[0], *others)

    def finish(self, me_narrow, narrow_count, turned, stacked=False):
        while self.level < len(self.orders[0]):
            self.step()
        return narrow_pieces(me_narrow, self.halves(), narrow_count, turned, stacked)


def hop(values, axis, bit):
    return values + swap(values, axis, bit)


def on_device(
    tokens,
    segments,
    destination,
    pair_index,
    targets,
    w_qkv,
    b_qv,
    w_o,
    b_o,
    gain_one,
    shift_one,
    w_in,
    b_in,
    w_out,
    b_out,
    gain_two,
    shift_two,
):
    wide_count = lax.axis_size("wide")
    narrow_count = lax.axis_size("narrow")
    slot_dev, row_len, width = tokens.shape
    kept_rows = slot_dev // 2
    units = w_in.shape[1]
    me = lax.axis_index("wide")
    me_line = me.astype(jnp.int32).reshape(1)
    me_narrow = lax.axis_index("narrow").astype(jnp.int32).reshape(1)
    line = lambda vector: vector.reshape(1, -1)

    sent = build_send(tokens, segments, destination, pair_index, targets, wide_count)
    got = lax.all_to_all(sent, "wide", split_axis=0, concat_axis=0, tiled=True)
    full_bias = jnp.concatenate(
        [b_qv[:width], jnp.zeros((width,), F32), b_qv[width:]]
    ).reshape(1, 3 * width)
    (
        stack,
        proj,
        probs,
        norm_one,
        rstd_one,
        labels,
        label_cols,
        meta,
        sources,
        act,
        slope,
        encoded,
        norm_two,
        rstd_two,
        pooled,
        pooled_copies,
    ) = forward(
        got,
        w_qkv,
        full_bias,
        w_o,
        line(b_o),
        line(gain_one),
        line(shift_one),
        w_in,
        line(b_in),
        w_out,
        line(b_out),
        line(gain_two),
        line(shift_two),
        kept_rows,
    )
    stack_recv = swap(stack, "wide", 0)
    act_recv = swap(act, "wide", 0)
    place, target, first, second = route(me_line, meta, pair_index, kept_rows)
    pooled_all = lax.all_to_all(
        pooled_copies, "wide", split_axis=0, concat_axis=0, tiled=True
    ).reshape(wide_count * kept_rows * SEG_ROW, width)
    similarity = cosine_pairs(first, second, pooled_all).reshape(-1)
    bits = wide_count.bit_length() - 1
    middle = 1 + (bits - 1) // 2
    low_first = list(range(1, bits))
    high_first = list(range(middle, bits)) + list(range(1, middle))
    orders = (low_first, high_first)
    first_bits = (low_first[0], high_first[0])
    half = wide_count // 2
    sum_b_in, d_one, d_attn_t, d_ctx, sums_one, sums_two, own_out, own_in, *sends = feed_back(
        me_line,
        pooled,
        pooled_all,
        place,
        target,
        labels,
        label_cols,
        norm_two,
        rstd_two,
        line(gain_two),
        w_out,
        w_in,
        slope,
        norm_one,
        rstd_one,
        line(gain_one),
        w_o,
        wide_count,
    )
    rows_out = own_out.shape[1]
    rows_in = own_in.shape[1]
    recv_out = to_partner(sends[:half])
    recv_in = to_partner(after(tuple(sends[half:]), tuple(recv_out)))
    fold_out = Folding(
        me_line,
        grad_terms(
            me_line,
            own_out,
            recv_out,
            [(act, None)],
            [(act_recv, None)],
            ((0, rows_out),),
            *first_bits,
            512,
        ),
        orders,
    )
    outs_in = grad_terms(
        me_line,
        own_in,
        after(tuple(recv_in), *fold_out.sent),
        [(stack, 2)],
        [(stack_recv, 2)],
        ((0, rows_in),),
        *first_bits,
        width // 2,
    )
    fold_out.gate(similarity, *outs_in)
    fold_out.step()
    fold_in = Folding(me_line, outs_in, orders, *fold_out.sent)
    d_rows, sums_qkv, own_mix, *send_mix = attend_back(
        sources,
        me_line,
        proj,
        probs,
        after(d_ctx, *fold_out.sent, *fold_in.sent),
        d_one,
        w_qkv,
        d_attn_t,
        wide_count,
    )
    recv_mix = to_partner(send_mix)
    vectors = pack_vectors(
        (sums_qkv, sums_one, sum_b_in, sums_two),
        (
            (0, 0, 0, width),
            (0, 0, 2 * width, 3 * width),
            (1, 2, 0, width),
            (1, 0, 0, width),
            (1, 1, 0, width),
            (2, 0, 0, units),
            (3, 2, 0, width),
            (3, 0, 0, width),
            (3, 1, 0, width),
        ),
    )
    fold_in.gate(d_rows, *fold_out.received)
    fold_in.step()
    fold_out.gate(d_rows)
    pieces_out = fold_out.finish(me_narrow, narrow_count, False)
    traded_out = trade(pieces_out)
    home = lax.all_to_all(
        after(d_rows, *fold_in.sent), "wide", split_axis=0, concat_axis=0, tiled=True
    )
    cols_qkv = 3 * width // wide_count
    rows_mix = own_mix.shape[1]
    (grad_w_out,) = sum_pieces(traded_out)
    grad_w_out = grad_w_out.T
    outs_mix = grad_terms(
        me_line,
        own_mix,
        after(tuple(recv_mix), tuple(pieces_out), *fold_in.sent),
        [(stack, 0), (stack, 1)],
        [(stack_recv, 0), (stack_recv, 1)],
        ((0, cols_qkv), (cols_qkv, rows_mix)),
        *first_bits,
        width // 2,
    )
    vectors = hop(vectors, "wide", 0)
    vectors = hop(vectors, "narrow", 0)
    fold_mix = Folding(
        me_line,
        outs_mix,
        orders,
        vectors,
        tuple(traded_out),
        *fold_in.received,
    )
    grad_tokens = home_rows(destination, home)
    pieces_in = fold_in.finish(me_narrow, narrow_count, True)
    traded_in = trade(pieces_in)
    fold_mix.gate(grad_tokens, tuple(traded_in))
    fold_mix.step()
    vectors = after(vectors, *fold_mix.sent)
    for bit in range(1, narrow_count.bit_length() - 1):
        vectors = hop(vectors, "narrow", bit)
    (grad_w_in,) = sum_pieces(traded_in)
    fold_mix.gate(vectors)
    (pieces_mix,) = fold_mix.finish(me_narrow, narrow_count, True, True)
    traded_mix = lax.all_to_all(pieces_mix, "narrow", split_axis=0, concat_axis=0, tiled=True)
    vectors = after(vectors, pieces_mix)
    for bit in range(1, bits):
        vectors = hop(vectors, "wide", bit)
    grad_w_qkv, grad_w_o = sum_pieces(
        (after(traded_mix, vectors),), (cols_qkv, rows_mix - cols_qkv)
    )
    vectors = vectors.reshape(-1)
    cuts = (2 * width, width, width, width, units, width, width, width)
    outs = []
    start = 0
    for size in cuts:
        outs.append(vectors[start : start + size])
        start += size
    grad_b_qv, grad_b_o, grad_gain_one, grad_shift_one = outs[:4]
    grad_b_in, grad_b_out, grad_gain_two, grad_shift_two = outs[4:]
    return (
        encoded.reshape(kept_rows, row_len, width),
        similarity,
        grad_tokens,
        grad_w_qkv,
        grad_b_qv,
        grad_w_o,
        grad_b_o,
        grad_gain_one,
        grad_shift_one,
        grad_w_in,
        grad_b_in,
        grad_w_out,
        grad_b_out,
        grad_gain_two,
        grad_shift_two,
    )


def solution(mesh):
    rows = ("wide", "narrow")
    in_specs = (P(rows, None, None), P(rows, None), P(rows), P(rows, None), P(rows)) + (P(),) * 12
    matrix = P("narrow", "wide")
    out_specs = (
        P(rows, None, None),
        P(rows),
        P(rows, None, None),
        matrix,
        P(),
        matrix,
        P(),
        P(),
        P(),
        matrix,
        P(),
        matrix,
        P(),
        P(),
        P(),
    )
    return jax.shard_map(
        on_device, mesh=mesh, in_specs=in_specs, out_specs=out_specs, check_vma=False
    )
```

```python
import functools
import math

import jax
import jax.numpy as jnp
from jax import lax
from jax.experimental import pallas as pl
from jax.experimental.pallas import tpu as pltpu
from jax.sharding import PartitionSpec as P

HEAD_DIM = 64
SEG_ROW = 8
LANES = 128
META_ROWS = 16
NEG_FILL = -1e30
NORM_EPS = 1e-12
COS_EPS = 1e-06
F32 = jnp.float32
BF16 = jnp.bfloat16
VMEM_LIMIT = 67043328


def cost(micros):
    return pl.CostEstimate(flops=0, bytes_accessed=int(micros * 3.0e6), transcendentals=0)


NT = (((1,), (1,)), ((), ()))
TN = (((0,), (0,)), ((), ()))


def vmem_spec():
    return pl.BlockSpec(memory_space=pltpu.VMEM)


def hbm_shape(shape, dtype):
    return pltpu.HBM(shape, dtype)


def make_shape(shape, dtype, make=jax.ShapeDtypeStruct):
    return make(shape, dtype)


def params(steps=0):
    return pltpu.CompilerParams(
        dimension_semantics=("arbitrary",) * steps if steps else None,
        vmem_limit_bytes=VMEM_LIMIT,
    )


def split_three(values):
    high = values.astype(BF16)
    rest = values - high.astype(F32)
    middle = rest.astype(BF16)
    low = (rest - middle.astype(F32)).astype(BF16)
    return (high, middle, low)


def dot(left, right, dims=None):
    if dims is None:
        return jnp.dot(left, right, preferred_element_type=F32)
    return lax.dot_general(left, right, dims, preferred_element_type=F32)


def column_sum(values):
    return jnp.sum(values, axis=0, keepdims=True)


def row_mean(values):
    return jnp.mean(values, axis=-1, keepdims=True)


def prep_kernel(dest_ref, pair_ref, targ_ref, tok_ref, seg_ref, out_ref, sems):
    slot_dev = dest_ref.shape[0]
    wide_count, _, width = out_ref.shape
    row_len = tok_ref.shape[1]
    sources = []
    lives = []
    copies = []
    for owner in range(wide_count):
        found = jnp.int32(0)
        live = dest_ref[0] == owner
        for slot in range(1, slot_dev):
            match = dest_ref[slot] == owner
            found = jnp.where(match, slot, found)
            live = live | match
        sources.append(found)
        lives.append(live)
        copy = pltpu.make_async_copy(
            tok_ref.at[found], out_ref.at[owner, pl.ds(0, row_len), :], sems.at[owner]
        )
        copy.start()
        copies.append(copy)
    lane = lax.broadcasted_iota(jnp.int32, (1, LANES), 1)
    dest = jnp.full((1, LANES), -1, jnp.int32)
    for slot in range(slot_dev):
        dest = jnp.where(lane // SEG_ROW == slot, dest_ref[slot], dest)
    partner = jnp.zeros((1, LANES), jnp.int32)
    target = jnp.zeros((1, LANES), F32)
    for pair in range(pair_ref.shape[1]):
        first = pair_ref[0, pair]
        second = pair_ref[1, pair]
        at_first = lane == first
        at_second = lane == second
        partner = jnp.where(at_first, second, jnp.where(at_second, first, partner))
        target = jnp.where(at_first | at_second, targ_ref[0, pair], target)
    high, middle, low = split_three(target)
    fixed = [dest.astype(F32), partner.astype(F32)]
    fixed += [high.astype(F32), middle.astype(F32), low.astype(F32)]
    fixed.append(jnp.zeros((META_ROWS - 1 - len(fixed), LANES), F32))
    for owner in range(wide_count):
        labels = seg_ref[pl.ds(sources[owner], 1), :].astype(F32)
        labels = jnp.where(lives[owner], labels, -1.0)
        table = jnp.concatenate([labels] + fixed, axis=0)
        out_ref[owner, row_len:, :LANES] = table.astype(BF16)
        out_ref[owner, row_len:, LANES:] = jnp.zeros((META_ROWS, width - LANES), BF16)
    for copy in copies:
        copy.wait()


def smem_spec():
    return pl.BlockSpec(memory_space=pltpu.SMEM)


def build_send(tokens, segments, destination, pair_index, targets, wide_count):
    slot_dev, row_len, width = tokens.shape
    return pl.pallas_call(
        prep_kernel,
        out_shape=jax.ShapeDtypeStruct((wide_count, row_len + META_ROWS, width), BF16),
        in_specs=[smem_spec()] * 3 + [pl.BlockSpec(memory_space=pl.ANY), vmem_spec()],
        out_specs=vmem_spec(),
        scratch_shapes=[pltpu.SemaphoreType.DMA((wide_count,))],
        cost_estimate=cost(3),
        compiler_params=params(),
        name="build_send",
    )(destination, pair_index.T, targets.reshape(1, -1), tokens, segments)


def attend_body(
    got_ref,
    wqkv_src,
    bias_ref,
    wo_src,
    bo_ref,
    gain_ref,
    shift_ref,
    rstd_ref,
    lab_ref,
    labcol_ref,
    meta_ref,
    source_ref,
    stack_ref,
    proj_ref,
    probs_ref,
    norm_ref,
    hid_ref,
    wqkv_ref,
    wo_ref,
    sems,
):
    x_ref, ctx_ref, low_ref = stack_ref.at[0], stack_ref.at[1], stack_ref.at[2]
    wide_count = got_ref.shape[0]
    tok_count, width = hid_ref.shape
    row_len = got_ref.shape[1] - META_ROWS
    kept_rows = tok_count // row_len
    total_cols = proj_ref.shape[1]
    parts = total_cols // width
    get_meta = pltpu.make_async_copy(
        got_ref.at[:, pl.ds(row_len, META_ROWS), pl.ds(0, LANES)], meta_ref, sems.at[0]
    )
    get_meta.start()
    get_weights = []
    for part in range(parts):
        span = pl.ds(part * width, width)
        get_weights.append(
            pltpu.make_async_copy(
                wqkv_src.at[:, span], wqkv_ref.at[:, span], sems.at[1 + part]
            )
        )
    get_wo = pltpu.make_async_copy(wo_src, wo_ref, sems.at[1 + parts])
    get_weights[0].start()
    get_meta.wait()
    seen = jnp.int32(0)
    sources = [jnp.int32(0)] * kept_rows
    for slot in range(wide_count):
        live = jnp.max(meta_ref[slot, 0:1, :].astype(F32)) >= 0.0
        for row in range(kept_rows):
            sources[row] = jnp.where(live & (seen == row), slot, sources[row])
        seen = seen + live.astype(jnp.int32)
    get_rows = []
    for row in range(kept_rows):
        source_ref[row] = sources[row]
        span = pl.ds(row * row_len, row_len)
        get_rows.append(
            pltpu.make_async_copy(
                got_ref.at[sources[row], pl.ds(0, row_len), :],
                x_ref.at[span, :],
                sems.at[2 + parts + row],
            )
        )
        get_rows[row].start()
    for copy in get_weights[1:] + [get_wo]:
        copy.start()
    for row in range(kept_rows):
        span = pl.ds(row * row_len, row_len)
        tag = meta_ref[sources[row], 0:1, :].astype(F32)
        lab_ref[row : row + 1, :] = tag
        labcol_ref[span, :] = jnp.broadcast_to(tag, (LANES, LANES)).T
    for copy in get_rows:
        copy.wait()
    tile = 256
    for start in range(0, total_cols, tile):
        if start % width == 0:
            get_weights[start // width].wait()
        cols = slice(start, start + tile)
        proj_ref[:, cols] = (dot(x_ref[...], wqkv_ref[:, cols]) + bias_ref[:, cols]).astype(BF16)

    scale = 1.0 / math.sqrt(HEAD_DIM)
    lane = lax.broadcasted_iota(jnp.int32, (row_len, LANES), 1)
    left = (lane < HEAD_DIM).astype(BF16)
    right = (lane >= HEAD_DIM).astype(BF16)

    def attend_row(row, carry):
        span = pl.ds(pl.multiple_of(row * row_len, row_len), row_len)
        same = labcol_ref[span, :] == lab_ref[pl.ds(row, 1), :]
        same = jnp.concatenate([same, same], axis=0)
        for pair in range(width // LANES):
            col = pair * LANES
            queries = proj_ref[span, col : col + LANES]
            key_rows = proj_ref[span, width + col : width + col + LANES]
            values = proj_ref[span, 2 * width + col : 2 * width + col + LANES]
            both = jnp.concatenate([queries * left, queries * right], axis=0)
            scores = jnp.where(same, dot(both, key_rows, NT) * scale, NEG_FILL)
            top = jnp.max(scores, axis=-1, keepdims=True)
            expo = jnp.exp(scores - top)
            total = jnp.sum(expo, axis=-1, keepdims=True)
            probs = (expo / total).astype(BF16)
            probs_ref[row, pair] = probs
            wide_probs = jnp.concatenate([probs[:row_len], probs[row_len:]], axis=1)
            split_values = jnp.concatenate([values * left, values * right], axis=0)
            ctx_ref[span, col : col + LANES] = dot(wide_probs, split_values).astype(BF16)
        return carry

    lax.fori_loop(0, kept_rows, attend_row, 0)
    get_wo.wait()
    for row in range(kept_rows):
        span = pl.ds(row * row_len, row_len)
        total = x_ref[span, :].astype(F32) + dot(ctx_ref[span, :], wo_ref[...]) + bo_ref[...]
        centered = total - row_mean(total)
        rstd = lax.rsqrt(row_mean(centered * centered) + NORM_EPS)
        normed = centered * rstd
        hidden = normed * gain_ref[...] + shift_ref[...]
        norm_ref[span, :] = normed
        rstd_ref[span, :] = rstd
        hid_ref[span, :] = hidden
        low_ref[span, :] = hidden.astype(BF16)


def forward_kernel(
    got_ref,
    wqkv_src,
    bias_ref,
    wo_src,
    bo_ref,
    gain_ref,
    shift_ref,
    win_ref,
    bin_ref,
    wout_ref,
    bout_ref,
    gain_two_ref,
    shift_two_ref,
    stack_out,
    proj_out,
    probs_out,
    norm_out,
    rstd_ref,
    lab_ref,
    labcol_ref,
    meta_ref,
    source_ref,
    act_ref,
    slope_ref,
    enc_ref,
    norm_two_ref,
    rstd_two_ref,
    pooled_ref,
    copies_ref,
    stack_ref,
    proj_ref,
    probs_ref,
    norm_ref,
    hid_ref,
    total_ref,
    wqkv_ref,
    wo_ref,
    sems,
    out_sems,
):
    step = pl.program_id(0)
    puts = [
        pltpu.make_async_copy(held, out, out_sems.at[index])
        for index, (held, out) in enumerate(
            (
                (stack_ref, stack_out),
                (proj_ref, proj_out),
                (probs_ref, probs_out),
                (norm_ref, norm_out),
            )
        )
    ]

    @pl.when(step == 0)
    def _():
        attend_body(
            got_ref,
            wqkv_src,
            bias_ref,
            wo_src,
            bo_ref,
            gain_ref,
            shift_ref,
            rstd_ref,
            lab_ref,
            labcol_ref,
            meta_ref,
            source_ref,
            stack_ref,
            proj_ref,
            probs_ref,
            norm_ref,
            hid_ref,
            wqkv_ref,
            wo_ref,
            sems,
        )
        for put in puts:
            put.start()
        total_ref[...] = hid_ref[...] + bout_ref[...]

    up = dot(stack_ref[2], win_ref[...]) + bin_ref[...]
    phi = 0.5 * (1.0 + lax.erf(up * (1.0 / math.sqrt(2.0))))
    density = jnp.exp(-0.5 * up * up) * (1.0 / math.sqrt(2.0 * math.pi))
    act = (up * phi).astype(BF16)
    act_ref[...] = act
    slope_ref[...] = (phi + up * density).astype(BF16)
    total_ref[...] += dot(act, wout_ref[...])

    @pl.when(step == pl.num_programs(0) - 1)
    def _():
        tok_count, width = total_ref.shape
        kept_rows = tok_count // LANES
        for row in range(kept_rows):
            span = slice(row * LANES, (row + 1) * LANES)
            total = total_ref[span, :]
            centered = total - row_mean(total)
            rstd = lax.rsqrt(row_mean(centered * centered) + NORM_EPS)
            normed = centered * rstd
            out = normed * gain_two_ref[...] + shift_two_ref[...]
            norm_two_ref[span, :] = normed
            rstd_two_ref[span, :] = rstd
            enc_ref[span, :] = out.astype(BF16)
            segment = lax.broadcasted_iota(jnp.int32, (SEG_ROW, LANES), 0).astype(F32)
            onehot = (lab_ref[row : row + 1, :] == segment).astype(F32)
            count = jnp.sum(onehot, axis=1, keepdims=True)
            high, middle, low = split_three(out)
            mask = onehot.astype(BF16)
            summed = dot(mask, high) + dot(mask, middle) + dot(mask, low)
            pooled_ref[row * SEG_ROW : (row + 1) * SEG_ROW, :] = (summed / count).astype(BF16)
        for owner in range(copies_ref.shape[0]):
            copies_ref[owner] = pooled_ref[...]
        for put in puts:
            put.wait()


def forward(
    got,
    w_qkv,
    bias,
    w_o,
    b_o,
    gain,
    shift,
    w_in,
    b_in,
    w_out,
    b_out,
    gain_two,
    shift_two,
    kept_rows,
):
    wide_count, slot_len, width = got.shape
    row_len = slot_len - META_ROWS
    tok_count = kept_rows * row_len
    units = w_in.shape[1]
    tile = 768
    whole = lambda step: (0, 0)
    hbm = pl.BlockSpec(memory_space=pl.ANY)
    wide_vector = pl.BlockSpec((1, 3 * width), whole)
    vector = pl.BlockSpec((1, width), whole)
    stack = (3, tok_count, width)
    proj = (tok_count, 3 * width)
    probs = (kept_rows, width // LANES, 2 * row_len, row_len)
    flat = (tok_count, width)
    own = (kept_rows * SEG_ROW, width)
    shapes = (
        (stack, BF16, hbm_shape),
        (proj, BF16, hbm_shape),
        (probs, BF16, hbm_shape),
        (flat, F32, hbm_shape),
        ((tok_count, 1), F32),
        ((8, LANES), F32),
        ((tok_count, LANES), F32),
        ((wide_count, META_ROWS, LANES), BF16),
        ((kept_rows,), jnp.int32),
        ((tok_count, units), BF16),
        ((tok_count, units), BF16),
        (flat, BF16),
        (flat, F32),
        ((tok_count, 1), F32),
        (own, BF16),
        ((wide_count,) + own, BF16),
    )
    return pl.pallas_call(
        forward_kernel,
        out_shape=[make_shape(*item) for item in shapes],
        grid_spec=pltpu.PrefetchScalarGridSpec(
            num_scalar_prefetch=0,
            grid=(units // tile,),
            in_specs=[
                hbm,
                hbm,
                wide_vector,
                hbm,
                vector,
                vector,
                vector,
                pl.BlockSpec((width, tile), lambda step: (0, step)),
                pl.BlockSpec((1, tile), lambda step: (0, step)),
                pl.BlockSpec((tile, width), lambda step: (step, 0)),
                vector,
                vector,
                vector,
            ],
            out_specs=[
                hbm,
                hbm,
                hbm,
                hbm,
                pl.BlockSpec((tok_count, 1), whole),
                pl.BlockSpec((8, LANES), whole),
                pl.BlockSpec((tok_count, LANES), whole),
                pl.BlockSpec((wide_count, META_ROWS, LANES), lambda step: (0, 0, 0)),
                smem_spec(),
                pl.BlockSpec((tok_count, tile), lambda step: (0, step)),
                pl.BlockSpec((tok_count, tile), lambda step: (0, step)),
                pl.BlockSpec(flat, whole),
                pl.BlockSpec(flat, whole),
                pl.BlockSpec((tok_count, 1), whole),
                pl.BlockSpec(own, whole),
                pl.BlockSpec((wide_count,) + own, lambda step: (0, 0, 0)),
            ],
            scratch_shapes=[
                pltpu.VMEM(stack, BF16),
                pltpu.VMEM(proj, BF16),
                pltpu.VMEM(probs, BF16),
                pltpu.VMEM(flat, F32),
                pltpu.VMEM(flat, F32),
                pltpu.VMEM(flat, F32),
                pltpu.VMEM(w_qkv.shape, BF16),
                pltpu.VMEM(w_o.shape, BF16),
                pltpu.SemaphoreType.DMA((5 + kept_rows,)),
                pltpu.SemaphoreType.DMA((4,)),
            ],
        ),
        cost_estimate=cost(20),
        compiler_params=params(1),
        name="forward",
    )(
        got,
        w_qkv,
        bias,
        w_o,
        b_o,
        gain,
        shift,
        w_in,
        b_in,
        w_out,
        b_out,
        gain_two,
        shift_two,
    )


def route_kernel(me_ref, meta_ref, pair_ref, place_ref, targ_ref, first_ref, second_ref):
    wide_count = meta_ref.shape[0]
    me = me_ref[0]
    kept_rows = place_ref.shape[0] // SEG_ROW
    me_f = me.astype(F32)

    def table(row):
        return jnp.concatenate(
            [meta_ref[j, row : row + 1, :LANES].astype(F32) for j in range(wide_count)], axis=0
        )

    labels = table(0)
    dest = table(1)
    lane = lax.broadcasted_iota(jnp.int32, (wide_count, LANES), 1)
    slots = SEG_ROW * 2 * kept_rows
    dest = jnp.where(lane < slots, dest, -1.0)
    partner = table(2)
    target = table(3) + table(4) + table(5)
    sends = jnp.zeros((wide_count, LANES), F32)
    for owner in range(wide_count):
        to_owner = jnp.max((dest == float(owner)).astype(F32), axis=1, keepdims=True)
        sends = sends + jnp.where(lane == owner, to_owner, 0.0)
    row_id = lax.broadcasted_iota(jnp.int32, (wide_count, wide_count), 0)
    col_id = lax.broadcasted_iota(jnp.int32, (wide_count, wide_count), 1)
    below = (col_id < row_id).astype(BF16)
    earlier = dot(below, sends.astype(BF16))
    rank = jnp.zeros((wide_count, LANES), F32)
    for owner in range(wide_count):
        rank = rank + jnp.where(dest == float(owner), earlier[:, owner : owner + 1], 0.0)
    segment = (lane % SEG_ROW).astype(F32)
    per_owner = float(kept_rows * SEG_ROW)
    place = jnp.where(dest >= 0.0, dest * per_owner + rank * float(SEG_ROW) + segment, -1.0)
    live = (labels[:, 0:1] >= 0.0).astype(F32)
    my_rank = dot(below, jnp.broadcast_to(live, (wide_count, LANES)).astype(BF16))
    seg_lane = lax.broadcasted_iota(jnp.int32, (SEG_ROW, LANES), 1)
    seg_id = lax.broadcasted_iota(jnp.int32, (SEG_ROW, LANES), 0)
    for row in range(kept_rows):
        chosen = (live > 0.0) & (my_rank[:, 0:1] == float(row))
        pick = lambda values: column_sum(jnp.where(chosen, values, 0.0))
        own = (pick(dest) == me_f) & (seg_lane % SEG_ROW == seg_id)
        gather = lambda mask, values: jnp.sum(jnp.where(mask, values, 0.0), axis=1, keepdims=True)
        other = gather(own, pick(partner))
        at_other = seg_lane.astype(F32) == other
        out = slice(row * SEG_ROW, (row + 1) * SEG_ROW)
        place_ref[out, :] = gather(at_other, pick(place))
        targ_ref[out, :] = gather(own, pick(target))
    mine = lax.broadcasted_iota(jnp.int32, (wide_count, LANES), 0) == me
    my_place = column_sum(jnp.where(mine, place, 0.0))
    pair_lane = lax.broadcasted_iota(jnp.int32, (pair_ref.shape[0], LANES), 1)
    for column, out_ref in ((0, first_ref), (1, second_ref)):
        at_slot = pair_lane == pair_ref[:, column : column + 1]
        out_ref[...] = jnp.sum(jnp.where(at_slot, my_place, 0.0), axis=1, keepdims=True)


def route(me, meta, pair_index, kept_rows):
    wide_count = meta.shape[0]
    own = kept_rows * SEG_ROW
    pairs = pair_index.shape[0]
    shapes = (
        ((own, 1), F32),
        ((own, 1), F32),
        ((pairs, 1), F32),
        ((pairs, 1), F32),
    )
    return pl.pallas_call(
        route_kernel,
        out_shape=[make_shape(*item) for item in shapes],
        in_specs=[smem_spec(), vmem_spec(), vmem_spec()],
        out_specs=[vmem_spec()] * len(shapes),
        cost_estimate=cost(1),
        compiler_params=params(),
        name="route",
    )(me, meta, pair_index)


def pick_rows(place_ref, all_ref):
    lane = lax.broadcasted_iota(jnp.int32, (place_ref.shape[0], all_ref.shape[0]), 1)
    return dot((lane.astype(F32) == place_ref[...]).astype(BF16), all_ref[...])


def cosine_parts(left, right):
    inner = row_mean(left * right)
    left_inv = lax.rsqrt(row_mean(left * left) + COS_EPS)
    right_inv = lax.rsqrt(row_mean(right * right) + COS_EPS)
    return (inner, left_inv, right_inv)


def cosine_kernel(first_ref, second_ref, all_ref, sim_ref):
    left = pick_rows(first_ref, all_ref)
    right = pick_rows(second_ref, all_ref)
    inner, left_inv, right_inv = cosine_parts(left, right)
    sim = inner * left_inv * right_inv
    sim_ref[...] = jnp.where(first_ref[...] >= 0.0, sim, 0.0)


def cosine_pairs(first, second, pooled_all):
    return pl.pallas_call(
        cosine_kernel,
        out_shape=jax.ShapeDtypeStruct(first.shape, F32),
        in_specs=[vmem_spec()] * 3,
        out_specs=vmem_spec(),
        cost_estimate=cost(1),
        compiler_params=params(),
        name="cosine_pairs",
    )(first, second, pooled_all)


def part_blocks(parity, held, own_ref, send_refs, first=0):
    for index in range(held.shape[0] // 2):
        own_ref[index] = held[2 * index + parity]
        send_refs[first + index][...] = held[2 * index + 1 - parity]


def norm_back(grad, normed, rstd, gain):
    scaled = grad * gain
    return rstd * (scaled - row_mean(scaled) - normed * row_mean(scaled * normed))


def loss_back_body(
    me_ref,
    own_ref,
    all_ref,
    place_ref,
    targ_ref,
    lab_ref,
    labcol_ref,
    norm_ref,
    rstd_ref,
    gain_ref,
    dres_ref,
    dffn_ref,
    sums_ref,
    kept_ref,
    send_refs,
    held,
):
    depth = held.shape[1]
    tok_count, width = norm_ref.shape
    kept_rows = tok_count // LANES
    left = own_ref[...].astype(F32)
    right = pick_rows(place_ref, all_ref)
    inner, left_inv, right_inv = cosine_parts(left, right)
    error = 2.0 * (inner * left_inv * right_inv - targ_ref[...])
    factor = error * left_inv * right_inv * (1.0 / width)
    d_pooled = (factor * (right - left * (inner * left_inv * left_inv))).astype(BF16).astype(F32)
    gain_sum = jnp.zeros((1, width), F32)
    shift_sum = jnp.zeros((1, width), F32)
    bias_sum = jnp.zeros((1, width), F32)
    lane = lax.broadcasted_iota(jnp.int32, (LANES, LANES), 1).astype(F32)
    for row in range(kept_rows):
        span = slice(row * LANES, (row + 1) * LANES)
        segment = lax.broadcasted_iota(jnp.int32, (SEG_ROW, LANES), 0).astype(F32)
        count = jnp.sum(
            (lab_ref[row : row + 1, :] == segment).astype(F32), axis=1, keepdims=True
        )
        per_token = d_pooled[row * SEG_ROW : (row + 1) * SEG_ROW, :] / count
        shift_sum = shift_sum + column_sum(per_token * count)
        padded = jnp.concatenate([per_token, jnp.zeros((LANES - SEG_ROW, width), F32)], axis=0)
        onehot = (labcol_ref[span, :] == lane).astype(BF16)
        high, middle, low = split_three(padded)
        d_out = dot(onehot, high) + dot(onehot, middle) + dot(onehot, low)
        normed = norm_ref[span, :]
        d_res = norm_back(d_out, normed, rstd_ref[span, :], gain_ref[...])
        d_low = d_res.astype(BF16)
        dres_ref[span, :] = d_res
        dffn_ref[span, :] = d_low
        turned = d_low.T
        for block in range(held.shape[0]):
            held[block, :, span] = turned[block * depth : (block + 1) * depth, :]
        gain_sum = gain_sum + column_sum(d_out * normed)
        bias_sum = bias_sum + column_sum(d_low.astype(F32))
    sums_ref[0:1, :] = gain_sum
    sums_ref[1:2, :] = shift_sum
    sums_ref[2:3, :] = bias_sum
    sums_ref[3:8, :] = jnp.zeros((5, width), F32)
    part_blocks(me_ref[0] & 1, held, kept_ref, send_refs)


def feed_back_kernel(
    half,
    me_ref,
    own_ref,
    all_ref,
    place_ref,
    targ_ref,
    lab_ref,
    labcol_ref,
    norm_two_ref,
    rstd_two_ref,
    gain_two_ref,
    wout_ref,
    win_ref,
    slope_ref,
    norm_src,
    rstd_ref,
    gain_ref,
    wo_src,
    bsum_ref,
    done_ref,
    dattn_t_ref,
    dctx_ref,
    sums_ref,
    sums_two_ref,
    kept_out_ref,
    kept_ref,
    *refs,
):
    send_out, send_refs, refs = refs[:half], refs[half : 2 * half], refs[2 * half :]
    held_out, held, dffn_ref, total_ref, norm_ref, wo_ref, sems = refs
    count, depth, _ = held.shape
    step = pl.program_id(0)
    copies = [
        pltpu.make_async_copy(norm_src, norm_ref, sems.at[0]),
        pltpu.make_async_copy(wo_src, wo_ref, sems.at[1]),
    ]

    @pl.when(step == 0)
    def _():
        for copy in copies:
            copy.start()
        loss_back_body(
            me_ref,
            own_ref,
            all_ref,
            place_ref,
            targ_ref,
            lab_ref,
            labcol_ref,
            norm_two_ref,
            rstd_two_ref,
            gain_two_ref,
            total_ref,
            dffn_ref,
            sums_two_ref,
            kept_out_ref,
            send_out,
            held_out,
        )

    d_up = (dot(dffn_ref[...], wout_ref[...], NT) * slope_ref[...].astype(F32)).astype(BF16)
    turned = d_up.T
    for block in range(count):
        held[block] = turned[block * depth : (block + 1) * depth, :]
    for at in range(half // (count // 2)):

        @pl.when(step == at)
        def _():
            part_blocks(me_ref[0] & 1, held, kept_ref, send_refs, at * (count // 2))

    bsum_ref[...] = column_sum(d_up.astype(F32))
    total_ref[...] += dot(d_up, win_ref[...], NT)

    @pl.when(step == pl.num_programs(0) - 1)
    def _():
        for copy in copies:
            copy.wait()
        tok_count, width = total_ref.shape
        kept_rows = tok_count // LANES
        gain_sum = jnp.zeros((1, width), F32)
        shift_sum = jnp.zeros((1, width), F32)
        bias_sum = jnp.zeros((1, width), F32)
        for row in range(kept_rows):
            span = slice(row * LANES, (row + 1) * LANES)
            d_hidden = total_ref[span, :]
            normed = norm_ref[span, :]
            d_res = norm_back(d_hidden, normed, rstd_ref[span, :], gain_ref[...])
            d_low = d_res.astype(BF16)
            done_ref[span, :] = d_res
            dattn_t_ref[:, span] = d_low.T
            dctx_ref[span, :] = dot(d_low, wo_ref[...], NT).astype(BF16)
            gain_sum = gain_sum + column_sum(d_hidden * normed)
            shift_sum = shift_sum + column_sum(d_hidden)
            bias_sum = bias_sum + column_sum(d_low.astype(F32))
        sums_ref[0:1, :] = gain_sum
        sums_ref[1:2, :] = shift_sum
        sums_ref[2:3, :] = bias_sum
        sums_ref[3:8, :] = jnp.zeros((5, width), F32)


def feed_back(
    me,
    own,
    pooled_all,
    place,
    target,
    labels,
    label_cols,
    normed_two,
    rstd_two,
    gain_two,
    w_out,
    w_in,
    slope,
    normed,
    rstd,
    gain,
    w_o,
    wide_count,
):
    tok_count, width = normed.shape
    units = w_in.shape[1]
    tile = 768
    depth = units // wide_count
    depth_out = width // wide_count
    half = wide_count // 2
    count = tile // depth
    whole = lambda step: (0, 0)
    fixed = lambda array: pl.BlockSpec(array.shape, whole)
    hbm = pl.BlockSpec(memory_space=pl.ANY)
    shapes = (
        (
            ((1, units), F32),
            ((tok_count, width), F32),
            ((width, tok_count), BF16),
            ((tok_count, width), BF16),
            ((8, width), F32),
            ((8, width), F32),
            ((half, depth_out, tok_count), BF16),
            ((half, depth, tok_count), BF16),
        )
        + (((depth_out, tok_count), BF16, hbm_shape),) * half
        + (((depth, tok_count), BF16, hbm_shape),) * half
    )
    return pl.pallas_call(
        functools.partial(feed_back_kernel, half),
        out_shape=[make_shape(*item) for item in shapes],
        grid_spec=pltpu.PrefetchScalarGridSpec(
            num_scalar_prefetch=0,
            grid=(units // tile,),
            in_specs=[
                smem_spec(),
                fixed(own),
                fixed(pooled_all),
                fixed(place),
                fixed(target),
                fixed(labels),
                fixed(label_cols),
                fixed(normed_two),
                fixed(rstd_two),
                fixed(gain_two),
                pl.BlockSpec((tile, width), lambda step: (step, 0)),
                pl.BlockSpec((width, tile), lambda step: (0, step)),
                pl.BlockSpec((tok_count, tile), lambda step: (0, step)),
                hbm,
                fixed(rstd),
                fixed(gain),
                hbm,
            ],
            out_specs=[
                pl.BlockSpec((1, tile), lambda step: (0, step)),
                pl.BlockSpec((tok_count, width), whole),
                pl.BlockSpec((width, tok_count), whole),
                pl.BlockSpec((tok_count, width), whole),
                pl.BlockSpec((8, width), whole),
                pl.BlockSpec((8, width), whole),
                pl.BlockSpec((half, depth_out, tok_count), lambda step: (0, 0, 0)),
                pl.BlockSpec((count // 2, depth, tok_count), lambda step: (step, 0, 0)),
            ]
            + [pl.BlockSpec((depth_out, tok_count), whole)] * half
            + [pl.BlockSpec((depth, tok_count), whole)] * half,
            scratch_shapes=[
                pltpu.VMEM((wide_count, depth_out, tok_count), BF16),
                pltpu.VMEM((count, depth, tok_count), BF16),
                pltpu.VMEM((tok_count, width), BF16),
                pltpu.VMEM((tok_count, width), F32),
                pltpu.VMEM((tok_count, width), F32),
                pltpu.VMEM(w_o.shape, BF16),
                pltpu.SemaphoreType.DMA((2,)),
            ],
        ),
        cost_estimate=cost(14),
        compiler_params=params(1),
        name="feed_back",
    )(
        me,
        own,
        pooled_all,
        place,
        target,
        labels,
        label_cols,
        normed_two,
        rstd_two,
        gain_two,
        w_out,
        w_in,
        slope,
        normed,
        rstd,
        gain,
        w_o,
    )


def attend_back_kernel(
    source_ref,
    me_ref,
    proj_ref,
    probs_ref,
    dctx_ref,
    done_ref,
    wqkv_ref,
    dattn_t_ref,
    dtok_ref,
    sums_ref,
    kept_ref,
    *refs,
):
    send_refs, held, dproj_ref = refs[:-2], refs[-2], refs[-1]
    row = pl.program_id(0)
    row_len, width = dctx_ref.shape
    blocks = held.shape[0]
    main = 3 * width // blocks
    scale = 1.0 / math.sqrt(HEAD_DIM)
    lane = lax.broadcasted_iota(jnp.int32, (row_len, LANES), 1)
    left = (lane < HEAD_DIM).astype(BF16)
    right = (lane >= HEAD_DIM).astype(BF16)

    def twice(values):
        return jnp.concatenate([values * left, values * right], axis=0)

    for pair in range(width // LANES):
        col = pair * LANES
        queries = proj_ref[:, col : col + LANES]
        key_rows = proj_ref[:, width + col : width + col + LANES]
        values = proj_ref[:, 2 * width + col : 2 * width + col + LANES]
        probs = probs_ref[0, pair]
        d_ctx = twice(dctx_ref[:, col : col + LANES])
        d_probs = dot(d_ctx, values, NT)
        probs_f = probs.astype(F32)
        inner = jnp.sum(probs_f * d_probs, axis=-1, keepdims=True)
        d_scores = (probs_f * (d_probs - inner)).astype(BF16)
        wide_scores = jnp.concatenate([d_scores[:row_len], d_scores[row_len:]], axis=1)
        d_query = dot(wide_scores, twice(key_rows)) * scale
        d_key = dot(d_scores, twice(queries), TN) * scale
        d_value = dot(probs, d_ctx, TN)
        for part, grad in ((0, d_query), (1, d_key), (2, d_value)):
            low = grad.astype(BF16)
            place = part * width + col
            dproj_ref[:, place : place + LANES] = low
            turned = low.T
            start = place
            while start < place + LANES:
                block, offset = divmod(start, main)
                stop = min(place + LANES, (block + 1) * main)
                held[block, offset : offset + stop - start, :] = turned[
                    start - place : stop - place, :
                ]
                start = stop
            before = jnp.where(row == 0, 0.0, sums_ref[:, place : place + LANES])
            sums_ref[:, place : place + LANES] = before + column_sum(low.astype(F32))

    rest = width // blocks
    for block in range(blocks):
        held[block, main:, :] = dattn_t_ref[block * rest : (block + 1) * rest, :]
    part_blocks(me_ref[0] & 1, held, kept_ref, send_refs)
    grad = done_ref[...] + dot(dproj_ref[...], wqkv_ref[...], NT)
    dtok_ref[0] = grad.astype(BF16)


def attend_back(sources, me, proj, probs, d_ctx, d_one, w_qkv, d_attn_t, wide_count):
    tok_count, width = d_ctx.shape
    kept_rows = tok_count // LANES
    half = wide_count // 2
    depth = 4 * width // wide_count
    shapes = (
        ((wide_count, LANES, width), BF16),
        ((1, 3 * width), F32),
        ((half, depth, tok_count), BF16),
    ) + (((depth, tok_count), BF16, hbm_shape),) * half
    return pl.pallas_call(
        attend_back_kernel,
        out_shape=[make_shape(*item) for item in shapes],
        grid_spec=pltpu.PrefetchScalarGridSpec(
            num_scalar_prefetch=2,
            grid=(kept_rows,),
            in_specs=[
                pl.BlockSpec((LANES, 3 * width), lambda row, src, me: (row, 0)),
                pl.BlockSpec((1,) + probs.shape[1:], lambda row, src, me: (row, 0, 0, 0)),
                pl.BlockSpec((LANES, width), lambda row, src, me: (row, 0)),
                pl.BlockSpec((LANES, width), lambda row, src, me: (row, 0)),
                pl.BlockSpec((width, 3 * width), lambda row, src, me: (0, 0)),
                pl.BlockSpec((width, LANES), lambda row, src, me: (0, row)),
            ],
            out_specs=[
                pl.BlockSpec((1, LANES, width), lambda row, src, me: (src[row], 0, 0)),
                pl.BlockSpec((1, 3 * width), lambda row, src, me: (0, 0)),
                pl.BlockSpec((half, depth, LANES), lambda row, src, me: (0, 0, row)),
            ]
            + [pl.BlockSpec((depth, LANES), lambda row, src, me: (0, row))] * half,
            scratch_shapes=[
                pltpu.VMEM((wide_count, depth, LANES), BF16),
                pltpu.VMEM((LANES, 3 * width), BF16),
            ],
        ),
        cost_estimate=cost(20),
        compiler_params=params(1),
        name="attend_back",
    )(sources, me, proj, probs, d_ctx, d_one, w_qkv, d_attn_t)


def home_kernel(dest_ref, rows_ref, out_ref, sems):
    slot_dev = out_ref.shape[0]

    def copy(slot):
        return pltpu.make_async_copy(
            rows_ref.at[jnp.maximum(dest_ref[slot], 0)], out_ref.at[slot], sems.at[slot]
        )

    for slot in range(slot_dev):
        copy(slot).start()
    for slot in range(slot_dev):
        copy(slot).wait()

        @pl.when(dest_ref[slot] < 0)
        def _():
            out_ref[slot] = jnp.zeros(out_ref.shape[1:], out_ref.dtype)


def home_rows(destination, rows):
    count = destination.shape[0]
    return pl.pallas_call(
        home_kernel,
        out_shape=jax.ShapeDtypeStruct((count,) + rows.shape[1:], rows.dtype),
        in_specs=[smem_spec(), pl.BlockSpec(memory_space=pl.ANY)],
        out_specs=vmem_spec(),
        scratch_shapes=[pltpu.SemaphoreType.DMA((count,))],
        cost_estimate=cost(3),
        compiler_params=params(),
        name="home_rows",
    )(destination, rows)


def block_at(index, bit, value):
    low = index & ((1 << bit) - 1)
    return ((index >> bit) << (bit + 1)) | (value << bit) | low


def grad_kernel(first_bit, second_bit, spans, blocks, me_ref, own_ref, *refs):
    recv_refs, refs = refs[:blocks], refs[blocks:]
    step = pl.program_id(0)
    half_steps = pl.num_programs(0) // 2
    terms = len(spans)
    own_xs, recv_xs = refs[:terms], refs[terms : 2 * terms]
    outs = refs[2 * terms : 2 * terms + 4]
    own_lefts = refs[2 * terms + 4 : 3 * terms + 4]
    recv_lefts = refs[3 * terms + 4 :]
    me = me_ref[0]
    for half, bit in ((0, first_bit), (1, second_bit)):

        @pl.when(step == half * half_steps)
        def _():
            side = (me >> bit) & 1
            for block in range(blocks):
                low = block & ((1 << (bit - 1)) - 1)
                rest = ((block >> bit) << (bit - 1)) | low
                kept = ((block >> (bit - 1)) & 1) == side
                index = jnp.where(kept, rest, rest + blocks // 2)
                for (start, stop), own_left, recv_left in zip(spans, own_lefts, recv_lefts):
                    own_left[index] = own_ref[block, start:stop, :]
                    recv_left[index] = recv_refs[block][start:stop, :]

    for term, (start, stop) in enumerate(spans):
        rows = stop - start
        chunk = blocks if blocks * rows <= 384 else blocks // 2
        for base in range(0, blocks, chunk):
            span = slice(base, base + chunk)
            flat = lambda left: left[span].reshape(chunk * rows, left.shape[2])
            part = dot(flat(own_lefts[term]), own_xs[term][...])
            part = part + dot(flat(recv_lefts[term]), recv_xs[term][...])
            part = part.astype(BF16).reshape(chunk, rows, part.shape[1])
            for index in range(chunk):
                block = base + index
                role, place = divmod(block, blocks // 2)
                for half in range(2):

                    @pl.when((step < half_steps) == (half == 0))
                    def _():
                        outs[2 * half + role][place, start:stop, :] = part[index]


def grad_terms(me, own, received, own_xs, recv_xs, spans, first_bit, second_bit, tile):
    blocks = len(received)
    rows, tok_count = received[0].shape
    columns = own_xs[0][0].shape[-1]
    steps = columns // tile
    half = steps // 2

    def x_spec(item):
        array, lead = item
        if lead is None:
            return pl.BlockSpec((tok_count, tile), lambda step: (0, step))
        return pl.BlockSpec((pl.Squeezed(), tok_count, tile), lambda step: (lead, 0, step))

    out_block = (blocks // 2, rows, tile)
    first_spec = pl.BlockSpec(out_block, lambda step: (0, 0, jnp.minimum(step, half - 1)))
    second_spec = pl.BlockSpec(out_block, lambda step: (0, 0, jnp.maximum(step - half, 0)))
    shape = hbm_shape((blocks // 2, rows, columns // 2), BF16)
    whole = lambda step: (0, 0, 0)
    lefts = [pltpu.VMEM((blocks, stop - start, tok_count), BF16) for start, stop in spans]
    return pl.pallas_call(
        functools.partial(grad_kernel, first_bit, second_bit, spans, blocks),
        out_shape=[shape] * 4,
        grid_spec=pltpu.PrefetchScalarGridSpec(
            num_scalar_prefetch=0,
            grid=(steps,),
            in_specs=[
                smem_spec(),
                pl.BlockSpec(own.shape, whole),
            ]
            + [pl.BlockSpec((rows, tok_count), lambda step: (0, 0))] * blocks
            + [x_spec(item) for item in own_xs + recv_xs],
            out_specs=[first_spec, first_spec, second_spec, second_spec],
            scratch_shapes=lefts + lefts,
        ),
        cost_estimate=cost(7),
        compiler_params=params(1),
        name="grad_terms",
    )(me, own, *received, *[item[0] for item in own_xs + recv_xs])


def fold_kernel(bits, places, me_ref, *refs):
    me = me_ref[0]
    for half in range(2):
        kept_ref, recv_ref = refs[2 * half], refs[2 * half + 1]
        keep_out, send_out = refs[4 + 2 * half], refs[5 + 2 * half]
        side = (me >> bits[half]) & 1
        for index in range(keep_out.shape[0]):
            for value, out_ref in ((1 - side, send_out), (side, keep_out)):
                block = block_at(index, places[half], value)
                out_ref[index] = add_low(kept_ref[block], recv_ref[block])


def fold(me, halves, bits, places):
    shapes = []
    for kept, _ in halves:
        shapes += [hbm_shape((kept.shape[0] // 2,) + kept.shape[1:], BF16)] * 2
    return pl.pallas_call(
        functools.partial(fold_kernel, bits, places),
        out_shape=shapes,
        in_specs=[smem_spec()] + [vmem_spec()] * 4,
        out_specs=[vmem_spec()] * 4,
        cost_estimate=cost(0.5),
        compiler_params=params(),
        name="fold",
    )(me, *halves[0], *halves[1])


def piece_kernel(turned, stacked, me_ref, *refs):
    outs, held = (refs[4:], refs[4]) if stacked else (refs[4:-1], refs[-1])
    count = held.shape[0]
    depth = held.shape[1] if turned else held.shape[2]
    for half in range(2):
        total = add_low(refs[2 * half][0], refs[2 * half + 1][0])
        if turned:
            total = total.T
        for index in range(count // 2):
            span = slice(index * depth, (index + 1) * depth)
            held[half * (count // 2) + index] = total[span, :] if turned else total[:, span]
    if not stacked:
        for step in range(count):
            outs[step][...] = held[me_ref[0] ^ step]


def narrow_pieces(me, halves, narrow_count, turned, stacked):
    _, rows, columns = halves[0][0].shape
    depth = 2 * columns // narrow_count
    shape = (depth, rows) if turned else (rows, depth)
    whole = (narrow_count,) + shape
    outs = [hbm_shape(whole, BF16)] if stacked else [hbm_shape(shape, BF16)] * narrow_count
    return pl.pallas_call(
        functools.partial(piece_kernel, turned, stacked),
        out_shape=outs,
        in_specs=[smem_spec()] + [vmem_spec()] * 4,
        out_specs=[vmem_spec()] * len(outs),
        scratch_shapes=[] if stacked else [pltpu.VMEM(whole, BF16)],
        cost_estimate=cost(1),
        compiler_params=params(),
        name="narrow_pieces",
    )(me, *halves[0], *halves[1])


def sum_kernel(count, *refs):
    terms = [ref[...] for ref in refs[:count]]
    if len(terms[0].shape) == 3:
        terms = [terms[0][place] for place in range(terms[0].shape[0])]
    total = terms[0].astype(F32)
    for term in terms[1:]:
        total = total + term.astype(F32)
    start = 0
    for out_ref in refs[count:]:
        out_ref[...] = total[:, start : start + out_ref.shape[1]]
        start += out_ref.shape[1]


def sum_pieces(pieces, cuts=None):
    shape = pieces[0].shape[-2:]
    outs = [jax.ShapeDtypeStruct((shape[0], cut), F32) for cut in cuts or (shape[1],)]
    return pl.pallas_call(
        functools.partial(sum_kernel, len(pieces)),
        out_shape=outs,
        in_specs=[vmem_spec()] * len(pieces),
        out_specs=[vmem_spec()] * len(outs),
        cost_estimate=cost(1),
        compiler_params=params(),
        name="sum_pieces",
    )(*pieces)


def pack_kernel(cuts, *refs):
    out_ref = refs[-1]
    place = 0
    for index, row, start, stop in cuts:
        for at in range(start, stop, LANES):
            out_ref[place : place + 1, :] = refs[index][row : row + 1, at : at + LANES]
            place += 1


def pack_vectors(arrays, cuts):
    lines = sum(stop - start for _, _, start, stop in cuts) // LANES
    return pl.pallas_call(
        functools.partial(pack_kernel, cuts),
        out_shape=jax.ShapeDtypeStruct((lines, LANES), F32),
        in_specs=[vmem_spec()] * len(arrays),
        out_specs=vmem_spec(),
        cost_estimate=cost(0.5),
        compiler_params=params(),
        name="pack_vectors",
    )(*arrays)


def swap(values, axis, bit):
    count = lax.axis_size(axis)
    return lax.ppermute(values, axis, [(i, i ^ (1 << bit)) for i in range(count)])


def trade(pieces):
    count = len(pieces)
    got = [pieces[0]]
    for step in range(1, count):
        got.append(lax.ppermute(pieces[step], "narrow", [(i, i ^ step) for i in range(count)]))
    return got


def pick(values, dim, index):
    return lax.dynamic_index_in_dim(values, index, dim, keepdims=False)


def add_low(kept, received):
    return (kept.astype(F32) + received.astype(F32)).astype(BF16)


def after(value, *others):
    return lax.optimization_barrier((value,) + others)[0]


def to_partner(blocks):
    return [swap(block, "wide", 0) for block in blocks]


class Folding:
    def __init__(self, me, outs, orders, *gates):
        self.me = me
        self.orders = orders
        self.left = [sorted(order) for order in orders]
        self.kept = [outs[0], outs[2]]
        self.sent = [outs[1], outs[3]]
        self.level = 0
        self.exchange(*gates)

    def exchange(self, *gates):
        self.received = [
            swap(after(self.sent[half], *gates), "wide", self.orders[half][self.level])
            for half in range(2)
        ]
        for half in range(2):
            self.left[half].remove(self.orders[half][self.level])
        self.level += 1

    def halves(self):
        return [(self.kept[half], self.received[half]) for half in range(2)]

    def step(self, *gates):
        bits = [order[self.level] for order in self.orders]
        places = [left.index(bit) for left, bit in zip(self.left, bits)]
        outs = fold(self.me, self.halves(), bits, places)
        self.kept = [outs[0], outs[2]]
        self.sent = [outs[1], outs[3]]
        self.exchange(*gates)

    def gate(self, *others):
        self.kept[0] = after(self.kept[0], *others)

    def finish(self, me_narrow, narrow_count, turned, stacked=False):
        while self.level < len(self.orders[0]):
            self.step()
        return narrow_pieces(me_narrow, self.halves(), narrow_count, turned, stacked)


def hop(values, axis, bit):
    return values + swap(values, axis, bit)


def on_device(
    tokens,
    segments,
    destination,
    pair_index,
    targets,
    w_qkv,
    b_qv,
    w_o,
    b_o,
    gain_one,
    shift_one,
    w_in,
    b_in,
    w_out,
    b_out,
    gain_two,
    shift_two,
):
    wide_count = lax.axis_size("wide")
    narrow_count = lax.axis_size("narrow")
    slot_dev, row_len, width = tokens.shape
    kept_rows = slot_dev // 2
    units = w_in.shape[1]
    me = lax.axis_index("wide")
    me_line = me.astype(jnp.int32).reshape(1)
    me_narrow = lax.axis_index("narrow").astype(jnp.int32).reshape(1)
    line = lambda vector: vector.reshape(1, -1)

    sent = build_send(tokens, segments, destination, pair_index, targets, wide_count)
    got = lax.all_to_all(sent, "wide", split_axis=0, concat_axis=0, tiled=True)
    full_bias = jnp.concatenate(
        [b_qv[:width], jnp.zeros((width,), F32), b_qv[width:]]
    ).reshape(1, 3 * width)
    (
        stack,
        proj,
        probs,
        norm_one,
        rstd_one,
        labels,
        label_cols,
        meta,
        sources,
        act,
        slope,
        encoded,
        norm_two,
        rstd_two,
        pooled,
        pooled_copies,
    ) = forward(
        got,
        w_qkv,
        full_bias,
        w_o,
        line(b_o),
        line(gain_one),
        line(shift_one),
        w_in,
        line(b_in),
        w_out,
        line(b_out),
        line(gain_two),
        line(shift_two),
        kept_rows,
    )
    stack_recv = swap(stack, "wide", 0)
    act_recv = swap(act, "wide", 0)
    place, target, first, second = route(me_line, meta, pair_index, kept_rows)
    pooled_all = lax.all_to_all(
        pooled_copies, "wide", split_axis=0, concat_axis=0, tiled=True
    ).reshape(wide_count * kept_rows * SEG_ROW, width)
    similarity = cosine_pairs(first, second, pooled_all).reshape(-1)
    bits = wide_count.bit_length() - 1
    middle = 1 + (bits - 1) // 2
    low_first = list(range(1, bits))
    high_first = list(range(middle, bits)) + list(range(1, middle))
    orders = (low_first, high_first)
    first_bits = (low_first[0], high_first[0])
    half = wide_count // 2
    sum_b_in, d_one, d_attn_t, d_ctx, sums_one, sums_two, own_out, own_in, *sends = feed_back(
        me_line,
        pooled,
        pooled_all,
        place,
        target,
        labels,
        label_cols,
        norm_two,
        rstd_two,
        line(gain_two),
        w_out,
        w_in,
        slope,
        norm_one,
        rstd_one,
        line(gain_one),
        w_o,
        wide_count,
    )
    rows_out = own_out.shape[1]
    rows_in = own_in.shape[1]
    recv_out = to_partner(sends[:half])
    recv_in = to_partner(after(tuple(sends[half:]), tuple(recv_out)))
    fold_out = Folding(
        me_line,
        grad_terms(
            me_line,
            own_out,
            recv_out,
            [(act, None)],
            [(act_recv, None)],
            ((0, rows_out),),
            *first_bits,
            768,
        ),
        orders,
    )
    outs_in = grad_terms(
        me_line,
        own_in,
        after(tuple(recv_in), *fold_out.sent),
        [(stack, 2)],
        [(stack_recv, 2)],
        ((0, rows_in),),
        *first_bits,
        width // 2,
    )
    fold_out.gate(similarity, *outs_in)
    fold_out.step()
    fold_in = Folding(me_line, outs_in, orders, *fold_out.sent)
    d_rows, sums_qkv, own_mix, *send_mix = attend_back(
        sources,
        me_line,
        proj,
        probs,
        after(d_ctx, *fold_out.sent, *fold_in.sent),
        d_one,
        w_qkv,
        d_attn_t,
        wide_count,
    )
    recv_mix = to_partner(send_mix)
    vectors = pack_vectors(
        (sums_qkv, sums_one, sum_b_in, sums_two),
        (
            (0, 0, 0, width),
            (0, 0, 2 * width, 3 * width),
            (1, 2, 0, width),
            (1, 0, 0, width),
            (1, 1, 0, width),
            (2, 0, 0, units),
            (3, 2, 0, width),
            (3, 0, 0, width),
            (3, 1, 0, width),
        ),
    )
    fold_in.gate(d_rows, *fold_out.received)
    fold_in.step()
    fold_out.gate(d_rows)
    pieces_out = fold_out.finish(me_narrow, narrow_count, False)
    traded_out = trade(pieces_out)
    home = lax.all_to_all(
        after(d_rows, *fold_in.sent), "wide", split_axis=0, concat_axis=0, tiled=True
    )
    cols_qkv = 3 * width // wide_count
    rows_mix = own_mix.shape[1]
    (grad_w_out,) = sum_pieces(traded_out)
    grad_w_out = grad_w_out.T
    outs_mix = grad_terms(
        me_line,
        own_mix,
        after(tuple(recv_mix), tuple(pieces_out), *fold_in.sent),
        [(stack, 0), (stack, 1)],
        [(stack_recv, 0), (stack_recv, 1)],
        ((0, cols_qkv), (cols_qkv, rows_mix)),
        *first_bits,
        width // 2,
    )
    vectors = hop(vectors, "wide", 0)
    vectors = hop(vectors, "narrow", 0)
    fold_mix = Folding(
        me_line,
        outs_mix,
        orders,
        vectors,
        tuple(traded_out),
        *fold_in.received,
    )
    grad_tokens = home_rows(destination, home)
    pieces_in = fold_in.finish(me_narrow, narrow_count, True)
    traded_in = trade(pieces_in)
    fold_mix.gate(grad_tokens, tuple(traded_in))
    fold_mix.step()
    vectors = after(vectors, *fold_mix.sent)
    for bit in range(1, narrow_count.bit_length() - 1):
        vectors = hop(vectors, "narrow", bit)
    (grad_w_in,) = sum_pieces(traded_in)
    fold_mix.gate(vectors)
    (pieces_mix,) = fold_mix.finish(me_narrow, narrow_count, True, True)
    traded_mix = lax.all_to_all(pieces_mix, "narrow", split_axis=0, concat_axis=0, tiled=True)
    vectors = after(vectors, pieces_mix)
    for bit in range(1, bits):
        vectors = hop(vectors, "wide", bit)
    grad_w_qkv, grad_w_o = sum_pieces(
        (after(traded_mix, vectors),), (cols_qkv, rows_mix - cols_qkv)
    )
    vectors = vectors.reshape(-1)
    cuts = (2 * width, width, width, width, units, width, width, width)
    outs = []
    start = 0
    for size in cuts:
        outs.append(vectors[start : start + size])
        start += size
    grad_b_qv, grad_b_o, grad_gain_one, grad_shift_one = outs[:4]
    grad_b_in, grad_b_out, grad_gain_two, grad_shift_two = outs[4:]
    return (
        encoded.reshape(kept_rows, row_len, width),
        similarity,
        grad_tokens,
        grad_w_qkv,
        grad_b_qv,
        grad_w_o,
        grad_b_o,
        grad_gain_one,
        grad_shift_one,
        grad_w_in,
        grad_b_in,
        grad_w_out,
        grad_b_out,
        grad_gain_two,
        grad_shift_two,
    )


def solution(mesh):
    rows = ("wide", "narrow")
    in_specs = (P(rows, None, None), P(rows, None), P(rows), P(rows, None), P(rows)) + (P(),) * 12
    matrix = P("narrow", "wide")
    out_specs = (
        P(rows, None, None),
        P(rows),
        P(rows, None, None),
        matrix,
        P(),
        matrix,
        P(),
        P(),
        P(),
        matrix,
        P(),
        matrix,
        P(),
        P(),
        P(),
    )
    return jax.shard_map(
        on_device, mesh=mesh, in_specs=in_specs, out_specs=out_specs, check_vma=False
    )
```
